32 devices in a mesh: section: 2 (over x), dp: 8 (over z, core), tensor: 2 (over y).
Axes of the slice: x: 2, y: 2, z: 4, core: 2. Of those that a mesh axis runs over, the one named last changes fastest.
Arguments:
- x_in: bfloat16 [4, 2048, 768], P(None, ('dp', 'tensor')), may hold values from -6 to 6
- d_out: bfloat16 [4, 2048, 768], P(None, ('dp', 'tensor')), may hold values from -6 to 6
- lengths: int32 [4, 8, 4], P(None, 'dp'), may hold values from 1 to 192, 256 in all within a row
- routes: int32 [2, 4, 2048, 1], P('section', None, 'dp'), may hold values from 0 to 7; in each aligned block of 256 rows (0 to 255, 256 to 511, ..., all dimensions but the last counted through in order) at most 64 rows name the same one
- gain_attn: bfloat16 [2, 768], P('section'), may hold values from 0.5 to 1.5
- w_qkv: bfloat16 [2, 3, 768, 768], P('section', None, 'dp', 'tensor'), may hold values from -0.21875 to 0.21875
- w_attn_out: bfloat16 [2, 768, 768], P('section', 'tensor', 'dp'), may hold values from -0.875 to 0.875
- gain_ffn: bfloat16 [2, 768], P('section'), may hold values from 0.5 to 1.5
- w_router: bfloat16 [2, 768, 8], P('section'), may hold values from -0.15625 to 0.15625
- w_in: bfloat16 [2, 8, 768, 3072], P('section', 'dp', None, 'tensor'), may hold values from -0.21875 to 0.21875
- w_exp_out: bfloat16 [2, 8, 3072, 768], P('section', 'dp', 'tensor'), may hold values from -0.875 to 0.875
Outputs:
- section_out: bfloat16 [2, 4, 2048, 768], P('section', None, ('dp', 'tensor'))
- section_in_grad: bfloat16 [2, 4, 2048, 768], P('section', None, ('dp', 'tensor'))
- g_gain_attn: float32 [2, 768], P('section')
- g_w_qkv: float32 [2, 3, 768, 768], P('section', None, 'dp', 'tensor')
- g_w_attn_out: float32 [2, 768, 768], P('section', 'tensor', 'dp')
- g_gain_ffn: float32 [2, 768], P('section')
- g_w_router: float32 [2, 768, 8], P('section')
- g_w_in: float32 [2, 8, 768, 3072], P('section', 'dp', None, 'tensor')
- g_w_exp_out: float32 [2, 8, 3072, 768], P('section', 'dp', 'tensor')
The draws below stay inside these ranges and needn't reach their ends.
Inputs may be any that keep to these rules, and one draw needn't show every extreme that they name: The 4 lengths of each group sum to 256, and the longest of each group is exactly 192. `routes`: within the 256 tokens of one group, one micro-batch and one layer, no expert is named by more than 64 tokens; in some of these blocks one expert is named by exactly 64.
All inputs are finite; a program needn't handle non-finite values.
Results may differ from the reference program's by a relative error of at most 0.025.
Values may be sent and summed in bfloat16 or wider, within the bound.
No kernel may reach another device: no remote copies, remote signals or barrier semaphores. Data moves between devices by JAX's collectives and lax.ppermute only.
A program may use at most 256 MiB of HBM per device.

```python
import math
import jax
import jax.numpy as jnp
import numpy as np
from jax import lax

D = 768
HD = 64
FF = 3072
MICRO = 4
NSEQ = 4
EXPERTS = 8
ROW = 256
LONGEST = 192
CAP = 64
TOKENS = 2048
N_SECTION = 2
N_DP = 8


def block_levels(rng, dims, shards, least, high):
    def one(axis_at, parts):
        steps = jax.random.uniform(jax.random.fold_in(jax.random.fold_in(rng, 6), axis_at), (parts,), jnp.float32, least / len(shards), high / len(shards))
        return jnp.repeat(jnp.exp(steps), dims[axis_at] // parts).reshape((-1,) + (1,) * (len(dims) - axis_at - 1))

    level = one(*shards[0])
    for cut in shards[1:]:
        level = level * one(*cut)
    return level


def profile(number_of, total, reach, lean):
    weights = [(1 << 20) // math.isqrt(rank ** lean) + 1 for rank in range(2, number_of + 1)]
    surplus, given = total - reach - (number_of - 1), [1] * (number_of - 1)
    while surplus > 0:
        candidates = [i for i in range(number_of - 1) if given[i] < reach]
        whole, remaining = sum([weights[i] for i in candidates]), surplus
        for i in candidates:
            extra = min(reach - given[i], max(1, remaining * weights[i] // whole), surplus)
            given[i] = given[i] + extra
            surplus = surplus - extra
    return np.array([reach] + given)


def ragged_sizes(rng, number_of, total, most, lean):
    if number_of == 2:
        one = jax.random.randint(rng, (), max(1, total - most), min(most, total - 1) + 1)
        return jnp.stack([one, total - one])
    tallies = jnp.asarray(profile(number_of, total, most, lean), jnp.int32)
    twos = (number_of - 1) // 2
    giver, sink = tallies[1:1 + 2 * twos:2], tallies[2:2 + 2 * twos:2]
    room = jnp.minimum(giver - 1, most - sink)
    moved = jax.random.randint(jax.random.fold_in(rng, 1), (twos,), 0, 1 << 20) % (room + 1)
    tallies = tallies.at[1:1 + 2 * twos:2].set(giver - moved).at[2:2 + 2 * twos:2].set(sink + moved)
    return tallies[jax.random.permutation(jax.random.fold_in(rng, 2), number_of)]


def deal_out(rng, own, number, rows, amount, top, limit, skew):
    order = jax.random.permutation(rng, amount)
    heavy_load, common = shares(amount, rows * top, limit, skew, True), shares(amount, rows * top, limit, skew, False)
    places = jnp.arange(amount)

    def named(tallies, rotation):
        used = int((tallies > 0).sum())
        fixed = max(1, used // 4)
        shifted = fixed + (places - fixed + rotation * (used - fixed)) % max(1, amount - fixed)
        return jnp.zeros((amount,), jnp.int32).at[order[jnp.where(places < fixed, places, shifted)]].set(jnp.asarray(tallies, jnp.int32))

    tallies = jnp.where(number % 4 == 0, named(heavy_load, number // 4), named(common, number - number // 4 - 1))
    mixed = jax.random.permutation(jax.random.fold_in(own, 3), amount)
    source_of, receiver = mixed[0:amount // 2 * 2:2], mixed[1:amount // 2 * 2:2]
    slack = jnp.minimum(tallies[source_of] - 1, limit - tallies[receiver]) // 2
    slack = jnp.where((source_of == order[0]) | (receiver == order[0]) | (tallies[receiver] == 0), 0, jnp.maximum(slack, 0))
    shifted = jax.random.randint(jax.random.fold_in(own, 4), (amount // 2,), 0, 1 << 20) % (slack + 1)
    tallies = tallies.at[source_of].add(-shifted).at[receiver].add(shifted)
    items = jnp.searchsorted(jnp.cumsum(tallies), jnp.arange(rows * top), side="right").astype(jnp.int32)
    listing = items.reshape(top, rows).T
    listing = listing[jax.random.permutation(jax.random.fold_in(own, 1), rows)]
    rotation = jax.random.randint(jax.random.fold_in(own, 2), (rows, 1), 0, top)
    return jnp.take_along_axis(listing, (jnp.arange(top)[None, :] + rotation) % top, axis=1)


def shares(count, total, limit, slope, full):
    loads = [(1 << 20) // math.isqrt(standing ** slope) + 1 for standing in range(1, count + 1)]
    largest = limit if full else min(limit, max(-(-total // count), total * loads[0] // sum(loads)))
    least = 1 if total - largest >= count - 1 else 0
    counts, spare = [largest] + [least] * (count - 1), total - largest - least * (count - 1)
    while spare > 0:
        movable = [i for i in range(1, count) if counts[i] < largest] or [i for i in range(1, count) if counts[i] < limit]
        mass, budget = sum([loads[i] for i in movable]), spare
        for i in movable:
            more = min(limit - counts[i], max(1, budget * loads[i] // mass), spare)
            counts[i] = counts[i] + more
            spare = spare - more
    return np.array(counts)


def bell_draw(stream_key, shape, deviation, reach, cuts=(), kind=jnp.bfloat16):
    loudness = block_levels(stream_key, shape, cuts, -0.22, 0.18) if cuts else 1.0
    entries = jax.random.normal(stream_key, shape, jnp.float32) * deviation * loudness
    return jnp.minimum(jnp.maximum(entries, -reach), reach).astype(kind)


def setup_inputs(seed: int = 0) -> dict:
    splits = jax.random.split(jax.random.key(seed), 12)
    x_in = bell_draw(splits[0], (MICRO, TOKENS, D), 1.0, 6.0, ((1, 16),))
    d_out = bell_draw(splits[1], (MICRO, TOKENS, D), 1.0, 6.0, ((1, 16),))
    lengths = jax.vmap(lambda own: ragged_sizes(own, NSEQ, ROW, LONGEST, 2))(jax.random.split(splits[2], MICRO * N_DP)).reshape((MICRO, N_DP, NSEQ)).astype(jnp.int32)
    routes_keys = jax.random.split(jax.random.fold_in(splits[3], 1), N_SECTION * MICRO * TOKENS // ROW)
    routes_turns = jax.random.permutation(jax.random.fold_in(splits[3], 3), N_SECTION * MICRO * TOKENS // ROW)
    routes = jax.vmap(lambda own, number: deal_out(jax.random.fold_in(splits[3], 2), own, number, ROW, EXPERTS, 1, CAP, 2))(routes_keys, routes_turns).reshape((N_SECTION, MICRO, TOKENS, 1))
    gain_attn = jnp.clip(1.0 + 0.1 * jax.random.normal(splits[4], (N_SECTION, D), jnp.float32), 0.5, 1.5).astype(jnp.bfloat16)
    w_qkv = bell_draw(splits[5], (N_SECTION, 3, D, D), D ** -0.5, 0.21875, ((0, 2), (2, 8), (3, 2)))
    w_attn_out = bell_draw(splits[6], (N_SECTION, D, D), (D // 16) ** -0.5, 0.875, ((0, 2), (1, 2), (2, 8)))
    gain_ffn = jnp.clip(1.0 + 0.1 * jax.random.normal(splits[7], (N_SECTION, D), jnp.float32), 0.5, 1.5).astype(jnp.bfloat16)
    w_router = bell_draw(splits[8], (N_SECTION, D, EXPERTS), (2 * D) ** -0.5, 0.15625, ((0, 2),))
    w_in = bell_draw(splits[9], (N_SECTION, EXPERTS, D, FF), D ** -0.5, 0.21875, ((0, 2), (1, 8), (3, 2)))
    w_exp_out = bell_draw(splits[10], (N_SECTION, EXPERTS, FF, D), (max(1, FF // (EXPERTS * EXPERTS))) ** -0.5, 0.875, ((0, 2), (1, 8), (2, 2)))
    return dict(x_in=x_in, d_out=d_out, lengths=lengths, routes=routes, gain_attn=gain_attn, w_qkv=w_qkv, w_attn_out=w_attn_out, gain_ffn=gain_ffn, w_router=w_router, w_in=w_in, w_exp_out=w_exp_out)


@jax.custom_vjp
def low(v):
    return lax.optimization_barrier(v.astype(jnp.bfloat16)).astype(jnp.float32)

@jax.custom_vjp
def low_back(v):
    return v

def low_keep(v):
    return (low(v), None)

def low_pass(kept, grad):
    return (grad,)

def back_keep(v):
    return (v, None)

def back_low(kept, grad):
    return (low(grad),)
low.defvjp(low_keep, low_pass)
low_back.defvjp(back_keep, back_low)
HIGH = lax.Precision.HIGHEST
EPSILON = 1e-06

def norm(inputs, gain):
    scaling = lax.rsqrt(lax.optimization_barrier(jnp.mean(inputs * inputs, axis=-1, keepdims=True)) + EPSILON)
    return inputs * scaling * gain

def sequence_mask(lengths_row, count):
    bounds = jnp.cumsum(lengths_row)
    places = jnp.arange(count, dtype=jnp.int32)
    segment = lax.optimization_barrier(jnp.sum((places[:, None] >= bounds[None, :]).astype(jnp.int32), axis=1))
    return (segment[:, None] == segment[None, :]) & (places[:, None] >= places[None, :])

def attend(qkv_w, normed_group, lengths_row):
    count = normed_group.shape[0]
    qkv = low(low_back(jnp.einsum('rd,cdk->crk', normed_group, qkv_w, precision=HIGH)))
    query = qkv[0].reshape(count, -1, HD)
    keys = qkv[1].reshape(count, -1, HD)
    values = qkv[2].reshape(count, -1, HD)
    scores = low_back(jnp.einsum('qhd,khd->hqk', query, keys, precision=HIGH) * (1.0 / math.sqrt(HD)))
    masked = jnp.where(sequence_mask(lengths_row, count)[None], scores, -1e+30)
    probs = low(jax.nn.softmax(masked, axis=-1))
    mixed = jnp.einsum('hqk,khd->qhd', probs, values, precision=HIGH).reshape(count, -1)
    return low(low_back(mixed))

def experts_branch(normed, router_w, in_w, expert_w, route_col, groups):
    tokens = normed.shape[0]
    experts = router_w.shape[1]
    group_rows = tokens // groups
    capacity = 2 * group_rows // experts
    chances = jax.nn.softmax(jnp.dot(normed, router_w, precision=HIGH), axis=-1)
    onehot = route_col[:, None] == jnp.arange(experts, dtype=jnp.int32)[None, :]
    gating = lax.optimization_barrier(jnp.sum(chances * onehot.astype(jnp.float32), axis=1))
    hot_int = onehot.astype(jnp.int32).reshape(groups, group_rows, experts)
    ranking = lax.optimization_barrier(jnp.sum((jnp.cumsum(hot_int, axis=1) - 1) * hot_int, axis=2)).reshape(tokens)
    places = jnp.arange(tokens, dtype=jnp.int32) // group_rows * capacity + ranking
    table = jnp.zeros((experts, groups * capacity), jnp.int32).at[route_col, places].set(jnp.arange(tokens, dtype=jnp.int32))
    filled = jnp.zeros((experts, groups * capacity), jnp.float32).at[route_col, places].set(1.0)
    gathered = normed[table] * filled[..., None]
    before = jnp.einsum('esd,edf->esf', gathered, in_w, precision=HIGH)
    active = low(jax.nn.gelu(low_back(before), approximate=True))
    result = jnp.einsum('esf,efd->esd', active, expert_w, precision=HIGH)
    picked = low_back(result[route_col, places])
    return gating[:, None] * picked

def layer(inputs, gain_a, qkv_w, out_w, gain_f, router_w, in_w, expert_w, lengths_mb, route_col):
    inputs = low_back(inputs)
    groups = lengths_mb.shape[0]
    tokens = inputs.shape[0]
    normed = low(norm(inputs, gain_a))
    step_fn = jax.checkpoint(lambda item: attend(qkv_w, item[0], item[1]))
    mixed = lax.map(step_fn, (normed.reshape(groups, tokens // groups, -1), lengths_mb))
    attended = low_back(jnp.dot(mixed.reshape(tokens, -1), out_w, precision=HIGH))
    hidden = inputs + attended
    normed_ffn = low(norm(hidden, gain_f))
    return hidden + experts_branch(normed_ffn, router_w, in_w, expert_w, route_col, groups)

def reference(x_in, d_out, lengths, routes, gain_attn, w_qkv, w_attn_out, gain_ffn, w_router, w_in, w_exp_out):
    weights = [tuple((arr[section_num].astype(jnp.float32) for arr in (gain_attn, w_qkv, w_attn_out, gain_ffn, w_router, w_in, w_exp_out))) for section_num in range(2)]
    totals = [tuple((jnp.zeros_like(arr) for arr in weights[section_num])) for section_num in range(2)]
    first_out, second_out, first_grad, second_grad = ([], [], [], [])
    for micro_num in range(x_in.shape[0]):
        lengths_mb = lengths[micro_num]
        route_first = routes[0, micro_num, :, 0]
        route_second = routes[1, micro_num, :, 0]

        def first_fn(inputs, *params):
            return low(layer(inputs, *params, lengths_mb, route_first))

        def second_fn(inputs, *params):
            return low(layer(inputs, *params, lengths_mb, route_second))
        first_val, first_back = jax.vjp(first_fn, x_in[micro_num].astype(jnp.float32), *weights[0])
        second_val, second_back = jax.vjp(second_fn, first_val, *weights[1])
        second_grads = second_back(d_out[micro_num].astype(jnp.float32))
        first_grads = first_back(second_grads[0])
        first_out.append(first_val)
        second_out.append(second_val)
        first_grad.append(first_grads[0])
        second_grad.append(second_grads[0])
        totals[0] = tuple((acc + new for acc, new in zip(totals[0], first_grads[1:])))
        totals[1] = tuple((acc + new for acc, new in zip(totals[1], second_grads[1:])))
    section_out = jnp.stack([jnp.stack(first_out), jnp.stack(second_out)]).astype(jnp.bfloat16)
    section_in_grad = jnp.stack([jnp.stack(first_grad), jnp.stack(second_grad)]).astype(jnp.bfloat16)
    stacked = [jnp.stack([totals[0][pos], totals[1][pos]]) for pos in range(7)]
    return (section_out, section_in_grad, stacked[0], stacked[1], stacked[2], stacked[3], stacked[4], stacked[5], stacked[6])
```

```python
import math

import jax
import jax.numpy as jnp
from jax import lax
from jax.sharding import PartitionSpec as P

HD = 64
EPSILON = 1e-06
NEGATIVE = -1e30
F32 = jnp.float32
BF16 = jnp.bfloat16


def swap(values, axis):
    return lax.ppermute(values, axis, [(0, 1), (1, 0)])


def one_way(values, axis, source, target):
    return lax.ppermute(values, axis, [(source, target)])


def all_to_all(values):
    return lax.all_to_all(values, "dp", split_axis=0, concat_axis=0, tiled=True)


def dot(left, right, left_dim, right_dim):
    return lax.dot_general(
        left, right, (((left_dim,), (right_dim,)), ((), ())), preferred_element_type=F32
    )


def ordered(index, own, other):
    return jnp.where(
        index == 0, jnp.concatenate([own, other], axis=0), jnp.concatenate([other, own], axis=0)
    )


def entry(array, index):
    return lax.dynamic_index_in_dim(array, index, 0, keepdims=False)


def norm_forward(inputs, gain):
    scaling = lax.rsqrt(jnp.mean(inputs * inputs, axis=-1, keepdims=True) + EPSILON)
    return (inputs * scaling * gain, scaling)


def norm_backward(upstream, inputs, scaling, gain):
    weighted = upstream * gain
    gain_grad = jnp.sum(upstream * inputs * scaling, axis=0)
    inner = jnp.mean(weighted * inputs, axis=-1, keepdims=True)
    return (scaling * weighted - inputs * scaling * scaling * scaling * inner, gain_grad)


def sequence_mask(lengths_row, count):
    bounds = jnp.cumsum(lengths_row)
    places = jnp.arange(count, dtype=jnp.int32)
    segment = jnp.sum((places[:, None] >= bounds[None, :]).astype(jnp.int32), axis=1)
    return (segment[:, None] == segment[None, :]) & (places[:, None] >= places[None, :])


def smooth_gate(values):
    return jax.nn.gelu(values, approximate=True)


def routing(route_row, experts):
    count = route_row.shape[0]
    capacity = 2 * count // experts
    hot = route_row[:, None] == jnp.arange(experts, dtype=jnp.int32)[None, :]
    places = jnp.arange(count, dtype=jnp.int32)
    earlier = (places[:, None] > places[None, :]).astype(BF16)
    ranks = dot(earlier, hot.astype(BF16), 1, 0)
    ranking = jnp.sum(ranks * hot.astype(F32), axis=1).astype(jnp.int32)
    slots = route_row * capacity + ranking
    placing = (
        slots[None, :] == jnp.arange(experts * capacity, dtype=jnp.int32)[:, None]
    ).astype(BF16)
    return (hot.astype(F32), placing)


def dispatch(placing, values):
    outgoing = dot(placing, values, 1, 0).astype(BF16)
    received = all_to_all(outgoing)
    return jnp.concatenate([received, swap(received, "tensor")], axis=0)


def collect(placing, partial):
    count = partial.shape[0] // 2
    total = partial[:count] + swap(partial[count:].astype(BF16), "tensor").astype(F32)
    return dot(placing, all_to_all(total.astype(BF16)), 0, 0)


def attention_parts(normed, weights, mask):
    count = normed.shape[0]
    qkvo = dot(normed, weights, 1, 0).astype(BF16).reshape(count, 2, 4, -1)
    query, key, value = (
        qkvo[:, :, part].reshape(count, -1, HD) for part in range(3)
    )
    scores = jnp.einsum("qhd,khd->hqk", query, key, preferred_element_type=F32)
    scores = jnp.where(mask[None], scores * (1.0 / math.sqrt(HD)), NEGATIVE)
    return (query, key, value, scores)


def layer_forward(inputs, params, mask, route_row):
    gain_a, gain_f, weights, router_w, in_w, expert_w = params
    count, width = inputs.shape
    normed, scale_attn = norm_forward(inputs, gain_a)
    normed = normed.astype(BF16)
    query, key, value, scores = attention_parts(normed, weights, mask)
    log_total = jax.nn.logsumexp(scores, axis=-1)
    probs = jnp.exp(scores - log_total[..., None])
    mixed = jnp.einsum("hqk,khd->qhd", probs.astype(BF16), value, preferred_element_type=F32)
    mixed = mixed.reshape(count, -1).astype(BF16)
    out_w = weights.reshape(width, 2, 4, -1)[:, :, 3].reshape(width, -1)
    hidden = inputs + dot(mixed, out_w, 1, 1)
    normed_ffn, scale_ffn = norm_forward(hidden, gain_f)
    normed_ffn = normed_ffn.astype(BF16)
    hot, placing = routing(route_row, router_w.shape[0])
    chances = jax.nn.softmax(dot(normed_ffn, router_w, 1, 1), axis=-1)
    gating = jnp.sum(chances * hot, axis=1)
    received = dispatch(placing, normed_ffn)
    before = dot(received, in_w, 1, 0)
    active = smooth_gate(before).astype(BF16)
    expert_out = collect(placing, dot(active, expert_w, 1, 0))
    result = (hidden + gating[:, None] * expert_out).astype(BF16)
    state = (
        inputs, scale_attn, normed, query, key, value, log_total, mixed, hidden, scale_ffn,
        normed_ffn, received, before, chances, gating, expert_out, hot, placing,
    )
    return (state, result)


def layer_backward(upstream, state, params, mask):
    (
        inputs, scale_attn, normed, query, key, value, log_total, mixed, hidden, scale_ffn,
        normed_ffn, received, before, chances, gating, expert_out, hot, placing,
    ) = state
    gain_a, gain_f, weights, router_w, in_w, expert_w = params
    count, width = inputs.shape
    gate_grad = jnp.sum(upstream * expert_out, axis=1)
    expert_grad = (gating[:, None] * upstream).astype(BF16)
    logit_grad = gating[:, None] * (hot - chances) * gate_grad[:, None]
    router_grad = jnp.dot(logit_grad.T, normed_ffn.astype(F32), precision=lax.Precision.HIGHEST)
    router_back = jnp.dot(logit_grad, router_w.astype(F32), precision=lax.Precision.HIGHEST)
    arriving = dispatch(placing, expert_grad)
    activated, gate_back = jax.vjp(smooth_gate, before)
    active_grad = dot(arriving, expert_w, 1, 1)
    before_grad = gate_back(active_grad)[0].astype(BF16)
    normed_grad = collect(placing, dot(before_grad, in_w, 1, 1)) + router_back
    in_w_grad = dot(received, before_grad, 0, 0)
    expert_w_grad = dot(activated.astype(BF16), arriving, 0, 0)
    hidden_part, gain_ffn_grad = norm_backward(normed_grad, hidden, scale_ffn, gain_f)
    hidden_grad = upstream + hidden_part
    attended_grad = hidden_grad.astype(BF16)
    split = weights.reshape(width, 2, 4, -1)
    out_w = split[:, :, 3].reshape(width, -1)
    mixed_heads = dot(attended_grad, out_w, 1, 0).astype(BF16).reshape(count, -1, HD)
    scores = jnp.einsum("qhd,khd->hqk", query, key, preferred_element_type=F32)
    scores = jnp.where(mask[None], scores * (1.0 / math.sqrt(HD)), NEGATIVE)
    probs = jnp.exp(scores - log_total[..., None])
    value_grad = jnp.einsum(
        "hqk,qhd->khd", probs.astype(BF16), mixed_heads, preferred_element_type=F32
    )
    prob_grad = jnp.einsum("qhd,khd->hqk", mixed_heads, value, preferred_element_type=F32)
    inner = jnp.sum(probs * prob_grad, axis=-1, keepdims=True)
    score_grad = (probs * (prob_grad - inner)).astype(BF16)
    factor = 1.0 / math.sqrt(HD)
    query_grad = jnp.einsum("hqk,khd->qhd", score_grad, key, preferred_element_type=F32) * factor
    key_grad = jnp.einsum("hqk,qhd->khd", score_grad, query, preferred_element_type=F32) * factor
    grads = [
        part.reshape(count, 2, 1, -1).astype(BF16) for part in (query_grad, key_grad, value_grad)
    ]
    qkv_grad = jnp.concatenate(grads, axis=2)
    qkv_w = split[:, :, :3].reshape(width, -1)
    normed_back = dot(qkv_grad.reshape(count, -1), qkv_w, 1, 1)
    qkv_w_grad = dot(normed, qkv_grad.reshape(count, -1), 0, 0).reshape(width, 2, 3, -1)
    out_w_grad = dot(attended_grad, mixed, 0, 0).reshape(width, 2, 1, -1)
    attn_grad = jnp.concatenate([qkv_w_grad, out_w_grad], axis=2).reshape(width, 2, -1)
    input_part, gain_attn_grad = norm_backward(normed_back, inputs, scale_attn, gain_a)
    input_grad = (hidden_grad + input_part).astype(BF16)
    small = jnp.concatenate([gain_attn_grad[None], gain_ffn_grad[None], router_grad], axis=0)
    return (input_grad, attn_grad, small, in_w_grad, expert_w_grad)


def reduce_attention(grad, section):
    width = grad.shape[0]
    count = lax.axis_size("dp")
    mine = grad[:, 0] + swap(grad[:, 1].astype(BF16), "tensor").astype(F32)
    halves = mine.reshape(count, 2, width // count // 2, -1)
    keep = lax.dynamic_index_in_dim(halves, section, 1, keepdims=False)
    send = lax.dynamic_index_in_dim(halves, 1 - section, 1, keepdims=False)
    total = keep + swap(send.astype(BF16), "section").astype(F32)
    return all_to_all(total.astype(BF16)).astype(F32).sum(axis=0)


def pair_up(values, tensor):
    half = values.shape[0] // 2
    halves = values.reshape(2, half, -1)
    own = entry(halves, tensor)
    other = swap(entry(halves, 1 - tensor), "tensor")
    return ordered(tensor, own[None], other[None])


def by_section(pairs, section):
    first, second = pairs
    own = jnp.where(section == 0, first, second)
    other = swap(jnp.where(section == 0, second, first), "section")
    return ordered(section, own, other)


def shards(
    x_in, d_out, lengths, routes, gain_attn, w_qkv, w_attn_out, gain_ffn, w_router, w_in, w_exp_out
):
    section = lax.axis_index("section")
    tensor = lax.axis_index("tensor")
    count = lax.axis_size("dp")
    width = x_in.shape[2]
    rows = 2 * x_in.shape[1]
    own_batch = 2 * section + tensor
    peer_batch = 2 * section + 1 - tensor

    def by_layer(own):
        other = swap(own, "section")
        return [jnp.where(section == layer, own, other) for layer in range(2)]

    packed = jnp.concatenate([w_qkv[0], w_attn_out[0].T[None]], axis=0)
    packed = jnp.moveaxis(packed, 0, 1).reshape(width // count, -1)
    packs = by_layer(packed)
    attn_w = [
        lax.all_gather(
            jnp.concatenate([pack, swap(pack, "tensor")], axis=1), "dp", axis=0, tiled=True
        )
        for pack in packs
    ]
    small = by_layer(jnp.concatenate([gain_attn, gain_ffn, w_router[0].T], axis=0))
    own_route = entry(routes[0, :, :, 0], own_batch)
    other_route = swap(entry(routes[0, :, :, 0], 2 * (1 - section) + tensor), "section")
    route = [jnp.where(section == layer, own_route, other_route) for layer in range(2)]
    in_w = by_layer(w_in[0, 0])
    expert_w = by_layer(w_exp_out[0, 0])
    params = [
        (
            small[layer][0].astype(F32),
            small[layer][1].astype(F32),
            attn_w[layer],
            small[layer][2:],
            in_w[layer],
            expert_w[layer],
        )
        for layer in range(2)
    ]
    mask = sequence_mask(entry(lengths[:, 0], own_batch), rows)

    def whole_group(array):
        return ordered(
            tensor, entry(array, own_batch), swap(entry(array, peer_batch), "tensor")
        )

    first = whole_group(x_in).astype(F32)
    upstream = whole_group(d_out).astype(F32)
    state0, out0 = layer_forward(first, params[0], mask, route[0])
    state1, out1 = layer_forward(out0.astype(F32), params[1], mask, route[1])
    grad1, attn1, small1, in1, expert1 = layer_backward(upstream, state1, params[1], mask)
    grad0, attn0, small0, in0, expert0 = layer_backward(grad1.astype(F32), state0, params[0], mask)
    section_out = by_section([pair_up(out0, tensor), pair_up(out1, tensor)], section)
    section_in_grad = by_section([pair_up(grad0, tensor), pair_up(grad1, tensor)], section)

    def settle(first_grad, second_grad):
        from_second = one_way(first_grad.astype(BF16), "section", 1, 0).astype(F32)
        from_first = one_way(second_grad.astype(BF16), "section", 0, 1).astype(F32)
        return jnp.where(section == 0, first_grad + from_second, second_grad + from_first)

    in_w_grad = settle(in0, in1)
    expert_w_grad = settle(expert0, expert1)
    reduced = [reduce_attention(attn0, section), reduce_attention(attn1, section)]
    own_half = jnp.where(section == 0, reduced[0], reduced[1])
    other_half = swap(
        jnp.where(section == 0, reduced[1], reduced[0]).astype(BF16), "section"
    ).astype(F32)
    attn_grad = ordered(section, own_half, other_half).reshape(width // count, 4, -1)
    qkv_grad = jnp.moveaxis(attn_grad[:, :3], 1, 0)
    out_grad = attn_grad[:, 3].T
    own_small = jnp.where(section == 0, small0, small1)
    own_small = own_small + swap(jnp.where(section == 0, small1, small0), "section")
    own_small = own_small + swap(own_small, "tensor")
    spread = jnp.broadcast_to(own_small[None], (count,) + own_small.shape)
    own_small = jnp.sum(all_to_all(spread), axis=0)
    return (
        section_out[None],
        section_in_grad[None],
        own_small[0][None],
        qkv_grad[None],
        out_grad[None],
        own_small[1][None],
        own_small[2:].T[None],
        in_w_grad[None, None],
        expert_w_grad[None, None],
    )


def solution(mesh):
    in_specs = (
        P(None, ("dp", "tensor"), None),
        P(None, ("dp", "tensor"), None),
        P(None, "dp", None),
        P("section", None, "dp", None),
        P("section", None),
        P("section", None, "dp", "tensor"),
        P("section", "tensor", "dp"),
        P("section", None),
        P("section", None, None),
        P("section", "dp", None, "tensor"),
        P("section", "dp", "tensor", None),
    )
    out_specs = (
        P("section", None, ("dp", "tensor"), None),
        P("section", None, ("dp", "tensor"), None),
        P("section", None),
        P("section", None, "dp", "tensor"),
        P("section", "tensor", "dp"),
        P("section", None),
        P("section", None, None),
        P("section", "dp", None, "tensor"),
        P("section", "dp", "tensor", None),
    )
    return jax.shard_map(shards, mesh=mesh, in_specs=in_specs, out_specs=out_specs, check_vma=False)
```

```python
import functools
import math

import jax
import jax.numpy as jnp
from jax import lax
from jax.experimental import pallas as pl
from jax.experimental.pallas import tpu as pltpu
from jax.sharding import PartitionSpec as P

HD = 64
EPSILON = 1e-06
NEGATIVE = -1e30
F32 = jnp.float32
BF16 = jnp.bfloat16


def swap(values, axis):
    return lax.ppermute(values, axis, [(0, 1), (1, 0)])


def one_way(values, axis, source, target):
    return lax.ppermute(values, axis, [(source, target)])


def all_to_all(values):
    return lax.all_to_all(values, "dp", split_axis=0, concat_axis=0, tiled=True)


def dot(left, right, left_dim, right_dim):
    return lax.dot_general(
        left, right, (((left_dim,), (right_dim,)), ((), ())), preferred_element_type=F32
    )


def ordered(index, own, other):
    return jnp.where(
        index == 0, jnp.concatenate([own, other], axis=0), jnp.concatenate([other, own], axis=0)
    )


def entry(array, index):
    return lax.dynamic_index_in_dim(array, index, 0, keepdims=False)


def norm_forward(inputs, gain):
    scaling = lax.rsqrt(jnp.mean(inputs * inputs, axis=-1, keepdims=True) + EPSILON)
    return (inputs * scaling * gain, scaling)


def smooth_gate(values):
    return jax.nn.gelu(values, approximate=True)


def routing(route_row, experts):
    count = route_row.shape[0]
    capacity = 2 * count // experts
    hot = route_row[:, None] == jnp.arange(experts, dtype=jnp.int32)[None, :]
    places = jnp.arange(count, dtype=jnp.int32)
    earlier = (places[:, None] > places[None, :]).astype(BF16)
    ranks = dot(earlier, hot.astype(BF16), 1, 0)
    ranking = jnp.sum(ranks * hot.astype(F32), axis=1).astype(jnp.int32)
    slots = route_row * capacity + ranking
    placing = (
        slots[None, :] == jnp.arange(experts * capacity, dtype=jnp.int32)[:, None]
    ).astype(BF16)
    return (hot.astype(F32), placing)


LANES = 128


def head_lanes(count):
    return lax.broadcasted_iota(jnp.int32, (count, LANES), 1) // HD


def attention_bias(seg_col, seg_row, count):
    rows = lax.broadcasted_iota(jnp.int32, (count, count), 0)
    cols = lax.broadcasted_iota(jnp.int32, (count, count), 1)
    return jnp.where((seg_col == seg_row) & (rows >= cols), 0.0, NEGATIVE)


def forward_kernel(
    a_ref, w_ref, gain_ref, router_ref, seg_col_ref, seg_row_ref, route_ref, placing_ref,
    xn_ref, qkv_ref, lse_ref, o_ref, h_ref, hn_ref, chances_ref, gate_ref, out_ref, *, experts,
):
    count, width = a_ref.shape
    part = width // 2
    pairs = part // LANES
    a = a_ref[...].astype(F32)
    xn = norm_forward(a, gain_ref[0:1, :])[0].astype(BF16)
    xn_ref[...] = xn
    bias = attention_bias(seg_col_ref[...], seg_row_ref[...], count)
    lanes = head_lanes(count)
    scale = 1.0 / math.sqrt(HD)
    for half in range(2):
        base = half * 3 * part
        qkv_ref[:, base:base + 3 * part] = dot(
            xn, w_ref[:, half * 4 * part:half * 4 * part + 3 * part], 1, 0
        ).astype(BF16)
    attended = a
    lse = jnp.zeros((count, LANES), F32)
    for half in range(2):
        base = half * 3 * part
        for pair in range(pairs):
            at = base + pair * LANES
            query = qkv_ref[:, at:at + LANES]
            key = qkv_ref[:, at + part:at + part + LANES]
            value = qkv_ref[:, at + 2 * part:at + 2 * part + LANES]
            mixed = None
            for head in range(2):
                own = jnp.where(lanes == head, query, jnp.zeros_like(query))
                scores = dot(own, key, 1, 1) * scale + bias
                top = jnp.max(scores, axis=-1, keepdims=True)
                weight = jnp.exp(scores - top)
                total = jnp.sum(weight, axis=-1, keepdims=True)
                probs = (weight * (1.0 / total)).astype(BF16)
                number = (half * pairs + pair) * 2 + head
                lse = jnp.where(
                    lax.broadcasted_iota(jnp.int32, lse.shape, 1) == number,
                    top + jnp.log(total), lse,
                )
                part_out = dot(probs, value, 1, 0)
                mixed = part_out if head == 0 else jnp.where(lanes == 0, mixed, part_out)
            o_at = half * part + pair * LANES
            o_ref[:, o_at:o_at + LANES] = mixed.astype(BF16)
        attended = attended + dot(
            o_ref[:, half * part:(half + 1) * part],
            w_ref[:, half * 4 * part + 3 * part:(half + 1) * 4 * part], 1, 1,
        )
    lse_ref[...] = lse
    h_ref[...] = attended
    hn = norm_forward(attended, gain_ref[1:2, :])[0].astype(BF16)
    hn_ref[...] = hn
    logits = dot(hn, router_ref[...], 1, 1)
    lane = lax.broadcasted_iota(jnp.int32, logits.shape, 1)
    logits = jnp.where(lane < experts, logits, NEGATIVE)
    raised = jnp.exp(logits - jnp.max(logits, axis=-1, keepdims=True))
    chances = raised * (1.0 / jnp.sum(raised, axis=-1, keepdims=True))
    chances_ref[...] = chances
    gate_ref[...] = jnp.sum(
        jnp.where(lane == route_ref[...], chances, 0.0), axis=-1, keepdims=True
    )
    out_ref[...] = dot(placing_ref[...], hn, 1, 0).astype(BF16)


def backward_kernel(
    back_ref, taking_ref, dz_ref, y_ref, a_ref, h_ref, hn_ref, qkv_ref, lse_ref, chances_ref,
    gate_ref, w_ref, gain_ref, router_ref, seg_col_ref, seg_row_ref, route_ref,
    da_ref, dqkv_ref, dattn_ref, small_ref, g_router_ref,
):
    count, width = a_ref.shape
    part = width // 2
    pairs = part // LANES
    dz = dz_ref[...].astype(F32)
    hidden = h_ref[...]
    chances = chances_ref[...]
    gate_grad = jnp.sum(dz * y_ref[...], axis=-1, keepdims=True)
    lane = lax.broadcasted_iota(jnp.int32, chances.shape, 1)
    hot = jnp.where(lane == route_ref[...], 1.0, 0.0)
    logit_grad = gate_ref[...] * (hot - chances) * gate_grad
    g_router_ref[...] = lax.dot_general(
        logit_grad, hn_ref[...].astype(F32), (((0,), (0,)), ((), ())),
        preferred_element_type=F32, precision=lax.Precision.HIGHEST,
    )
    hn_grad = dot(taking_ref[...], back_ref[...], 1, 0) + lax.dot_general(
        logit_grad, router_ref[...].astype(F32), (((1,), (0,)), ((), ())),
        preferred_element_type=F32, precision=lax.Precision.HIGHEST,
    )

    def norm_back(upstream, inputs, gain):
        scaling = lax.rsqrt(jnp.mean(inputs * inputs, axis=-1, keepdims=True) + EPSILON)
        weighted = upstream * gain
        scaled = inputs * scaling
        inner = jnp.mean(weighted * inputs, axis=-1, keepdims=True)
        return (
            scaling * weighted - scaled * (scaling * scaling * inner),
            jnp.sum(upstream * scaled, axis=0, keepdims=True),
        )

    hidden_part, gain_f_grad = norm_back(hn_grad, hidden, gain_ref[1:2, :])
    hidden_grad = dz + hidden_part
    attended_grad = hidden_grad.astype(BF16)
    dattn_ref[...] = attended_grad
    bias = attention_bias(seg_col_ref[...], seg_row_ref[...], count)
    lanes = head_lanes(count)
    scale = 1.0 / math.sqrt(HD)
    normed_grad = jnp.zeros((count, width), F32)
    for half in range(2):
        base = half * 3 * part
        mixed_grad = dot(
            attended_grad, w_ref[:, half * 4 * part + 3 * part:(half + 1) * 4 * part], 1, 0
        ).astype(BF16)
        for pair in range(pairs):
            at = base + pair * LANES
            query = qkv_ref[:, at:at + LANES]
            key = qkv_ref[:, at + part:at + part + LANES]
            value = qkv_ref[:, at + 2 * part:at + 2 * part + LANES]
            grad = mixed_grad[:, pair * LANES:(pair + 1) * LANES]
            dq = dk = dv = None
            for head in range(2):
                number = (half * pairs + pair) * 2 + head
                zero = jnp.zeros_like(query)
                own_q = jnp.where(lanes == head, query, zero)
                own_g = jnp.where(lanes == head, grad, zero)
                scores = dot(own_q, key, 1, 1) * scale + bias
                probs = jnp.exp(scores - lse_ref[:, number:number + 1])
                prob_grad = dot(own_g, value, 1, 1)
                inner = jnp.sum(probs * prob_grad, axis=-1, keepdims=True)
                score_grad = (probs * (prob_grad - inner)).astype(BF16)
                head_dv = dot(probs.astype(BF16), own_g, 0, 0)
                head_dk = dot(score_grad, own_q, 0, 0)
                head_dq = dot(score_grad, key, 1, 0)
                if head == 0:
                    dq, dk, dv = (head_dq, head_dk, head_dv)
                else:
                    dq = jnp.where(lanes == 0, dq, head_dq)
                    dk = dk + head_dk
                    dv = dv + head_dv
            dqkv_ref[:, at:at + LANES] = (dq * scale).astype(BF16)
            dqkv_ref[:, at + part:at + part + LANES] = (dk * scale).astype(BF16)
            dqkv_ref[:, at + 2 * part:at + 2 * part + LANES] = dv.astype(BF16)
        normed_grad = normed_grad + dot(
            dqkv_ref[:, base:base + 3 * part],
            w_ref[:, half * 4 * part:half * 4 * part + 3 * part], 1, 1,
        )
    input_part, gain_a_grad = norm_back(normed_grad, a_ref[...].astype(F32), gain_ref[0:1, :])
    small_ref[0:1, :] = gain_a_grad
    small_ref[1:2, :] = gain_f_grad
    da_ref[...] = (hidden_grad + input_part).astype(BF16)


def kernel_call(kernel, outs, flops, *args):
    moved = sum(math.prod(v.shape) * v.dtype.itemsize for v in (*args, *outs))
    return pl.pallas_call(
        kernel,
        out_shape=outs,
        in_specs=[pl.BlockSpec(memory_space=pltpu.VMEM)] * len(args),
        out_specs=[pl.BlockSpec(memory_space=pltpu.VMEM)] * len(outs),
        compiler_params=pltpu.CompilerParams(vmem_limit_bytes=48 * 1024 * 1024),
        cost_estimate=pl.CostEstimate(flops=flops, bytes_accessed=moved, transcendentals=0),
    )(*args)


def layer_start(inputs, params, segments, route_col, placing):
    gains, weights, router_w, experts = params
    count, width = inputs.shape
    struct = jax.ShapeDtypeStruct
    outs = [
        struct((count, width), BF16),
        struct((count, 3 * width), BF16),
        struct((count, LANES), F32),
        struct((count, width), BF16),
        struct((count, width), F32),
        struct((count, width), BF16),
        struct((count, LANES), F32),
        struct((count, 1), F32),
        struct((placing.shape[0], width), BF16),
    ]
    return kernel_call(
        functools.partial(forward_kernel, experts=experts), outs, 3 * 10**9,
        inputs, weights, gains, router_w, *segments, route_col, placing,
    )


def layer_end(back, taking, upstream, expert_out, inputs, state, params, segments, route_col):
    gains, weights, router_w, experts = params
    normed, qkv, lse, mixed, hidden, normed_ffn, chances, gate = state
    count, width = inputs.shape
    struct = jax.ShapeDtypeStruct
    outs = [
        struct((count, width), BF16),
        struct((count, 3 * width), BF16),
        struct((count, width), BF16),
        struct((2, width), F32),
        struct((LANES, width), F32),
    ]
    return kernel_call(
        backward_kernel, outs, 5 * 10**9,
        back, taking, upstream, expert_out, inputs, hidden, normed_ffn, qkv, lse, chances,
        gate, weights, gains, router_w, *segments, route_col,
    )

def attention_grads(normed, qkv_grad, mixed, attended_grad, section):
    width = normed.shape[1]
    part = width // 2

    def both(left, right):
        left = jnp.concatenate([left, swap(left, "tensor")], axis=0)
        wide = right.shape[1] // 2
        right = jnp.concatenate([right[:, :wide], swap(right[:, wide:], "tensor")], axis=0)
        return across(dot(left, right, 0, 0), section)

    return jnp.concatenate([both(normed, qkv_grad), both(attended_grad, mixed)], axis=1)


def across(grad, section):
    width = grad.shape[0]
    count = lax.axis_size("dp")
    halves = grad.reshape(count, 2, width // count // 2, -1)
    keep = lax.dynamic_index_in_dim(halves, section, 1, keepdims=False)
    send = lax.dynamic_index_in_dim(halves, 1 - section, 1, keepdims=False)
    total = keep + swap(send.astype(BF16), "section").astype(F32)
    return all_to_all(total.astype(BF16)).astype(F32).sum(axis=0)


def pair_up(values, tensor):
    half = values.shape[0] // 2
    halves = values.reshape(2, half, -1)
    own = entry(halves, tensor)
    other = swap(entry(halves, 1 - tensor), "tensor")
    return ordered(tensor, own[None], other[None])


def by_section(pairs, section):
    first, second = pairs
    own = jnp.where(section == 0, first, second)
    other = swap(jnp.where(section == 0, second, first), "section")
    return ordered(section, own, other)


def gelu_pair(before, active_grad):
    activated, back = jax.vjp(smooth_gate, before)
    return (activated.astype(BF16), back(active_grad)[0].astype(BF16))


def shards(
    x_in, d_out, lengths, routes, gain_attn, w_qkv, w_attn_out, gain_ffn, w_router, w_in, w_exp_out
):
    section = lax.axis_index("section")
    tensor = lax.axis_index("tensor")
    count = lax.axis_size("dp")
    width = x_in.shape[2]
    rows = 2 * x_in.shape[1]
    experts = w_router.shape[2]
    own_batch = 2 * section + tensor
    peer_batch = 2 * section + 1 - tensor

    def by_layer(own):
        other = swap(own, "section")
        return [jnp.where(section == layer, own, other) for layer in range(2)]

    packed = jnp.concatenate([w_qkv[0], w_attn_out[0].T[None]], axis=0)
    packed = jnp.moveaxis(packed, 0, 1).reshape(width // count, -1)
    beside = by_layer(packed)
    cross = lax.ppermute(packed, ("section", "tensor"), [(0, 3), (1, 2), (2, 1), (3, 0)])
    above = swap(packed, "tensor")
    beyond = [jnp.where(section == layer, above, cross) for layer in range(2)]
    attn_w = [
        lax.all_gather(
            jnp.concatenate([beside[layer], beyond[layer]], axis=1), "dp", axis=0, tiled=True
        )
        for layer in range(2)
    ]
    small = by_layer(jnp.concatenate([gain_attn, gain_ffn, w_router[0].T], axis=0))
    own_route = entry(routes[0, :, :, 0], own_batch)
    other_route = swap(entry(routes[0, :, :, 0], 2 * (1 - section) + tensor), "section")
    route = [jnp.where(section == layer, own_route, other_route) for layer in range(2)]
    placing = [routing(row, experts)[1] for row in route]
    taking = [table.T for table in placing]
    route_col = [row[:, None] for row in route]
    in_w = by_layer(w_in[0, 0])
    expert_w = by_layer(w_exp_out[0, 0])
    params = [
        (
            small[layer][:2].astype(F32),
            attn_w[layer],
            jnp.pad(small[layer][2:], ((0, LANES - experts), (0, 0))),
            experts,
        )
        for layer in range(2)
    ]
    bounds = jnp.cumsum(entry(lengths[:, 0], own_batch))
    places = jnp.arange(rows, dtype=jnp.int32)
    segment = jnp.sum((places[:, None] >= bounds[None, :]).astype(jnp.int32), axis=1)
    segments = (segment[:, None], segment[None, :])

    def whole_group(array):
        return ordered(
            tensor, entry(array, own_batch), swap(entry(array, peer_batch), "tensor")
        )

    def spread(outgoing):
        received = all_to_all(outgoing)
        return jnp.concatenate([received, swap(received, "tensor")], axis=0)

    def gathered(partial):
        half = partial.shape[0] // 2
        total = partial[:half] + swap(partial[half:].astype(BF16), "tensor").astype(F32)
        return all_to_all(total.astype(BF16))

    inputs = [whole_group(x_in), None]
    upstream = [None, whole_group(d_out)]
    states, received, before, expert_out, outs = ([], [], [], [], [])
    for layer in range(2):
        *state, outgoing = layer_start(
            inputs[layer], params[layer], segments, route_col[layer], placing[layer]
        )
        states.append(state)
        received.append(spread(outgoing))
        before.append(dot(received[layer], in_w[layer], 1, 0))
        active = smooth_gate(before[layer]).astype(BF16)
        back = gathered(dot(active, expert_w[layer], 1, 0))
        expert_out.append(dot(taking[layer], back, 1, 0))
        outs.append((state[4] + state[7] * expert_out[layer]).astype(BF16))
        if layer == 0:
            inputs[1] = outs[0]
    section_out = by_section([pair_up(out, tensor) for out in outs], section)
    arriving, active, before_grad = ([None, None], [None, None], [None, None])
    input_grads, attn_grads, smalls = ([None, None], [None, None], [None, None])
    for layer in (1, 0):
        state = states[layer]
        expert_grad = (state[7] * upstream[layer].astype(F32)).astype(BF16)
        arriving[layer] = spread(dot(placing[layer], expert_grad, 1, 0).astype(BF16))
        active[layer], before_grad[layer] = gelu_pair(
            before[layer], dot(arriving[layer], expert_w[layer], 1, 1)
        )
        back = gathered(dot(before_grad[layer], in_w[layer], 1, 1))
        input_grads[layer], qkv_grad, attended_grad, gains, g_router = layer_end(
            back, taking[layer], upstream[layer], expert_out[layer], inputs[layer], state,
            params[layer], segments, route_col[layer],
        )
        attn_grads[layer] = attention_grads(state[0], qkv_grad, state[3], attended_grad, section)
        smalls[layer] = jnp.concatenate([gains, g_router[:experts]], axis=0)
        if layer == 1:
            upstream[0] = input_grads[1]
    section_in_grad = by_section([pair_up(grad, tensor) for grad in input_grads], section)

    def own_layer(pair):
        return jnp.where(section == 0, pair[0], pair[1])

    def other_layer(pair):
        return jnp.where(section == 0, pair[1], pair[0])

    def from_other(pair):
        return jnp.where(
            section == 0, one_way(pair[0], "section", 1, 0), one_way(pair[1], "section", 0, 1)
        )

    far_rows = from_other(received)
    far_grads = from_other(arriving)
    far_before = dot(far_rows, w_in[0, 0], 1, 0)
    far_active, far_before_grad = gelu_pair(far_before, dot(far_grads, w_exp_out[0, 0], 1, 1))
    in_w_grad = dot(own_layer(received), own_layer(before_grad), 0, 0) + dot(
        far_rows, far_before_grad, 0, 0
    )
    expert_w_grad = dot(own_layer(active), own_layer(arriving), 0, 0) + dot(
        far_active, far_grads, 0, 0
    )
    own_half = own_layer(attn_grads)
    other_half = swap(other_layer(attn_grads).astype(BF16), "section").astype(F32)
    joined = ordered(section, own_half, other_half)
    part = width // 2
    qkv_grad = jnp.stack([joined[:, part * kind:part * (kind + 1)] for kind in range(3)])
    out_grad = joined[:, 3 * part:].T
    own_small = own_layer(smalls) + swap(other_layer(smalls), "section")
    own_small = own_small + swap(own_small, "tensor")
    copies = jnp.broadcast_to(own_small[None], (count,) + own_small.shape)
    own_small = jnp.sum(all_to_all(copies), axis=0)
    return (
        section_out[None],
        section_in_grad[None],
        own_small[0][None],
        qkv_grad[None],
        out_grad[None],
        own_small[1][None],
        own_small[2:].T[None],
        in_w_grad[None, None],
        expert_w_grad[None, None],
    )


def solution(mesh):
    in_specs = (
        P(None, ("dp", "tensor"), None),
        P(None, ("dp", "tensor"), None),
        P(None, "dp", None),
        P("section", None, "dp", None),
        P("section", None),
        P("section", None, "dp", "tensor"),
        P("section", "tensor", "dp"),
        P("section", None),
        P("section", None, None),
        P("section", "dp", None, "tensor"),
        P("section", "dp", "tensor", None),
    )
    out_specs = (
        P("section", None, ("dp", "tensor"), None),
        P("section", None, ("dp", "tensor"), None),
        P("section", None),
        P("section", None, "dp", "tensor"),
        P("section", "tensor", "dp"),
        P("section", None),
        P("section", None, None),
        P("section", "dp", None, "tensor"),
        P("section", "dp", "tensor", None),
    )
    return jax.shard_map(shards, mesh=mesh, in_specs=in_specs, out_specs=out_specs, check_vma=False)
```

```python
import functools
import math

import jax
import jax.numpy as jnp
from jax import lax
from jax.experimental import pallas as pl
from jax.experimental.pallas import tpu as pltpu
from jax.sharding import PartitionSpec as P

HD = 64
LANES = 128
EPSILON = 1e-06
NEGATIVE = -1e30
F32 = jnp.float32
BF16 = jnp.bfloat16
CUBIC = 0.044715
SLOPE = math.sqrt(2.0 / math.pi)


def swap(values, axis):
    return lax.ppermute(values, axis, [(0, 1), (1, 0)])


def one_way(values, axis, source, target):
    return lax.ppermute(values, axis, [(source, target)])


def all_to_all(values):
    return lax.all_to_all(values, "dp", split_axis=0, concat_axis=0, tiled=True)


def after(value, *anchors):
    return lax.optimization_barrier((value, anchors))[0]


def dot(left, right, left_dim, right_dim):
    return lax.dot_general(
        left, right, (((left_dim,), (right_dim,)), ((), ())), preferred_element_type=F32
    )


def ordered(index, own, other):
    return jnp.where(
        index == 0, jnp.concatenate([own, other], axis=0), jnp.concatenate([other, own], axis=0)
    )


def entry(array, index):
    return lax.dynamic_index_in_dim(array, index, 0, keepdims=False)


def norm_forward(inputs, gain):
    scaling = lax.rsqrt(jnp.mean(inputs * inputs, axis=-1, keepdims=True) + EPSILON)
    return inputs * scaling * gain


def norm_back(upstream, inputs, gain):
    scaling = lax.rsqrt(jnp.mean(inputs * inputs, axis=-1, keepdims=True) + EPSILON)
    weighted = upstream * gain
    scaled = inputs * scaling
    inner = jnp.mean(weighted * inputs, axis=-1, keepdims=True)
    return (
        scaling * weighted - scaled * (scaling * scaling * inner),
        jnp.sum(upstream * scaled, axis=0, keepdims=True),
    )


def smooth_gate(values):
    return jax.nn.gelu(values, approximate=True)


def routing(route_row, experts):
    count = route_row.shape[0]
    capacity = 2 * count // experts
    hot = route_row[:, None] == jnp.arange(experts, dtype=jnp.int32)[None, :]
    places = jnp.arange(count, dtype=jnp.int32)
    earlier = (places[:, None] > places[None, :]).astype(BF16)
    ranks = dot(earlier, hot.astype(BF16), 1, 0)
    ranking = jnp.sum(ranks * hot.astype(F32), axis=1).astype(jnp.int32)
    slots = route_row * capacity + ranking
    places = jnp.arange(experts * capacity, dtype=jnp.int32)
    return (
        (slots[None, :] == places[:, None]).astype(BF16),
        (slots[:, None] == places[None, :]).astype(BF16),
    )


def head_lanes(count):
    return lax.broadcasted_iota(jnp.int32, (count, LANES), 1) // HD


def attention_bias(seg_col, seg_row, count):
    rows = lax.broadcasted_iota(jnp.int32, (count, count), 0)
    cols = lax.broadcasted_iota(jnp.int32, (count, count), 1)
    return jnp.where((seg_col == seg_row) & (rows >= cols), 0.0, NEGATIVE)


def expert_chances(rows, router, experts):
    logits = dot(rows, router, 1, 1)
    lane = lax.broadcasted_iota(jnp.int32, logits.shape, 1)
    logits = jnp.where(lane < experts, logits, NEGATIVE)
    raised = jnp.exp(logits - jnp.max(logits, axis=-1, keepdims=True))
    return raised * (1.0 / jnp.sum(raised, axis=-1, keepdims=True))


def forward_kernel(get, outs, *, experts, joined):
    (xn_ref, qkv_ref, lse_ref, o_ref, h_ref, gate_ref, out_ref) = outs[:7]
    if joined:
        mixed_in = dot(get("taking")[...], get("back")[...], 1, 0)
        result = (get("h_before")[...] + get("gate_before")[...] * mixed_in).astype(BF16)
        outs[7][...] = result
        a = result.astype(F32)
    else:
        a = get("a")[...].astype(F32)
    count, width = a.shape
    part = width // 2
    pairs = part // LANES
    gains = get("gains")
    xn = norm_forward(a, gains[0:1, :]).astype(BF16)
    xn_ref[...] = xn
    bias = attention_bias(get("seg_col")[...], get("seg_row")[...], count)
    lanes = head_lanes(count)
    scale = 1.0 / math.sqrt(HD)
    w_ref = get("weights")
    for half in range(2):
        base = half * 3 * part
        qkv_ref[:, base:base + 3 * part] = dot(
            xn, w_ref[:, half * 4 * part:half * 4 * part + 3 * part], 1, 0
        ).astype(BF16)
    attended = a
    lse = jnp.zeros((count, LANES), F32)
    for half in range(2):
        base = half * 3 * part
        for pair in range(pairs):
            at = base + pair * LANES
            query = qkv_ref[:, at:at + LANES]
            key = qkv_ref[:, at + part:at + part + LANES]
            value = qkv_ref[:, at + 2 * part:at + 2 * part + LANES]
            mixed = None
            for head in range(2):
                own = jnp.where(lanes == head, query, jnp.zeros_like(query))
                scores = dot(own, key, 1, 1) * scale + bias
                top = jnp.max(scores, axis=-1, keepdims=True)
                weight = jnp.exp(scores - top)
                total = jnp.sum(weight, axis=-1, keepdims=True)
                probs = (weight * (1.0 / total)).astype(BF16)
                number = (half * pairs + pair) * 2 + head
                lse = jnp.where(
                    lax.broadcasted_iota(jnp.int32, lse.shape, 1) == number,
                    top + jnp.log(total), lse,
                )
                part_out = dot(probs, value, 1, 0)
                mixed = part_out if head == 0 else jnp.where(lanes == 0, mixed, part_out)
            o_at = half * part + pair * LANES
            o_ref[:, o_at:o_at + LANES] = mixed.astype(BF16)
        attended = attended + dot(
            o_ref[:, half * part:(half + 1) * part],
            w_ref[:, half * 4 * part + 3 * part:(half + 1) * 4 * part], 1, 1,
        )
    lse_ref[...] = lse
    h_ref[...] = attended
    hn = norm_forward(attended, gains[1:2, :]).astype(BF16)
    out_ref[...] = dot(get("placing")[...], hn, 1, 0).astype(BF16)
    chances = expert_chances(hn, get("router")[...], experts)
    lane = lax.broadcasted_iota(jnp.int32, chances.shape, 1)
    gate_ref[...] = jnp.sum(
        jnp.where(lane == get("route")[...], chances, 0.0), axis=-1, keepdims=True
    )


def backward_kernel(get, outs, *, spread):
    (da_ref, dqkv_ref, dattn_ref, small_ref) = outs[:4]
    hn_grad = dot(get("taking")[...], get("back")[...], 1, 0)
    gains = get("gains")
    dz = get("dz")[...].astype(F32)
    hidden = get("h")[...]
    count, width = hidden.shape
    part = width // 2
    pairs = part // LANES
    hidden_part, gain_f_grad = norm_back(hn_grad, hidden, gains[1:2, :])
    hidden_grad = dz + hidden_part
    attended_grad = hidden_grad.astype(BF16)
    dattn_ref[...] = attended_grad
    bias = attention_bias(get("seg_col")[...], get("seg_row")[...], count)
    lanes = head_lanes(count)
    scale = 1.0 / math.sqrt(HD)
    qkv_ref, lse_ref, w_ref = (get("qkv"), get("lse"), get("weights"))
    normed_grad = jnp.zeros((count, width), F32)
    for half in range(2):
        base = half * 3 * part
        mixed_grad = dot(
            attended_grad, w_ref[:, half * 4 * part + 3 * part:(half + 1) * 4 * part], 1, 0
        ).astype(BF16)
        for pair in range(pairs):
            at = base + pair * LANES
            query = qkv_ref[:, at:at + LANES]
            key = qkv_ref[:, at + part:at + part + LANES]
            value = qkv_ref[:, at + 2 * part:at + 2 * part + LANES]
            grad = mixed_grad[:, pair * LANES:(pair + 1) * LANES]
            dq = dk = dv = None
            for head in range(2):
                number = (half * pairs + pair) * 2 + head
                zero = jnp.zeros_like(query)
                own_q = jnp.where(lanes == head, query, zero)
                own_g = jnp.where(lanes == head, grad, zero)
                scores = dot(own_q, key, 1, 1) * scale + bias
                probs = jnp.exp(scores - lse_ref[:, number:number + 1])
                prob_grad = dot(own_g, value, 1, 1)
                inner = jnp.sum(probs * prob_grad, axis=-1, keepdims=True)
                score_grad = (probs * (prob_grad - inner)).astype(BF16)
                head_dv = dot(probs.astype(BF16), own_g, 0, 0)
                head_dk = dot(score_grad, own_q, 0, 0)
                head_dq = dot(score_grad, key, 1, 0)
                if head == 0:
                    dq, dk, dv = (head_dq, head_dk, head_dv)
                else:
                    dq = jnp.where(lanes == 0, dq, head_dq)
                    dk = dk + head_dk
                    dv = dv + head_dv
            dqkv_ref[:, at:at + LANES] = (dq * scale).astype(BF16)
            dqkv_ref[:, at + part:at + part + LANES] = (dk * scale).astype(BF16)
            dqkv_ref[:, at + 2 * part:at + 2 * part + LANES] = dv.astype(BF16)
        normed_grad = normed_grad + dot(
            dqkv_ref[:, base:base + 3 * part],
            w_ref[:, half * 4 * part:half * 4 * part + 3 * part], 1, 1,
        )
    input_part, gain_a_grad = norm_back(normed_grad, get("a")[...].astype(F32), gains[0:1, :])
    small_ref[0:1, :] = gain_a_grad
    small_ref[1:2, :] = gain_f_grad
    input_grad = (hidden_grad + input_part).astype(BF16)
    da_ref[...] = input_grad
    if spread:
        outs[4][...] = dot(get("placing")[...], input_grad, 1, 0).astype(BF16)


def staged_call(kernel, inputs, outs, flops):
    names = list(inputs)
    args = [inputs[name] for name in names]
    count = len(args)

    def body(*refs):
        sources, targets = (refs[:count], refs[count:count + len(outs)])
        held, marks = (refs[count + len(outs):-1], refs[-1])
        copies = [
            pltpu.make_async_copy(sources[i], held[i], marks.at[i]) for i in range(count)
        ]
        for copy in copies:
            copy.start()
        ready = set()

        def get(name):
            number = names.index(name)
            if number not in ready:
                ready.add(number)
                copies[number].wait()
            return held[number]

        kernel(get, targets)

    moved = sum(math.prod(v.shape) * v.dtype.itemsize for v in (*args, *outs))
    return pl.pallas_call(
        body,
        out_shape=outs,
        in_specs=[pl.BlockSpec(memory_space=pl.ANY)] * count,
        out_specs=[pl.BlockSpec(memory_space=pltpu.VMEM)] * len(outs),
        scratch_shapes=[pltpu.VMEM(v.shape, v.dtype) for v in args]
        + [pltpu.SemaphoreType.DMA((count,))],
        compiler_params=pltpu.CompilerParams(vmem_limit_bytes=40 * 1024 * 1024),
        cost_estimate=pl.CostEstimate(flops=flops, bytes_accessed=moved, transcendentals=0),
    )(*args)


def layer_start(source, params, segments, route_col, placing):
    gains, weights, router_w, experts = params
    joined = "back" in source
    struct = jax.ShapeDtypeStruct
    count = route_col.shape[0]
    width = weights.shape[0]
    outs = [
        struct((count, width), BF16),
        struct((count, 3 * width), BF16),
        struct((count, LANES), F32),
        struct((count, width), BF16),
        struct((count, width), F32),
        struct((count, 1), F32),
        struct((placing.shape[0], width), BF16),
    ]
    if joined:
        outs.append(struct((count, width), BF16))
    inputs = dict(
        source, gains=gains, seg_col=segments[0], seg_row=segments[1], weights=weights,
        placing=placing, router=router_w, route=route_col,
    )
    return staged_call(
        functools.partial(forward_kernel, experts=experts, joined=joined), inputs, outs, 3 * 10**9
    )


def layer_end(back, taking, upstream, inputs, state, params, segments, placing):
    gains, weights = params[:2]
    count, width = inputs.shape
    struct = jax.ShapeDtypeStruct
    outs = [
        struct((count, width), BF16),
        struct((count, 3 * width), BF16),
        struct((count, width), BF16),
        struct((2, width), F32),
    ]
    given = dict(
        taking=taking, back=back, gains=gains, dz=upstream, h=state["h"], seg_col=segments[0],
        seg_row=segments[1], weights=weights, qkv=state["qkv"], lse=state["lse"], a=inputs,
    )
    if placing is not None:
        given["placing"] = placing
        outs.append(struct((placing.shape[0], width), BF16))
    return staged_call(
        functools.partial(backward_kernel, spread=placing is not None), given, outs, 5 * 10**9
    )


def split_dot(left, right, left_dim, right_dim):
    high = left.astype(BF16)
    low = (left - high.astype(F32)).astype(BF16)
    return dot(high, right, left_dim, right_dim) + dot(low, right, left_dim, right_dim)


def expert_kernel(
    rows_ref, dz_ref, in_ref, out_ref, router_ref, hot_ref,
    dx_ref, act_ref, dpre_ref, dy_ref, g_router_ref, chance_ref, gate_ref, total_ref, *, experts,
):
    step = pl.program_id(0)
    rows = rows_ref[...]

    @pl.when(step == 0)
    def _():
        chances = expert_chances(rows, router_ref[...], experts)
        chance_ref[...] = chances
        gate = jnp.sum(chances * hot_ref[...], axis=-1, keepdims=True)
        dy_ref[...] = (gate * dz_ref[...].astype(F32)).astype(BF16)
        gate_ref[...] = jnp.zeros_like(gate_ref)
        total_ref[...] = jnp.zeros_like(total_ref)

    before = dot(rows, in_ref[...], 1, 0)
    square = before * before
    bent = jnp.tanh(SLOPE * before * (1.0 + CUBIC * square))
    lifted = 0.5 * (1.0 + bent)
    act = (before * lifted).astype(BF16)
    slope = lifted + 0.5 * before * (1.0 - bent * bent) * (
        SLOPE * (1.0 + 3.0 * CUBIC * square)
    )
    act_grad = dot(dy_ref[...], out_ref[...], 1, 1)
    dpre = (act_grad * slope).astype(BF16)
    act_ref[...] = act
    dpre_ref[...] = dpre
    gate_ref[...] += jnp.sum(act_grad * act.astype(F32), axis=-1, keepdims=True)
    total_ref[...] += dot(dpre, in_ref[...], 1, 1)

    @pl.when(step == pl.num_programs(0) - 1)
    def _():
        logit_grad = (hot_ref[...] - chance_ref[...]) * gate_ref[...]
        g_router_ref[...] = split_dot(logit_grad, rows, 0, 0)
        dx_ref[...] = (total_ref[...] + split_dot(logit_grad, router_ref[...], 1, 0)).astype(
            dx_ref.dtype
        )


def expert_back(rows, dz, in_w, expert_w, router_w, hot_row, experts, kind):
    count, width = rows.shape
    hidden = in_w.shape[1]
    block = 512
    struct = jax.ShapeDtypeStruct
    whole = pl.BlockSpec((count, width), lambda j: (0, 0))
    wide = pl.BlockSpec((count, block), lambda j: (0, j))
    router_spec = pl.BlockSpec((LANES, width), lambda j: (0, 0))
    return pl.pallas_call(
        functools.partial(expert_kernel, experts=experts),
        grid=(hidden // block,),
        out_shape=[
            struct((count, width), kind),
            struct((count, hidden), BF16),
            struct((count, hidden), BF16),
            struct((count, width), BF16),
            struct((LANES, width), F32),
        ],
        in_specs=[
            whole,
            whole,
            pl.BlockSpec((width, block), lambda j: (0, j)),
            pl.BlockSpec((block, width), lambda j: (j, 0)),
            router_spec,
            pl.BlockSpec((1, LANES), lambda j: (0, 0)),
        ],
        out_specs=[whole, wide, wide, whole, router_spec],
        scratch_shapes=[
            pltpu.VMEM((count, LANES), F32),
            pltpu.VMEM((count, 1), F32),
            pltpu.VMEM((count, width), F32),
        ],
        compiler_params=pltpu.CompilerParams(
            dimension_semantics=("arbitrary",), vmem_limit_bytes=40 * 1024 * 1024
        ),
        cost_estimate=pl.CostEstimate(
            flops=6 * count * width * hidden, bytes_accessed=12 * 10**6, transcendentals=0
        ),
    )(rows, dz, in_w, expert_w, router_w, hot_row)


def exchange_across(grad, section):
    width = grad.shape[0]
    count = lax.axis_size("dp")
    halves = grad.reshape(count, 2, width // count // 2, -1)
    keep = lax.dynamic_index_in_dim(halves, section, 1, keepdims=False)
    send = lax.dynamic_index_in_dim(halves, 1 - section, 1, keepdims=False)
    return (keep + swap(send.astype(BF16), "section").astype(F32)).astype(BF16)


def pair_up(values, tensor):
    half = values.shape[0] // 2
    halves = values.reshape(2, half, -1)
    own = entry(halves, tensor)
    other = swap(entry(halves, 1 - tensor), "tensor")
    return ordered(tensor, own[None], other[None])


def by_section(pairs, section):
    first, second = pairs
    own = jnp.where(section == 0, first, second)
    other = swap(jnp.where(section == 0, second, first), "section")
    return ordered(section, own, other)


def gelu_pair(before, active_grad):
    activated, back = jax.vjp(smooth_gate, before)
    return (activated.astype(BF16), back(active_grad)[0].astype(BF16))


def shards(
    x_in, d_out, lengths, routes, gain_attn, w_qkv, w_attn_out, gain_ffn, w_router, w_in, w_exp_out
):
    section = lax.axis_index("section")
    tensor = lax.axis_index("tensor")
    count = lax.axis_size("dp")
    width = x_in.shape[2]
    part = width // 2
    rows = 2 * x_in.shape[1]
    experts = w_router.shape[2]
    own_batch = 2 * section + tensor
    peer_batch = 2 * section + 1 - tensor

    def of_layer(layer, own, other):
        return jnp.where(section == layer, own, other)

    def by_layer(own):
        other = swap(own, "section")
        return [of_layer(layer, own, other) for layer in range(2)]

    def whole_group(array):
        return ordered(
            tensor, entry(array, own_batch), swap(entry(array, peer_batch), "tensor")
        )

    packed = jnp.concatenate([w_qkv[0], w_attn_out[0].T[None]], axis=0)
    packed = jnp.moveaxis(packed, 0, 1).reshape(width // count, -1)
    small = by_layer(jnp.concatenate([gain_attn, gain_ffn, w_router[0].T], axis=0))
    own_route = entry(routes[0, :, :, 0], own_batch)
    other_route = swap(entry(routes[0, :, :, 0], 2 * (1 - section) + tensor), "section")
    route = [of_layer(layer, own_route, other_route) for layer in range(2)]
    first_pack = of_layer(0, packed, one_way(packed, "section", 0, 1))
    first_beside = swap(first_pack, "tensor")
    first_w = lax.all_gather(
        jnp.concatenate([first_pack, first_beside], axis=1), "dp", axis=0, tiled=True
    )
    x_own = whole_group(x_in)
    own_in, own_out, later_pack, d_last = after(
        (w_in[0, 0], w_exp_out[0, 0], packed, d_out), first_beside
    )
    second_pack = of_layer(1, packed, one_way(later_pack, "section", 1, 0))
    second_pack = jnp.concatenate([second_pack, swap(second_pack, "tensor")], axis=1)
    dz_last = whole_group(d_last)
    in_w = by_layer(own_in)
    expert_w = by_layer(own_out)

    tables = [routing(row, experts) for row in route]
    placing = [table[0] for table in tables]
    taking = [table[1] for table in tables]
    route_col = [row[:, None] for row in route]
    gains = [small[layer][:2].astype(F32) for layer in range(2)]
    router_w = [jnp.pad(small[layer][2:], ((0, LANES - experts), (0, 0))) for layer in range(2)]
    bounds = jnp.cumsum(entry(lengths[:, 0], own_batch))
    places = jnp.arange(rows, dtype=jnp.int32)
    segment = jnp.sum((places[:, None] >= bounds[None, :]).astype(jnp.int32), axis=1)
    segments = (segment[:, None], segment[None, :])
    hot_row = (
        jnp.arange(LANES, dtype=jnp.int32)[None, :] == lax.axis_index("dp")
    ).astype(F32)
    keys = ("xn", "qkv", "lse", "o", "h", "gate")

    def expert_forward(values, layer):
        active = smooth_gate(dot(values, in_w[layer], 1, 0)).astype(BF16)
        return dot(active, expert_w[layer], 1, 0)

    def fold(own, peer):
        return (own + swap(peer.astype(BF16), "tensor").astype(F32)).astype(BF16)

    params0 = (gains[0], first_w, router_w[0], experts)
    *state0, outgoing0 = layer_start(
        {"a": x_own}, params0, segments, route_col[0], placing[0]
    )
    state0 = dict(zip(keys, state0))
    mine0 = all_to_all(outgoing0)
    side_xn0 = swap(state0["xn"], "tensor")
    side_o0 = swap(state0["o"][:, part:], "tensor")
    peer0 = swap(after(mine0, side_xn0, side_o0), "tensor")
    second_w = lax.all_gather(after(second_pack, mine0), "dp", axis=0, tiled=True)
    back0 = all_to_all(fold(expert_forward(mine0, 0), expert_forward(peer0, 0)))

    dz_out1 = dot(placing[1], dz_last, 1, 0).astype(BF16)
    mine_dz1 = all_to_all(after(dz_out1, back0))
    params1 = (gains[1], second_w, router_w[1], experts)
    *state1, outgoing1, out0 = layer_start(
        {"taking": taking[0], "back": back0, "h_before": state0["h"],
         "gate_before": state0["gate"]},
        params1, segments, route_col[1], placing[1],
    )
    state1 = dict(zip(keys, state1))
    side_xn1 = swap(state1["xn"], "tensor")
    side_o1 = swap(state1["o"][:, part:], "tensor")
    peer_dz1 = swap(after(mine_dz1, side_xn1, side_o1), "tensor")
    mine1 = all_to_all(after(outgoing1, mine_dz1))
    peer1 = swap(after(mine1, peer_dz1), "tensor")

    def both_back(layer, mine, peer, mine_dz, peer_dz):
        args = (in_w[layer], expert_w[layer], router_w[layer], hot_row, experts)
        return (
            expert_back(mine, mine_dz, *args, F32),
            expert_back(peer, peer_dz, *args, BF16),
        )

    own_b1, peer_b1 = both_back(1, mine1, peer1, mine_dz1, peer_dz1)
    peer_dx1 = swap(peer_b1[0], "tensor")
    dback1 = all_to_all((own_b1[0] + peer_dx1.astype(F32)).astype(BF16))
    late_mine1, late_peer1 = after((mine1, peer1), peer_b1[0])
    own_y1 = expert_forward(late_mine1, 1)
    peer_y1 = expert_forward(late_peer1, 1)
    total_y1 = fold(own_y1, after(peer_y1.astype(BF16), peer_dx1))
    grad1, dqkv1, dattn1, gains1, outgoing_dz0 = layer_end(
        dback1, taking[1], dz_last, out0, state1, params1, segments, placing[0]
    )

    mine_dz0 = all_to_all(outgoing_dz0)
    side_dqkv1 = swap(dqkv1[:, 3 * part:], "tensor")
    side_dattn1 = swap(dattn1, "tensor")
    peer_dz0 = swap(after(mine_dz0, side_dqkv1, side_dattn1), "tensor")

    def stack(first, second):
        return jnp.concatenate([first, second], axis=0)

    def attention_grad(xn, side_xn, dqkv, side_dqkv):
        return dot(stack(xn, side_xn), stack(dqkv[:, :3 * part], side_dqkv), 0, 0)

    def output_grad(dattn, side_dattn, mixed, side_mixed):
        return dot(stack(dattn, side_dattn), stack(mixed[:, :part], side_mixed), 0, 0)

    ready_xn1, ready_dattn1 = after((state1["xn"], dattn1), mine_dz0)
    full1 = jnp.concatenate(
        [
            attention_grad(ready_xn1, side_xn1, dqkv1, side_dqkv1),
            output_grad(ready_dattn1, side_dattn1, state1["o"], side_o1),
        ],
        axis=1,
    )
    peer_dz0 = after(peer_dz0, full1)
    own_b0, peer_b0 = both_back(0, mine0, peer0, mine_dz0, peer_dz0)
    half1 = exchange_across(full1, section)
    reduced1 = all_to_all(after(half1, peer_b0[0])).astype(F32).sum(axis=0)
    dback0 = all_to_all(fold(own_b0[0], peer_b0[0]))

    def pick(first, second):
        return jnp.where(section == 0, first, second)

    def gather_rows(number, index):
        return stack((own_b0, own_b1)[number][index], (peer_b0, peer_b1)[number][index])

    rows0, rows1 = (stack(mine0, peer0), stack(mine1, peer1))
    dy0, dy1 = (gather_rows(0, 3), gather_rows(1, 3))
    near_rows = pick(rows0, rows1)
    near_dy = pick(dy0, dy1)
    near_act = pick(gather_rows(0, 1), gather_rows(1, 1))
    near_dpre = pick(gather_rows(0, 2), gather_rows(1, 2))
    near_in = dot(near_rows, near_dpre, 0, 0)
    near_out = dot(near_act, near_dy, 0, 0)
    far_rows = pick(one_way(rows0, "section", 1, 0), one_way(rows1, "section", 0, 1))
    far_dy = pick(one_way(dy0, "section", 1, 0), one_way(dy1, "section", 0, 1))

    grad0, dqkv0, dattn0, gains0 = layer_end(
        after(dback0, near_in, near_out), taking[0], grad1, x_own, state0, params0, segments, None
    )

    side_dqkv0 = swap(dqkv0[:, 3 * part:], "tensor")
    side_dattn0 = swap(after(dattn0, side_dqkv0), "tensor")
    far_rows, far_dy = after((far_rows, far_dy), dqkv0)
    far_before = dot(far_rows, w_in[0, 0], 1, 0)
    far_act, far_dpre = gelu_pair(far_before, dot(far_dy, w_exp_out[0, 0], 1, 1))
    in_w_grad = near_in + dot(far_rows, far_dpre, 0, 0)
    expert_w_grad = near_out + dot(far_act, far_dy, 0, 0)
    qkv_half0 = exchange_across(
        attention_grad(state0["xn"], side_xn0, dqkv0, side_dqkv0), section
    )
    out_half0 = exchange_across(
        output_grad(dattn0, side_dattn0, state0["o"], side_o0), section
    )
    back1 = all_to_all(after(total_y1, dqkv0))
    out1 = (state1["h"] + state1["gate"] * dot(taking[1], back1, 1, 0)).astype(BF16)

    smalls = [
        jnp.concatenate([gain, (own[4] + peer[4])[:experts]], axis=0)
        for gain, own, peer in ((gains0, own_b0, peer_b0), (gains1, own_b1, peer_b1))
    ]
    own_small = pick(*smalls) + swap(pick(*reversed(smalls)), "section")
    own_small = own_small + swap(own_small, "tensor")
    copies = jnp.broadcast_to(own_small[None], (count,) + own_small.shape)
    own_small = jnp.sum(all_to_all(copies), axis=0)

    reduced0 = jnp.concatenate(
        [
            all_to_all(qkv_half0).astype(F32).sum(axis=0),
            all_to_all(out_half0).astype(F32).sum(axis=0),
        ],
        axis=1,
    )
    own_half = pick(reduced0, reduced1)
    other_half = swap(pick(reduced1, reduced0).astype(BF16), "section").astype(F32)
    joined = ordered(section, own_half, other_half)
    qkv_grad = jnp.stack([joined[:, part * kind:part * (kind + 1)] for kind in range(3)])
    out_grad = joined[:, 3 * part:].T
    section_out = by_section([pair_up(out0, tensor), pair_up(out1, tensor)], section)
    section_in_grad = by_section([pair_up(grad0, tensor), pair_up(grad1, tensor)], section)
    return (
        section_out[None],
        section_in_grad[None],
        own_small[0][None],
        qkv_grad[None],
        out_grad[None],
        own_small[1][None],
        own_small[2:].T[None],
        in_w_grad[None, None],
        expert_w_grad[None, None],
    )


def solution(mesh):
    in_specs = (
        P(None, ("dp", "tensor"), None),
        P(None, ("dp", "tensor"), None),
        P(None, "dp", None),
        P("section", None, "dp", None),
        P("section", None),
        P("section", None, "dp", "tensor"),
        P("section", "tensor", "dp"),
        P("section", None),
        P("section", None, None),
        P("section", "dp", None, "tensor"),
        P("section", "dp", "tensor", None),
    )
    out_specs = (
        P("section", None, ("dp", "tensor"), None),
        P("section", None, ("dp", "tensor"), None),
        P("section", None),
        P("section", None, "dp", "tensor"),
        P("section", "tensor", "dp"),
        P("section", None),
        P("section", None, None),
        P("section", "dp", None, "tensor"),
        P("section", "dp", "tensor", None),
    )
    return jax.shard_map(shards, mesh=mesh, in_specs=in_specs, out_specs=out_specs, check_vma=False)
```

```python
import functools
import math

import jax
import jax.numpy as jnp
from jax import lax
from jax.experimental import pallas as pl
from jax.experimental.pallas import tpu as pltpu
from jax.sharding import PartitionSpec as P

HD = 64
LANES = 128
EPSILON = 1e-06
NEGATIVE = -1e30
F32 = jnp.float32
BF16 = jnp.bfloat16
CUBIC = 0.044715
VMEM_LIMIT = 56 * 1024 * 1024
SLOPE = math.sqrt(2.0 / math.pi)


def swap(values, axis):
    return lax.ppermute(values, axis, [(0, 1), (1, 0)])


def one_way(values, axis, source, target):
    return lax.ppermute(values, axis, [(source, target)])


def all_to_all(values):
    return lax.all_to_all(values, "dp", split_axis=0, concat_axis=0, tiled=True)


def after(value, *anchors):
    return lax.optimization_barrier((value, anchors))[0]


def dot(left, right, left_dim, right_dim):
    return lax.dot_general(
        left, right, (((left_dim,), (right_dim,)), ((), ())), preferred_element_type=F32
    )


def ordered(index, own, other):
    return jnp.where(
        index == 0, jnp.concatenate([own, other], axis=0), jnp.concatenate([other, own], axis=0)
    )


def entry(array, index):
    return lax.dynamic_index_in_dim(array, index, 0, keepdims=False)


def norm_forward(inputs, gain):
    scaling = lax.rsqrt(jnp.mean(inputs * inputs, axis=-1, keepdims=True) + EPSILON)
    return inputs * scaling * gain


def norm_back(upstream, inputs, gain):
    scaling = lax.rsqrt(jnp.mean(inputs * inputs, axis=-1, keepdims=True) + EPSILON)
    weighted = upstream * gain
    scaled = inputs * scaling
    inner = jnp.mean(weighted * inputs, axis=-1, keepdims=True)
    return (
        scaling * weighted - scaled * (scaling * scaling * inner),
        jnp.sum(upstream * scaled, axis=0, keepdims=True),
    )


def smooth_gate(values):
    return jax.nn.gelu(values, approximate=True)


def routing(route_row, experts):
    count = route_row.shape[0]
    capacity = 2 * count // experts
    hot = route_row[:, None] == jnp.arange(experts, dtype=jnp.int32)[None, :]
    places = jnp.arange(count, dtype=jnp.int32)
    earlier = (places[:, None] > places[None, :]).astype(BF16)
    ranks = dot(earlier, hot.astype(BF16), 1, 0)
    ranking = jnp.sum(ranks * hot.astype(F32), axis=1).astype(jnp.int32)
    slots = route_row * capacity + ranking
    places = jnp.arange(experts * capacity, dtype=jnp.int32)
    return (
        (slots[None, :] == places[:, None]).astype(BF16),
        (slots[:, None] == places[None, :]).astype(BF16),
    )


def head_lanes(count):
    return lax.broadcasted_iota(jnp.int32, (count, LANES), 1) // HD


def attention_bias(seg_col, seg_row, count):
    rows = lax.broadcasted_iota(jnp.int32, (count, count), 0)
    cols = lax.broadcasted_iota(jnp.int32, (count, count), 1)
    return jnp.where((seg_col == seg_row) & (rows >= cols), 0.0, NEGATIVE)


def expert_chances(rows, router, experts):
    logits = dot(rows, router, 1, 1)
    lane = lax.broadcasted_iota(jnp.int32, logits.shape, 1)
    logits = jnp.where(lane < experts, logits, NEGATIVE)
    raised = jnp.exp(logits - jnp.max(logits, axis=-1, keepdims=True))
    return raised * (1.0 / jnp.sum(raised, axis=-1, keepdims=True))


def forward_kernel(get, outs, send, *, experts, joined):
    (xn_ref, qkv_ref, lse_ref, *o_refs) = outs[:5]
    (h_ref, gate_ref, out_ref) = outs[5:8]
    if joined:
        mixed_in = dot(get("taking")[...], get("back")[...], 1, 0)
        result = (get("h_before")[...] + get("gate_before")[...] * mixed_in).astype(BF16)
        outs[8][...] = result
        send(8)
        a = result.astype(F32)
    else:
        a = get("a")[...].astype(F32)
    count, width = a.shape
    part = width // 2
    pairs = part // LANES
    gains = get("gains")
    xn = norm_forward(a, gains[0:1, :]).astype(BF16)
    xn_ref[...] = xn
    send(0)
    bias = attention_bias(get("seg_col")[...], get("seg_row")[...], count)
    lanes = head_lanes(count)
    scale = 1.0 / math.sqrt(HD)
    w_ref = get("weights")
    for half in range(2):
        base = half * 3 * part
        qkv_ref[:, base:base + 3 * part] = dot(
            xn, w_ref[:, half * 4 * part:half * 4 * part + 3 * part], 1, 0
        ).astype(BF16)
    send(1)
    attended = a
    lse = jnp.zeros((count, LANES), F32)
    for half in range(2):
        base = half * 3 * part
        for pair in range(pairs):
            at = base + pair * LANES
            query = qkv_ref[:, at:at + LANES]
            key = qkv_ref[:, at + part:at + part + LANES]
            value = qkv_ref[:, at + 2 * part:at + 2 * part + LANES]
            mixed = None
            for head in range(2):
                own = jnp.where(lanes == head, query, jnp.zeros_like(query))
                scores = dot(own, key, 1, 1) * scale + bias
                top = jnp.max(scores, axis=-1, keepdims=True)
                weight = jnp.exp(scores - top)
                total = jnp.sum(weight, axis=-1, keepdims=True)
                probs = (weight * (1.0 / total)).astype(BF16)
                number = (half * pairs + pair) * 2 + head
                lse = jnp.where(
                    lax.broadcasted_iota(jnp.int32, lse.shape, 1) == number,
                    top + jnp.log(total), lse,
                )
                part_out = dot(probs, value, 1, 0)
                mixed = part_out if head == 0 else jnp.where(lanes == 0, mixed, part_out)
            o_refs[half][:, pair * LANES:(pair + 1) * LANES] = mixed.astype(BF16)
        send(3 + half)
        attended = attended + dot(
            o_refs[half][...],
            w_ref[:, half * 4 * part + 3 * part:(half + 1) * 4 * part], 1, 1,
        )
    lse_ref[...] = lse
    send(2)
    h_ref[...] = attended
    send(5)
    hn = norm_forward(attended, gains[1:2, :]).astype(BF16)
    out_ref[...] = dot(get("placing")[...], hn, 1, 0).astype(BF16)
    send(7)
    chances = expert_chances(hn, get("router")[...], experts)
    lane = lax.broadcasted_iota(jnp.int32, chances.shape, 1)
    gate_ref[...] = jnp.sum(
        jnp.where(lane == get("route")[...], chances, 0.0), axis=-1, keepdims=True
    )
    send(6)


def hidden_kernel(get, outs, send):
    (dattn_ref, dh_ref, small_ref) = outs
    hn_grad = dot(get("taking")[...], get("back")[...], 1, 0)
    gains = get("gains")
    dz = get("dz")[...].astype(F32)
    hidden_part, small_ref[...] = norm_back(hn_grad, get("h")[...], gains[1:2, :])
    hidden_grad = dz + hidden_part
    dattn_ref[...] = hidden_grad.astype(BF16)
    send(0)
    dh_ref[...] = hidden_grad
    send(1)
    send(2)


def backward_kernel(get, outs, send, *, spread):
    (da_ref, *dqkv_refs, small_ref) = outs[:4]
    gains = get("gains")
    attended_grad = get("dattn")[...]
    count, width = attended_grad.shape
    part = width // 2
    pairs = part // LANES
    bias = attention_bias(get("seg_col")[...], get("seg_row")[...], count)
    lanes = head_lanes(count)
    scale = 1.0 / math.sqrt(HD)
    w_ref, qkv_ref, lse_ref = (get("weights"), get("qkv"), get("lse"))
    normed_grad = jnp.zeros((count, width), F32)
    for half in range(2):
        base = half * 3 * part
        mixed_grad = dot(
            attended_grad, w_ref[:, half * 4 * part + 3 * part:(half + 1) * 4 * part], 1, 0
        ).astype(BF16)
        for pair in range(pairs):
            at = base + pair * LANES
            query = qkv_ref[:, at:at + LANES]
            key = qkv_ref[:, at + part:at + part + LANES]
            value = qkv_ref[:, at + 2 * part:at + 2 * part + LANES]
            grad = mixed_grad[:, pair * LANES:(pair + 1) * LANES]
            dq = dk = dv = None
            for head in range(2):
                number = (half * pairs + pair) * 2 + head
                zero = jnp.zeros_like(query)
                own_q = jnp.where(lanes == head, query, zero)
                own_g = jnp.where(lanes == head, grad, zero)
                scores = dot(own_q, key, 1, 1) * scale + bias
                probs = jnp.exp(scores - lse_ref[:, number:number + 1])
                prob_grad = dot(own_g, value, 1, 1)
                inner = jnp.sum(probs * prob_grad, axis=-1, keepdims=True)
                score_grad = (probs * (prob_grad - inner)).astype(BF16)
                head_dv = dot(probs.astype(BF16), own_g, 0, 0)
                head_dk = dot(score_grad, own_q, 0, 0)
                head_dq = dot(score_grad, key, 1, 0)
                if head == 0:
                    dq, dk, dv = (head_dq, head_dk, head_dv)
                else:
                    dq = jnp.where(lanes == 0, dq, head_dq)
                    dk = dk + head_dk
                    dv = dv + head_dv
            at = pair * LANES
            dqkv_refs[half][:, at:at + LANES] = (dq * scale).astype(BF16)
            dqkv_refs[half][:, at + part:at + part + LANES] = (dk * scale).astype(BF16)
            dqkv_refs[half][:, at + 2 * part:at + 2 * part + LANES] = dv.astype(BF16)
        send(1 + half)
        normed_grad = normed_grad + dot(
            dqkv_refs[half][...],
            w_ref[:, half * 4 * part:half * 4 * part + 3 * part], 1, 1,
        )
    input_part, small_ref[...] = norm_back(
        normed_grad, get("a")[...].astype(F32), gains[0:1, :]
    )
    input_grad = (get("dh")[...] + input_part).astype(BF16)
    if spread:
        outs[4][...] = dot(get("placing")[...], input_grad, 1, 0).astype(BF16)
        send(4)
    da_ref[...] = input_grad
    send(0)
    send(3)


def staged_call(kernel, inputs, outs, flops):
    names = list(inputs)
    args = [inputs[name] for name in names]
    count = len(args)
    total = count + len(outs)

    def body(*refs):
        held, marks = (refs[total:-1], refs[-1])
        copies = [
            pltpu.make_async_copy(*pair, marks.at[number])
            for number, pair in enumerate(
                [(refs[i], held[i]) for i in range(count)]
                + [(held[i], refs[i]) for i in range(count, total)]
            )
        ]
        for copy in copies[:count]:
            copy.start()
        ready = set()

        def get(name):
            number = names.index(name)
            if number not in ready:
                ready.add(number)
                copies[number].wait()
            return held[number]

        kernel(get, held[count:], lambda number: copies[count + number].start())
        for copy in copies[count:]:
            copy.wait()

    moved = sum(math.prod(v.shape) * v.dtype.itemsize for v in (*args, *outs))
    return pl.pallas_call(
        body,
        out_shape=outs,
        in_specs=[pl.BlockSpec(memory_space=pltpu.HBM)] * count,
        out_specs=[pl.BlockSpec(memory_space=pltpu.HBM)] * len(outs),
        scratch_shapes=[pltpu.VMEM(v.shape, v.dtype) for v in (*args, *outs)]
        + [pltpu.SemaphoreType.DMA((total,))],
        compiler_params=pltpu.CompilerParams(vmem_limit_bytes=VMEM_LIMIT),
        cost_estimate=pl.CostEstimate(flops=flops, bytes_accessed=moved, transcendentals=0),
    )(*args)


def layer_start(source, params, segments, route_col, placing):
    gains, weights, router_w, experts = params
    joined = "back" in source
    struct = jax.ShapeDtypeStruct
    count = route_col.shape[0]
    width = weights.shape[0]
    outs = [
        struct((count, width), BF16),
        struct((count, 3 * width), BF16),
        struct((count, LANES), F32),
        struct((count, width // 2), BF16),
        struct((count, width // 2), BF16),
        struct((count, width), F32),
        struct((count, 1), F32),
        struct((placing.shape[0], width), BF16),
    ]
    if joined:
        outs.append(struct((count, width), BF16))
    inputs = dict(
        source, gains=gains, seg_col=segments[0], seg_row=segments[1], weights=weights,
        placing=placing, router=router_w, route=route_col,
    )
    return staged_call(
        functools.partial(forward_kernel, experts=experts, joined=joined), inputs, outs, 3 * 10**9
    )


def hidden_end(back, taking, upstream, state, params):
    count, width = upstream.shape
    struct = jax.ShapeDtypeStruct
    outs = [struct((count, width), BF16), struct((count, width), F32), struct((1, width), F32)]
    given = dict(taking=taking, back=back, gains=params[0], dz=upstream, h=state["h"])
    return staged_call(hidden_kernel, given, outs, 3 * 10**8)


def layer_end(dattn, hidden_grad, inputs, state, params, segments, placing):
    gains, weights = params[:2]
    count, width = inputs.shape
    struct = jax.ShapeDtypeStruct
    outs = [
        struct((count, width), BF16),
        struct((count, 3 * width // 2), BF16),
        struct((count, 3 * width // 2), BF16),
        struct((1, width), F32),
    ]
    given = dict(
        gains=gains, dattn=dattn, seg_col=segments[0], seg_row=segments[1], weights=weights,
        qkv=state["qkv"], lse=state["lse"], a=inputs, dh=hidden_grad,
    )
    if placing is not None:
        given["placing"] = placing
        outs.append(struct((placing.shape[0], width), BF16))
    return staged_call(
        functools.partial(backward_kernel, spread=placing is not None), given, outs, 5 * 10**9
    )


def split_dot(left, right, left_dim, right_dim):
    high = left.astype(BF16)
    low = (left - high.astype(F32)).astype(BF16)
    return dot(high, right, left_dim, right_dim) + dot(low, right, left_dim, right_dim)


def expert_kernel(
    rows_ref, dz_ref, in_ref, out_ref, router_ref, hot_ref,
    dx_ref, act_ref, dpre_ref, dy_ref, g_router_ref, chance_ref, gate_ref, total_ref, *, experts,
):
    step = pl.program_id(0)
    rows = rows_ref[...]

    @pl.when(step == 0)
    def _():
        chances = expert_chances(rows, router_ref[...], experts)
        chance_ref[...] = chances
        gate = jnp.sum(chances * hot_ref[...], axis=-1, keepdims=True)
        dy_ref[...] = (gate * dz_ref[...].astype(F32)).astype(BF16)
        gate_ref[...] = jnp.zeros_like(gate_ref)
        total_ref[...] = jnp.zeros_like(total_ref)

    before = dot(rows, in_ref[...], 1, 0)
    square = before * before
    bent = jnp.tanh(SLOPE * before * (1.0 + CUBIC * square))
    lifted = 0.5 * (1.0 + bent)
    act = (before * lifted).astype(BF16)
    slope = lifted + 0.5 * before * (1.0 - bent * bent) * (
        SLOPE * (1.0 + 3.0 * CUBIC * square)
    )
    act_grad = dot(dy_ref[...], out_ref[...], 1, 1)
    dpre = (act_grad * slope).astype(BF16)
    act_ref[...] = act
    dpre_ref[...] = dpre
    gate_ref[...] += jnp.sum(act_grad * act.astype(F32), axis=-1, keepdims=True)
    total_ref[...] += dot(dpre, in_ref[...], 1, 1)

    @pl.when(step == pl.num_programs(0) - 1)
    def _():
        logit_grad = (hot_ref[...] - chance_ref[...]) * gate_ref[...]
        g_router_ref[...] = split_dot(logit_grad, rows, 0, 0)
        dx_ref[...] = (total_ref[...] + split_dot(logit_grad, router_ref[...], 1, 0)).astype(
            dx_ref.dtype
        )


def expert_back(rows, dz, in_w, expert_w, layer, router_w, hot_row, experts, kind):
    count, width = rows.shape
    hidden = in_w.shape[1]
    block = 512
    struct = jax.ShapeDtypeStruct
    whole = pl.BlockSpec((count, width), lambda j: (0, 0))
    wide = pl.BlockSpec((count, block), lambda j: (0, j))
    router_spec = pl.BlockSpec((LANES, width), lambda j: (0, 0))
    return pl.pallas_call(
        functools.partial(expert_kernel, experts=experts),
        grid=(hidden // block,),
        out_shape=[
            struct((count, width), kind),
            struct((count, hidden), BF16),
            struct((count, hidden), BF16),
            struct((count, width), BF16),
            struct((LANES, width), F32),
        ],
        in_specs=[
            whole,
            whole,
            pl.BlockSpec((width, block), lambda j: (0, j)),
            pl.BlockSpec((None, block, width), lambda j: (layer, j, 0)),
            router_spec,
            pl.BlockSpec((1, LANES), lambda j: (0, 0)),
        ],
        out_specs=[whole, wide, wide, whole, router_spec],
        scratch_shapes=[
            pltpu.VMEM((count, LANES), F32),
            pltpu.VMEM((count, 1), F32),
            pltpu.VMEM((count, width), F32),
        ],
        compiler_params=pltpu.CompilerParams(
            dimension_semantics=("arbitrary",), vmem_limit_bytes=VMEM_LIMIT
        ),
        cost_estimate=pl.CostEstimate(
            flops=6 * count * width * hidden, bytes_accessed=12 * 10**6, transcendentals=0
        ),
    )(rows, dz, in_w, expert_w, router_w, hot_row)


def across_parts(grad, section):
    width = grad.shape[0]
    count = lax.axis_size("dp")
    halves = grad.reshape(count, 2, width // count // 2, -1)
    keep = lax.dynamic_index_in_dim(halves, section, 1, keepdims=False)
    send = lax.dynamic_index_in_dim(halves, 1 - section, 1, keepdims=False)
    return (keep, send.astype(BF16))


def across_sum(keep, send):
    return (keep + swap(send, "section").astype(F32)).astype(BF16)


def exchange_across(grad, section):
    return across_sum(*across_parts(grad, section))


def pair_up(values, tensor):
    half = values.shape[0] // 2
    halves = values.reshape(2, half, -1)
    own = entry(halves, tensor)
    other = swap(entry(halves, 1 - tensor), "tensor")
    return ordered(tensor, own[None], other[None])


def by_section(pairs, fars, section):
    own = jnp.where(section == 0, pairs[0], pairs[1])
    return ordered(section, own, jnp.where(section == 0, fars[0], fars[1]))


def gelu_pair(before, active_grad):
    activated, back = jax.vjp(smooth_gate, before)
    return (activated.astype(BF16), back(active_grad)[0].astype(BF16))


def shards(
    x_in, d_out, lengths, routes, gain_attn, w_qkv, w_attn_out, gain_ffn, w_router, w_in, w_exp_out
):
    section = lax.axis_index("section")
    tensor = lax.axis_index("tensor")
    count = lax.axis_size("dp")
    width = x_in.shape[2]
    part = width // 2
    rows = 2 * x_in.shape[1]
    experts = w_router.shape[2]
    own_batch = 2 * section + tensor
    peer_batch = 2 * section + 1 - tensor

    def of_layer(layer, own, other):
        return jnp.where(section == layer, own, other)

    def by_layer(own):
        other = swap(own, "section")
        return [of_layer(layer, own, other) for layer in range(2)]

    def whole_group(array):
        return ordered(
            tensor, entry(array, own_batch), swap(entry(array, peer_batch), "tensor")
        )

    packed = jnp.concatenate([w_qkv[0], w_attn_out[0].T[None]], axis=0)
    packed = jnp.moveaxis(packed, 0, 1).reshape(width // count, -1)
    small = by_layer(jnp.concatenate([gain_attn, gain_ffn, w_router[0].T], axis=0))
    own_route = entry(routes[0, :, :, 0], own_batch)
    other_route = swap(entry(routes[0, :, :, 0], 2 * (1 - section) + tensor), "section")
    route = [of_layer(layer, own_route, other_route) for layer in range(2)]
    first_pack = of_layer(0, packed, one_way(packed, "section", 0, 1))
    first_beside = swap(first_pack, "tensor")
    first_w = lax.all_gather(
        jnp.concatenate([first_pack, first_beside], axis=1), "dp", axis=0, tiled=True
    )
    x_own = whole_group(x_in)
    later_pack, d_last = after((packed, d_out), first_beside)
    second_pack = of_layer(1, packed, one_way(later_pack, "section", 1, 0))
    second_pack = jnp.concatenate([second_pack, swap(second_pack, "tensor")], axis=1)
    dz_last = whole_group(d_last)
    far_in = swap(w_in[0, 0], "section")
    in_w = [of_layer(layer, w_in[0, 0], far_in) for layer in range(2)]
    both_out = lax.all_gather(after(w_exp_out[0, 0], x_own), "section", axis=0)
    expert_w = [both_out[0], both_out[1]]

    tables = [routing(row, experts) for row in route]
    placing = [table[0] for table in tables]
    taking = [table[1] for table in tables]
    route_col = [row[:, None] for row in route]
    gains = [small[layer][:2].astype(F32) for layer in range(2)]
    router_w = [jnp.pad(small[layer][2:], ((0, LANES - experts), (0, 0))) for layer in range(2)]
    bounds = jnp.cumsum(entry(lengths[:, 0], own_batch))
    places = jnp.arange(rows, dtype=jnp.int32)
    segment = jnp.sum((places[:, None] >= bounds[None, :]).astype(jnp.int32), axis=1)
    segments = (segment[:, None], segment[None, :])
    hot_row = (
        jnp.arange(LANES, dtype=jnp.int32)[None, :] == lax.axis_index("dp")
    ).astype(F32)
    keys = ("xn", "qkv", "lse", "o", "o_far", "h", "gate")

    def expert_forward(values, layer):
        active = smooth_gate(dot(values, in_w[layer], 1, 0)).astype(BF16)
        return dot(active, expert_w[layer], 1, 0)

    def fold(own, peer):
        own = lax.optimization_barrier(own)
        return (own + swap(peer.astype(BF16), "tensor").astype(F32)).astype(BF16)

    params0 = (gains[0], first_w, router_w[0], experts)
    *state0, outgoing0 = layer_start(
        {"a": after(x_own, far_in)}, params0, segments, route_col[0], placing[0]
    )
    state0 = dict(zip(keys, state0))
    mine0 = all_to_all(outgoing0)
    side_xn0 = swap(state0["xn"], "tensor")
    side_o0 = swap(state0["o_far"], "tensor")
    peer0 = swap(
        after(mine0, side_xn0, side_o0, in_w), "tensor"
    )
    second_w = lax.all_gather(after(second_pack, mine0, both_out), "dp", axis=0, tiled=True)
    back0 = all_to_all(fold(expert_forward(mine0, 0), expert_forward(peer0, 0)))

    far_mine0 = one_way(after(mine0, peer0), "section", 1, 0)
    far_peer0 = one_way(after(peer0, back0), "section", 1, 0)
    dz_out1 = dot(placing[1], dz_last, 1, 0).astype(BF16)
    mine_dz1 = all_to_all(after(dz_out1, back0))
    params1 = (gains[1], second_w, router_w[1], experts)
    *state1, outgoing1, out0 = layer_start(
        {"taking": taking[0], "back": after(back0, far_mine0), "h_before": state0["h"],
         "gate_before": state0["gate"]},
        params1, segments, route_col[1], placing[1],
    )
    state1 = dict(zip(keys, state1))
    peer_dz1 = swap(mine_dz1, "tensor")
    pair_out0 = pair_up(out0, tensor)
    mine1 = all_to_all(after(outgoing1, mine_dz1, pair_out0, far_peer0))
    peer1 = swap(after(mine1, peer_dz1), "tensor")

    def both_back(layer, mine, peer, mine_dz, peer_dz):
        args = (in_w[layer], both_out, layer, router_w[layer], hot_row, experts)
        own = expert_back(mine, mine_dz, *args, F32)
        peer, peer_dz = after((peer, peer_dz), own[0])
        return (own, expert_back(peer, peer_dz, *args, BF16))

    own_b1, peer_b1 = both_back(1, mine1, peer1, mine_dz1, peer_dz1)
    peer_dx1 = swap(peer_b1[0], "tensor")
    far_mine1 = one_way(mine1, "section", 0, 1)
    far_peer1 = one_way(after(peer1, own_b1[0]), "section", 0, 1)
    far_dys1 = [
        one_way(after(part_b1[3], peer_b1[0]), "section", 0, 1) for part_b1 in (own_b1, peer_b1)
    ]
    far_out0 = one_way(pair_out0, "section", 1, 0)
    far_peer0 = one_way(after(peer0, own_b1[0]), "section", 1, 0)
    dback1 = all_to_all(
        after((own_b1[0] + peer_dx1.astype(F32)).astype(BF16), far_mine1)
    )
    late_mine1, late_peer1 = after((mine1, peer1), peer_b1[0])
    peer_y1 = expert_forward(late_peer1, 1).astype(BF16)
    own_y1 = expert_forward(late_mine1, 1)
    side_y1 = swap(after(peer_y1, peer_dx1), "tensor")
    total_y1 = (own_y1 + side_y1.astype(F32)).astype(BF16)
    side_xn1, side_o1 = [
        swap(half, "tensor")
        for half in after((state1["xn"], state1["o_far"]), peer_dx1)
    ]
    dattn1, dh1, gain_f1 = hidden_end(
        after(dback1, own_y1, peer_y1, side_xn1, side_o1, far_out0, far_peer1), taking[1], dz_last, state1, params1
    )
    side_dattn1 = swap(dattn1, "tensor")
    grad1, dqkv1, dqkv_far1, gain_a1, outgoing_dz0 = layer_end(
        dattn1, dh1, out0, state1, params1, segments, placing[0]
    )

    mine_dz0 = all_to_all(after(outgoing_dz0, side_dattn1))
    side_dqkv1 = swap(dqkv_far1, "tensor")
    def stack(first, second):
        return jnp.concatenate([first, second], axis=0)

    def attention_grad(xn, side_xn, dqkv, side_dqkv):
        return dot(stack(xn, side_xn), stack(dqkv, side_dqkv), 0, 0)

    def output_grad(dattn, side_dattn, mixed, side_mixed):
        return dot(stack(dattn, side_dattn), stack(mixed, side_mixed), 0, 0)

    full1 = jnp.concatenate(
        [
            attention_grad(state1["xn"], side_xn1, dqkv1, side_dqkv1),
            output_grad(dattn1, side_dattn1, state1["o"], side_o1),
        ],
        axis=1,
    )
    keep1, send1 = across_parts(full1, section)
    peer_dz0 = swap(after(mine_dz0, send1, side_y1), "tensor")
    own_b0, peer_b0 = both_back(0, mine0, peer0, mine_dz0, peer_dz0)
    back1 = all_to_all(after(total_y1, own_b0[0]))
    peer_dx0 = swap(peer_b0[0], "tensor")
    pair_grad1 = pair_up(after(grad1, peer_dx0), tensor)
    far_grad1 = one_way(pair_grad1, "section", 0, 1)

    def pick(first, second, index=section):
        return jnp.where(index == 0, first, second)

    def gather_rows(number, index):
        return stack((own_b0, own_b1)[number][index], (peer_b0, peer_b1)[number][index])

    late_mine0, late_mine1, own_b1, peer_b1 = after((mine0, mine1, own_b1, peer_b1), peer_b0[0])
    near_rows = pick(stack(late_mine0, peer0), stack(late_mine1, peer1))
    near_dpre = pick(gather_rows(0, 2), gather_rows(1, 2))
    near_in = dot(near_rows, near_dpre, 0, 0)
    far_dys0 = [
        one_way(after(part_b0[3], peer_b0[0]), "section", 1, 0) for part_b0 in (own_b0, peer_b0)
    ]
    total_dx0 = after(
        (own_b0[0] + peer_dx0.astype(F32)).astype(BF16), near_in, back1
    )
    dback0 = all_to_all(total_dx0)
    dy0, dy1 = (gather_rows(0, 3), gather_rows(1, 3))
    late = after(section, total_dx0)
    near_dy = pick(dy0, dy1)
    late_back1 = after(back1, total_dx0)
    out1 = (state1["h"] + state1["gate"] * dot(taking[1], late_back1, 1, 0)).astype(BF16)
    pair_out1 = pair_up(out1, tensor)
    far_out1 = one_way(pair_out1, "section", 0, 1)
    near_act = pick(gather_rows(0, 1), gather_rows(1, 1), late)
    near_out = dot(near_act, near_dy, 0, 0)
    dattn0, dh0, gain_f0 = hidden_end(
        after(dback0, near_out, pair_out1), taking[0], grad1, state0, params0
    )
    side_dattn0 = swap(dattn0, "tensor")
    grad0, dqkv0, dqkv_far0, gain_a0 = layer_end(
        dattn0, dh0, x_own, state0, params0, segments, None
    )

    side_dqkv0 = swap(dqkv_far0, "tensor")
    smalls = jnp.stack(
        [
            jnp.concatenate([*gain, (own[4] + peer[4])[:experts]], axis=0)
            for gain, own, peer in (
                ((gain_a0, gain_f0), own_b0, peer_b0), ((gain_a1, gain_f1), own_b1, peer_b1)
            )
        ]
    )
    smalls = all_to_all(jnp.broadcast_to(smalls[None], (count,) + smalls.shape)).sum(axis=0)
    late_dattn0, late_side, late_keep1 = after((dattn0, side_dattn0, keep1), dqkv0)
    reduced1 = all_to_all(after(across_sum(late_keep1, send1), smalls))
    out_keep, out_send = across_parts(
        output_grad(late_dattn0, late_side, state0["o"], side_o0), section
    )
    late = after(section, dqkv0)
    far_rows = stack(pick(far_mine0, far_mine1, late), pick(far_peer0, far_peer1, late))
    far_dy = stack(pick(far_dys0[0], far_dys1[0], late), pick(far_dys0[1], far_dys1[1], late))
    far_before = dot(far_rows, w_in[0, 0], 1, 0)
    ready_xn0 = after(state0["xn"], out_send, far_before)
    qkv_keep, qkv_send = across_parts(
        attention_grad(ready_xn0, side_xn0, dqkv0, side_dqkv0), section
    )
    far_act, far_dpre = gelu_pair(
        far_before, dot(after(far_dy, qkv_send), w_exp_out[0, 0], 1, 1)
    )
    half0 = jnp.concatenate(
        [
            across_sum(after(qkv_keep, far_act, far_dpre), qkv_send),
            across_sum(out_keep, out_send),
        ],
        axis=2,
    )
    reduced0 = all_to_all(half0)
    grad0, far_act, far_dpre, reduced1 = after((grad0, far_act, far_dpre, reduced1), half0)
    pair_grad0 = pair_up(grad0, tensor)
    far_grad0 = one_way(pair_grad0, "section", 1, 0)
    in_w_grad = near_in + dot(far_rows, far_dpre, 0, 0)
    expert_w_grad = near_out + dot(far_act, far_dy, 0, 0)

    smalls = after(smalls, qkv_send)
    smalls = smalls + swap(smalls, "tensor")
    own_small = pick(smalls[0], smalls[1]) + swap(pick(smalls[1], smalls[0]), "section")

    reduced1 = reduced1.astype(F32).sum(axis=0)
    reduced0 = after(reduced0, in_w_grad, expert_w_grad, far_grad0, far_out1, own_small)
    reduced0 = reduced0.astype(F32).sum(axis=0)
    own_half = pick(reduced0, reduced1)
    other_half = swap(pick(reduced1, reduced0).astype(BF16), "section").astype(F32)
    joined = ordered(section, own_half, other_half)
    qkv_grad = jnp.stack([joined[:, part * kind:part * (kind + 1)] for kind in range(3)])
    out_grad = joined[:, 3 * part:].T
    section_out = by_section([pair_out0, pair_out1], [far_out0, far_out1], section)
    section_in_grad = by_section([pair_grad0, pair_grad1], [far_grad0, far_grad1], section)
    return (
        section_out[None],
        section_in_grad[None],
        own_small[0][None],
        qkv_grad[None],
        out_grad[None],
        own_small[1][None],
        own_small[2:].T[None],
        in_w_grad[None, None],
        expert_w_grad[None, None],
    )


def solution(mesh):
    in_specs = (
        P(None, ("dp", "tensor"), None),
        P(None, ("dp", "tensor"), None),
        P(None, "dp", None),
        P("section", None, "dp", None),
        P("section", None),
        P("section", None, "dp", "tensor"),
        P("section", "tensor", "dp"),
        P("section", None),
        P("section", None, None),
        P("section", "dp", None, "tensor"),
        P("section", "dp", "tensor", None),
    )
    out_specs = (
        P("section", None, ("dp", "tensor"), None),
        P("section", None, ("dp", "tensor"), None),
        P("section", None),
        P("section", None, "dp", "tensor"),
        P("section", "tensor", "dp"),
        P("section", None),
        P("section", None, None),
        P("section", "dp", None, "tensor"),
        P("section", "dp", "tensor", None),
    )
    return jax.shard_map(shards, mesh=mesh, in_specs=in_specs, out_specs=out_specs, check_vma=False)
```

```python
import functools
import math

import jax
import jax.numpy as jnp
from jax import lax
from jax.experimental import pallas as pl
from jax.experimental.pallas import tpu as pltpu
from jax.sharding import PartitionSpec as P

HD = 64
LANES = 128
EPSILON = 1e-06
NEGATIVE = -1e30
F32 = jnp.float32
BF16 = jnp.bfloat16
CUBIC = 0.044715
VMEM_LIMIT = 56 * 1024 * 1024
SLOPE = math.sqrt(2.0 / math.pi)


def swap(values, axis):
    return lax.ppermute(values, axis, [(0, 1), (1, 0)])


def one_way(values, axis, source, target):
    return lax.ppermute(values, axis, [(source, target)])


def all_to_all(values):
    return lax.all_to_all(values, "dp", split_axis=0, concat_axis=0, tiled=True)


def after(value, *anchors):
    return lax.optimization_barrier((value, anchors))[0]


def dot(left, right, left_dim, right_dim):
    return lax.dot_general(
        left, right, (((left_dim,), (right_dim,)), ((), ())), preferred_element_type=F32
    )


def ordered(index, own, other):
    return jnp.where(
        index == 0, jnp.concatenate([own, other], axis=0), jnp.concatenate([other, own], axis=0)
    )


def entry(array, index):
    return lax.dynamic_index_in_dim(array, index, 0, keepdims=False)


def norm_forward(inputs, gain):
    scaling = lax.rsqrt(jnp.mean(inputs * inputs, axis=-1, keepdims=True) + EPSILON)
    return inputs * scaling * gain


def norm_back(upstream, inputs, gain):
    scaling = lax.rsqrt(jnp.mean(inputs * inputs, axis=-1, keepdims=True) + EPSILON)
    weighted = upstream * gain
    scaled = inputs * scaling
    inner = jnp.mean(weighted * inputs, axis=-1, keepdims=True)
    return (
        scaling * weighted - scaled * (scaling * scaling * inner),
        jnp.sum(upstream * scaled, axis=0, keepdims=True),
    )


def smooth_gate(values):
    return jax.nn.gelu(values, approximate=True)


def routing(route_row, experts):
    count = route_row.shape[0]
    capacity = 2 * count // experts
    hot = route_row[:, None] == jnp.arange(experts, dtype=jnp.int32)[None, :]
    places = jnp.arange(count, dtype=jnp.int32)
    earlier = (places[:, None] > places[None, :]).astype(BF16)
    ranks = dot(earlier, hot.astype(BF16), 1, 0)
    ranking = jnp.sum(ranks * hot.astype(F32), axis=1).astype(jnp.int32)
    slots = route_row * capacity + ranking
    places = jnp.arange(experts * capacity, dtype=jnp.int32)
    return (
        (slots[None, :] == places[:, None]).astype(BF16),
        (slots[:, None] == places[None, :]).astype(BF16),
    )


def head_lanes(count):
    return lax.broadcasted_iota(jnp.int32, (count, LANES), 1) // HD


def attention_bias(seg_col, seg_row, count):
    rows = lax.broadcasted_iota(jnp.int32, (count, count), 0)
    cols = lax.broadcasted_iota(jnp.int32, (count, count), 1)
    return jnp.where((seg_col == seg_row) & (rows >= cols), 0.0, NEGATIVE)


def expert_chances(rows, router, experts):
    logits = dot(rows, router, 1, 1)
    lane = lax.broadcasted_iota(jnp.int32, logits.shape, 1)
    logits = jnp.where(lane < experts, logits, NEGATIVE)
    raised = jnp.exp(logits - jnp.max(logits, axis=-1, keepdims=True))
    return raised * (1.0 / jnp.sum(raised, axis=-1, keepdims=True))


def forward_kernel(get, outs, send, *, experts, joined):
    (xn_ref, qkv_ref, lse_ref, *o_refs) = outs[:5]
    (h_ref, gate_ref, out_ref) = outs[5:8]
    if joined:
        mixed_in = dot(get("taking")[...], get("back")[...], 1, 0)
        result = (get("h_before")[...] + get("gate_before")[...] * mixed_in).astype(BF16)
        outs[8][...] = result
        send(8)
        a = result.astype(F32)
    else:
        a = get("a")[...].astype(F32)
    count, width = a.shape
    part = width // 2
    pairs = part // LANES
    gains = get("gains")
    xn = norm_forward(a, gains[0:1, :]).astype(BF16)
    xn_ref[...] = xn
    send(0)
    bias = attention_bias(get("seg_col")[...], get("seg_row")[...], count)
    lanes = head_lanes(count)
    scale = 1.0 / math.sqrt(HD)
    w_ref = get("weights")
    for half in range(2):
        base = half * 3 * part
        qkv_ref[:, base:base + 3 * part] = dot(
            xn, w_ref[:, half * 4 * part:half * 4 * part + 3 * part], 1, 0
        ).astype(BF16)
    send(1)
    attended = a
    lse = jnp.zeros((count, LANES), F32)
    for half in range(2):
        base = half * 3 * part
        for pair in range(pairs):
            at = base + pair * LANES
            query = qkv_ref[:, at:at + LANES]
            key = qkv_ref[:, at + part:at + part + LANES]
            value = qkv_ref[:, at + 2 * part:at + 2 * part + LANES]
            mixed = None
            for head in range(2):
                own = jnp.where(lanes == head, query, jnp.zeros_like(query))
                scores = dot(own, key, 1, 1) * scale + bias
                top = jnp.max(scores, axis=-1, keepdims=True)
                weight = jnp.exp(scores - top)
                total = jnp.sum(weight, axis=-1, keepdims=True)
                probs = (weight * (1.0 / total)).astype(BF16)
                number = (half * pairs + pair) * 2 + head
                lse = jnp.where(
                    lax.broadcasted_iota(jnp.int32, lse.shape, 1) == number,
                    top + jnp.log(total), lse,
                )
                part_out = dot(probs, value, 1, 0)
                mixed = part_out if head == 0 else jnp.where(lanes == 0, mixed, part_out)
            o_refs[half][:, pair * LANES:(pair + 1) * LANES] = mixed.astype(BF16)
        send(3 + half)
        attended = attended + dot(
            o_refs[half][...],
            w_ref[:, half * 4 * part + 3 * part:(half + 1) * 4 * part], 1, 1,
        )
    lse_ref[...] = lse
    send(2)
    h_ref[...] = attended
    send(5)
    hn = norm_forward(attended, gains[1:2, :]).astype(BF16)
    out_ref[...] = dot(get("placing")[...], hn, 1, 0).astype(BF16)
    send(7)
    chances = expert_chances(hn, get("router")[...], experts)
    lane = lax.broadcasted_iota(jnp.int32, chances.shape, 1)
    gate_ref[...] = jnp.sum(
        jnp.where(lane == get("route")[...], chances, 0.0), axis=-1, keepdims=True
    )
    send(6)


def hidden_kernel(get, outs, send):
    (dattn_ref, dh_ref, small_ref) = outs
    hn_grad = dot(get("taking")[...], get("back")[...], 1, 0)
    gains = get("gains")
    dz = get("dz")[...].astype(F32)
    hidden_part, small_ref[...] = norm_back(hn_grad, get("h")[...], gains[1:2, :])
    hidden_grad = dz + hidden_part
    dattn_ref[...] = hidden_grad.astype(BF16)
    send(0)
    dh_ref[...] = hidden_grad
    send(1)
    send(2)


def backward_kernel(get, outs, send, *, spread):
    (da_ref, *dqkv_refs, small_ref) = outs[:4]
    gains = get("gains")
    attended_grad = get("dattn")[...]
    count, width = attended_grad.shape
    part = width // 2
    pairs = part // LANES
    bias = attention_bias(get("seg_col")[...], get("seg_row")[...], count)
    lanes = head_lanes(count)
    scale = 1.0 / math.sqrt(HD)
    w_ref, qkv_ref, lse_ref = (get("weights"), get("qkv"), get("lse"))
    normed_grad = jnp.zeros((count, width), F32)
    for half in range(2):
        base = half * 3 * part
        mixed_grad = dot(
            attended_grad, w_ref[:, half * 4 * part + 3 * part:(half + 1) * 4 * part], 1, 0
        ).astype(BF16)
        for pair in range(pairs):
            at = base + pair * LANES
            query = qkv_ref[:, at:at + LANES]
            key = qkv_ref[:, at + part:at + part + LANES]
            value = qkv_ref[:, at + 2 * part:at + 2 * part + LANES]
            grad = mixed_grad[:, pair * LANES:(pair + 1) * LANES]
            dq = dk = dv = None
            for head in range(2):
                number = (half * pairs + pair) * 2 + head
                zero = jnp.zeros_like(query)
                own_q = jnp.where(lanes == head, query, zero)
                own_g = jnp.where(lanes == head, grad, zero)
                scores = dot(own_q, key, 1, 1) * scale + bias
                probs = jnp.exp(scores - lse_ref[:, number:number + 1])
                prob_grad = dot(own_g, value, 1, 1)
                inner = jnp.sum(probs * prob_grad, axis=-1, keepdims=True)
                score_grad = (probs * (prob_grad - inner)).astype(BF16)
                head_dv = dot(probs.astype(BF16), own_g, 0, 0)
                head_dk = dot(score_grad, own_q, 0, 0)
                head_dq = dot(score_grad, key, 1, 0)
                if head == 0:
                    dq, dk, dv = (head_dq, head_dk, head_dv)
                else:
                    dq = jnp.where(lanes == 0, dq, head_dq)
                    dk = dk + head_dk
                    dv = dv + head_dv
            at = pair * LANES
            dqkv_refs[half][:, at:at + LANES] = (dq * scale).astype(BF16)
            dqkv_refs[half][:, at + part:at + part + LANES] = (dk * scale).astype(BF16)
            dqkv_refs[half][:, at + 2 * part:at + 2 * part + LANES] = dv.astype(BF16)
        send(1 + half)
        normed_grad = normed_grad + dot(
            dqkv_refs[half][...],
            w_ref[:, half * 4 * part:half * 4 * part + 3 * part], 1, 1,
        )
    input_part, small_ref[...] = norm_back(
        normed_grad, get("a")[...].astype(F32), gains[0:1, :]
    )
    input_grad = (get("dh")[...] + input_part).astype(BF16)
    if spread:
        outs[4][...] = dot(get("placing")[...], input_grad, 1, 0).astype(BF16)
        send(4)
    da_ref[...] = input_grad
    send(0)
    send(3)


def staged_call(kernel, inputs, outs, flops):
    names = list(inputs)
    args = [inputs[name] for name in names]
    count = len(args)
    total = count + len(outs)

    def body(*refs):
        held, marks = (refs[total:-1], refs[-1])
        copies = [
            pltpu.make_async_copy(*pair, marks.at[number])
            for number, pair in enumerate(
                [(refs[i], held[i]) for i in range(count)]
                + [(held[i], refs[i]) for i in range(count, total)]
            )
        ]
        for copy in copies[:count]:
            copy.start()
        ready = set()

        def get(name):
            number = names.index(name)
            if number not in ready:
                ready.add(number)
                copies[number].wait()
            return held[number]

        kernel(get, held[count:], lambda number: copies[count + number].start())
        for copy in copies[count:]:
            copy.wait()

    moved = sum(math.prod(v.shape) * v.dtype.itemsize for v in (*args, *outs))
    return pl.pallas_call(
        body,
        out_shape=outs,
        in_specs=[pl.BlockSpec(memory_space=pltpu.HBM)] * count,
        out_specs=[pl.BlockSpec(memory_space=pltpu.HBM)] * len(outs),
        scratch_shapes=[pltpu.VMEM(v.shape, v.dtype) for v in (*args, *outs)]
        + [pltpu.SemaphoreType.DMA((total,))],
        compiler_params=pltpu.CompilerParams(vmem_limit_bytes=VMEM_LIMIT),
        cost_estimate=pl.CostEstimate(flops=flops, bytes_accessed=moved, transcendentals=0),
    )(*args)


def layer_start(source, params, segments, route_col, placing):
    gains, weights, router_w, experts = params
    joined = "back" in source
    struct = jax.ShapeDtypeStruct
    count = route_col.shape[0]
    width = weights.shape[0]
    outs = [
        struct((count, width), BF16),
        struct((count, 3 * width), BF16),
        struct((count, LANES), F32),
        struct((count, width // 2), BF16),
        struct((count, width // 2), BF16),
        struct((count, width), F32),
        struct((count, 1), F32),
        struct((placing.shape[0], width), BF16),
    ]
    if joined:
        outs.append(struct((count, width), BF16))
    inputs = dict(
        source, gains=gains, seg_col=segments[0], seg_row=segments[1], weights=weights,
        placing=placing, router=router_w, route=route_col,
    )
    return staged_call(
        functools.partial(forward_kernel, experts=experts, joined=joined), inputs, outs, 3 * 10**9
    )


def hidden_end(back, taking, upstream, state, params):
    count, width = upstream.shape
    struct = jax.ShapeDtypeStruct
    outs = [struct((count, width), BF16), struct((count, width), F32), struct((1, width), F32)]
    given = dict(taking=taking, back=back, gains=params[0], dz=upstream, h=state["h"])
    return staged_call(hidden_kernel, given, outs, 3 * 10**8)


def layer_end(dattn, hidden_grad, inputs, state, params, segments, placing):
    gains, weights = params[:2]
    count, width = inputs.shape
    struct = jax.ShapeDtypeStruct
    outs = [
        struct((count, width), BF16),
        struct((count, 3 * width // 2), BF16),
        struct((count, 3 * width // 2), BF16),
        struct((1, width), F32),
    ]
    given = dict(
        gains=gains, dattn=dattn, seg_col=segments[0], seg_row=segments[1], weights=weights,
        qkv=state["qkv"], lse=state["lse"], a=inputs, dh=hidden_grad,
    )
    if placing is not None:
        given["placing"] = placing
        outs.append(struct((placing.shape[0], width), BF16))
    return staged_call(
        functools.partial(backward_kernel, spread=placing is not None), given, outs, 5 * 10**9
    )


def split_dot(left, right, left_dim, right_dim):
    high = left.astype(BF16)
    low = (left - high.astype(F32)).astype(BF16)
    return dot(high, right, left_dim, right_dim) + dot(low, right, left_dim, right_dim)


def expert_kernel(
    rows_ref, dz_ref, in_ref, out_ref, router_ref, hot_ref,
    dx_ref, act_ref, dpre_ref, dy_ref, g_router_ref, chance_ref, gate_ref, total_ref, *, experts,
):
    step = pl.program_id(0)
    rows = rows_ref[...]

    @pl.when(step == 0)
    def _():
        chances = expert_chances(rows, router_ref[...], experts)
        chance_ref[...] = chances
        gate = jnp.sum(chances * hot_ref[...], axis=-1, keepdims=True)
        dy_ref[...] = (gate * dz_ref[...].astype(F32)).astype(BF16)
        gate_ref[...] = jnp.zeros_like(gate_ref)
        total_ref[...] = jnp.zeros_like(total_ref)

    before = dot(rows, in_ref[...], 1, 0)
    square = before * before
    bent = jnp.tanh(SLOPE * before * (1.0 + CUBIC * square))
    lifted = 0.5 * (1.0 + bent)
    act = (before * lifted).astype(BF16)
    slope = lifted + 0.5 * before * (1.0 - bent * bent) * (
        SLOPE * (1.0 + 3.0 * CUBIC * square)
    )
    act_grad = dot(dy_ref[...], out_ref[...], 1, 1)
    dpre = (act_grad * slope).astype(BF16)
    act_ref[...] = act
    dpre_ref[...] = dpre
    gate_ref[...] += jnp.sum(act_grad * act.astype(F32), axis=-1, keepdims=True)
    total_ref[...] += dot(dpre, in_ref[...], 1, 1)

    @pl.when(step == pl.num_programs(0) - 1)
    def _():
        logit_grad = (hot_ref[...] - chance_ref[...]) * gate_ref[...]
        g_router_ref[...] = split_dot(logit_grad, rows, 0, 0)
        dx_ref[...] = (total_ref[...] + split_dot(logit_grad, router_ref[...], 1, 0)).astype(
            dx_ref.dtype
        )


def expert_back(rows, dz, in_w, expert_w, layer, router_w, hot_row, experts, kind):
    count, width = rows.shape
    hidden = in_w.shape[1]
    block = 512
    struct = jax.ShapeDtypeStruct
    whole = pl.BlockSpec((count, width), lambda j: (0, 0))
    wide = pl.BlockSpec((count, block), lambda j: (0, j))
    router_spec = pl.BlockSpec((LANES, width), lambda j: (0, 0))
    return pl.pallas_call(
        functools.partial(expert_kernel, experts=experts),
        grid=(hidden // block,),
        out_shape=[
            struct((count, width), kind),
            struct((count, hidden), BF16),
            struct((count, hidden), BF16),
            struct((count, width), BF16),
            struct((LANES, width), F32),
        ],
        in_specs=[
            whole,
            whole,
            pl.BlockSpec((width, block), lambda j: (0, j)),
            pl.BlockSpec((None, block, width), lambda j: (layer, j, 0)),
            router_spec,
            pl.BlockSpec((1, LANES), lambda j: (0, 0)),
        ],
        out_specs=[whole, wide, wide, whole, router_spec],
        scratch_shapes=[
            pltpu.VMEM((count, LANES), F32),
            pltpu.VMEM((count, 1), F32),
            pltpu.VMEM((count, width), F32),
        ],
        compiler_params=pltpu.CompilerParams(
            dimension_semantics=("arbitrary",), vmem_limit_bytes=VMEM_LIMIT
        ),
        cost_estimate=pl.CostEstimate(
            flops=6 * count * width * hidden, bytes_accessed=12 * 10**6, transcendentals=0
        ),
    )(rows, dz, in_w, expert_w, router_w, hot_row)


def across_parts(grad, section):
    width = grad.shape[0]
    count = lax.axis_size("dp")
    halves = grad.reshape(count, 2, width // count // 2, -1)
    keep = lax.dynamic_index_in_dim(halves, section, 1, keepdims=False)
    send = lax.dynamic_index_in_dim(halves, 1 - section, 1, keepdims=False)
    return (keep, send.astype(BF16))


def across_sum(keep, send):
    return (keep + swap(send, "section").astype(F32)).astype(BF16)


def exchange_across(grad, section):
    return across_sum(*across_parts(grad, section))


def pair_up(values, tensor):
    half = values.shape[0] // 2
    halves = values.reshape(2, half, -1)
    own = entry(halves, tensor)
    other = swap(entry(halves, 1 - tensor), "tensor")
    return ordered(tensor, own[None], other[None])


def by_section(pairs, fars, section):
    own = jnp.where(section == 0, pairs[0], pairs[1])
    return ordered(section, own, jnp.where(section == 0, fars[0], fars[1]))


def gelu_pair(before, active_grad):
    activated, back = jax.vjp(smooth_gate, before)
    return (activated.astype(BF16), back(active_grad)[0].astype(BF16))


def shards(
    x_in, d_out, lengths, routes, gain_attn, w_qkv, w_attn_out, gain_ffn, w_router, w_in, w_exp_out
):
    section = lax.axis_index("section")
    tensor = lax.axis_index("tensor")
    count = lax.axis_size("dp")
    width = x_in.shape[2]
    part = width // 2
    rows = 2 * x_in.shape[1]
    experts = w_router.shape[2]
    own_batch = 2 * section + tensor
    peer_batch = 2 * section + 1 - tensor

    def of_layer(layer, own, other):
        return jnp.where(section == layer, own, other)

    def by_layer(own):
        other = swap(own, "section")
        return [of_layer(layer, own, other) for layer in range(2)]

    def whole_group(array):
        return ordered(
            tensor, entry(array, own_batch), swap(entry(array, peer_batch), "tensor")
        )

    packed = jnp.concatenate([w_qkv[0], w_attn_out[0].T[None]], axis=0)
    packed = jnp.moveaxis(packed, 0, 1).reshape(width // count, -1)
    small = by_layer(jnp.concatenate([gain_attn, gain_ffn, w_router[0].T], axis=0))
    own_route = entry(routes[0, :, :, 0], own_batch)
    other_route = swap(entry(routes[0, :, :, 0], 2 * (1 - section) + tensor), "section")
    route = [of_layer(layer, own_route, other_route) for layer in range(2)]
    first_pack = of_layer(0, packed, one_way(packed, "section", 0, 1))
    first_beside = swap(first_pack, "tensor")
    first_packs = jnp.concatenate([first_pack, first_beside], axis=1)
    first_w = lax.all_gather(first_packs, "dp", axis=0, tiled=True)
    x_own = whole_group(x_in)
    later_pack, d_last = after((packed, d_out), first_beside)
    second_pack = of_layer(1, packed, one_way(later_pack, "section", 1, 0))
    second_pack = jnp.concatenate([second_pack, swap(second_pack, "tensor")], axis=1)
    dz_last = whole_group(d_last)
    far_in = swap(w_in[0, 0], "section")
    in_w = [of_layer(layer, w_in[0, 0], far_in) for layer in range(2)]
    both_out = lax.all_gather(after(w_exp_out[0, 0], first_packs), "section", axis=0)
    expert_w = [both_out[0], both_out[1]]

    tables = [routing(row, experts) for row in route]
    placing = [table[0] for table in tables]
    taking = [table[1] for table in tables]
    route_col = [row[:, None] for row in route]
    gains = [small[layer][:2].astype(F32) for layer in range(2)]
    router_w = [jnp.pad(small[layer][2:], ((0, LANES - experts), (0, 0))) for layer in range(2)]
    bounds = jnp.cumsum(entry(lengths[:, 0], own_batch))
    places = jnp.arange(rows, dtype=jnp.int32)
    segment = jnp.sum((places[:, None] >= bounds[None, :]).astype(jnp.int32), axis=1)
    segments = (segment[:, None], segment[None, :])
    hot_row = (
        jnp.arange(LANES, dtype=jnp.int32)[None, :] == lax.axis_index("dp")
    ).astype(F32)
    keys = ("xn", "qkv", "lse", "o", "o_far", "h", "gate")

    def expert_forward(values, layer):
        active = smooth_gate(dot(values, in_w[layer], 1, 0)).astype(BF16)
        return dot(active, expert_w[layer], 1, 0)

    def fold(own, peer):
        own = lax.optimization_barrier(own)
        return (own + swap(peer.astype(BF16), "tensor").astype(F32)).astype(BF16)

    params0 = (gains[0], first_w, router_w[0], experts)
    *state0, outgoing0 = layer_start(
        {"a": after(x_own, far_in)}, params0, segments, route_col[0], placing[0]
    )
    state0 = dict(zip(keys, state0))
    mine0 = all_to_all(outgoing0)
    side_xn0 = swap(state0["xn"], "tensor")
    side_o0 = swap(state0["o_far"], "tensor")
    peer0 = swap(
        after(mine0, side_xn0, side_o0, in_w), "tensor"
    )
    second_w = lax.all_gather(after(second_pack, mine0), "dp", axis=0, tiled=True)
    back0 = all_to_all(fold(expert_forward(mine0, 0), expert_forward(peer0, 0)))

    far_mine0 = one_way(after(mine0, peer0), "section", 1, 0)
    far_peer0 = one_way(after(peer0, back0), "section", 1, 0)
    dz_out1 = dot(placing[1], dz_last, 1, 0).astype(BF16)
    mine_dz1 = all_to_all(after(dz_out1, back0))
    params1 = (gains[1], second_w, router_w[1], experts)
    *state1, outgoing1, out0 = layer_start(
        {"taking": taking[0], "back": after(back0, far_mine0), "h_before": state0["h"],
         "gate_before": state0["gate"]},
        params1, segments, route_col[1], placing[1],
    )
    state1 = dict(zip(keys, state1))
    peer_dz1 = swap(mine_dz1, "tensor")
    pair_out0 = pair_up(out0, tensor)
    mine1 = all_to_all(after(outgoing1, mine_dz1, pair_out0, far_peer0))
    peer1 = swap(after(mine1, peer_dz1), "tensor")

    def both_back(layer, mine, peer, mine_dz, peer_dz):
        args = (in_w[layer], both_out, layer, router_w[layer], hot_row, experts)
        own = expert_back(mine, mine_dz, *args, F32)
        peer, peer_dz = after((peer, peer_dz), own[0])
        return (own, expert_back(peer, peer_dz, *args, BF16))

    own_b1, peer_b1 = both_back(1, mine1, peer1, mine_dz1, peer_dz1)
    peer_dx1 = swap(peer_b1[0], "tensor")
    far_mine1 = one_way(mine1, "section", 0, 1)
    far_peer1 = one_way(after(peer1, own_b1[0]), "section", 0, 1)
    far_out0 = one_way(pair_out0, "section", 1, 0)
    far_peer0 = one_way(after(peer0, own_b1[0]), "section", 1, 0)
    dback1 = all_to_all(
        after((own_b1[0] + peer_dx1.astype(F32)).astype(BF16), far_mine1)
    )
    late_mine1, late_peer1 = after((mine1, peer1), peer_b1[0])
    peer_y1 = expert_forward(late_peer1, 1).astype(BF16)
    own_y1 = expert_forward(late_mine1, 1)
    side_y1 = swap(after(peer_y1, peer_dx1), "tensor")
    total_y1 = (own_y1 + side_y1.astype(F32)).astype(BF16)
    side_xn1, side_o1 = [
        swap(half, "tensor")
        for half in after((state1["xn"], state1["o_far"]), peer_dx1)
    ]
    dattn1, dh1, gain_f1 = hidden_end(
        after(dback1, own_y1, peer_y1, side_xn1, side_o1, far_out0, far_peer1), taking[1], dz_last, state1, params1
    )
    side_dattn1 = swap(dattn1, "tensor")
    grad1, dqkv1, dqkv_far1, gain_a1, outgoing_dz0 = layer_end(
        dattn1, dh1, out0, state1, params1, segments, placing[0]
    )

    mine_dz0 = all_to_all(outgoing_dz0)
    side_dqkv1 = swap(dqkv_far1, "tensor")
    def stack(first, second):
        return jnp.concatenate([first, second], axis=0)

    def attention_grad(xn, side_xn, dqkv, side_dqkv):
        return dot(stack(xn, side_xn), stack(dqkv, side_dqkv), 0, 0)

    def output_grad(dattn, side_dattn, mixed, side_mixed):
        return dot(stack(dattn, side_dattn), stack(mixed, side_mixed), 0, 0)

    full1 = jnp.concatenate(
        [
            attention_grad(state1["xn"], side_xn1, dqkv1, side_dqkv1),
            output_grad(dattn1, side_dattn1, state1["o"], side_o1),
        ],
        axis=1,
    )
    keep1, send1 = across_parts(full1, section)
    peer_dz0 = swap(after(mine_dz0, send1, side_y1), "tensor")
    across1 = swap(send1, "section")
    back1 = all_to_all(after(total_y1, mine_dz0))
    peer_dz0 = after(peer_dz0, across1, back1)
    own_b0, peer_b0 = both_back(0, mine0, peer0, mine_dz0, peer_dz0)
    keep1, across1 = after((keep1, across1), own_b0[0])
    reduced1 = all_to_all((keep1 + across1.astype(F32)).astype(BF16))
    peer_dx0 = swap(peer_b0[0], "tensor")
    pair_grad1 = pair_up(after(grad1, peer_dx0), tensor)
    far_grad1 = one_way(pair_grad1, "section", 0, 1)

    def pick(first, second, index=section):
        return jnp.where(index == 0, first, second)

    def gather_rows(number, index):
        return stack((own_b0, own_b1)[number][index], (peer_b0, peer_b1)[number][index])

    late_mine0, late_mine1, own_b1, peer_b1 = after((mine0, mine1, own_b1, peer_b1), peer_b0[0])
    near_rows = pick(stack(late_mine0, peer0), stack(late_mine1, peer1))
    near_dpre = pick(gather_rows(0, 2), gather_rows(1, 2))
    near_in = dot(near_rows, near_dpre, 0, 0)
    far_dys1 = [
        one_way(after(part_b1[3], peer_b0[0]), "section", 0, 1) for part_b1 in (own_b1, peer_b1)
    ]
    far_dys0 = [
        one_way(after(part_b0[3], peer_b0[0]), "section", 1, 0) for part_b0 in (own_b0, peer_b0)
    ]
    total_dx0 = after(
        (own_b0[0] + peer_dx0.astype(F32)).astype(BF16), near_in, reduced1
    )
    dback0 = all_to_all(total_dx0)
    dy0, dy1 = (gather_rows(0, 3), gather_rows(1, 3))
    late = after(section, total_dx0)
    near_dy = pick(dy0, dy1)
    late_back1 = after(back1, total_dx0)
    out1 = (state1["h"] + state1["gate"] * dot(taking[1], late_back1, 1, 0)).astype(BF16)
    pair_out1 = pair_up(out1, tensor)
    far_out1 = one_way(pair_out1, "section", 0, 1)
    near_act = pick(gather_rows(0, 1), gather_rows(1, 1), late)
    near_out = dot(near_act, near_dy, 0, 0)
    dattn0, dh0, gain_f0 = hidden_end(
        after(dback0, near_out, pair_out1), taking[0], grad1, state0, params0
    )
    side_dattn0 = swap(dattn0, "tensor")
    grad0, dqkv0, dqkv_far0, gain_a0 = layer_end(
        dattn0, dh0, x_own, state0, params0, segments, None
    )

    side_dqkv0 = swap(dqkv_far0, "tensor")
    late_dattn0, late_side = after((dattn0, side_dattn0), dqkv0)
    out_keep, out_send = across_parts(
        output_grad(late_dattn0, late_side, state0["o"], side_o0), section
    )
    smalls = jnp.stack(
        [
            jnp.concatenate([*gain, (own[4] + peer[4])[:experts]], axis=0)
            for gain, own, peer in (
                ((gain_a0, gain_f0), own_b0, peer_b0), ((gain_a1, gain_f1), own_b1, peer_b1)
            )
        ]
    )
    smalls = after(smalls, out_send)
    smalls = all_to_all(jnp.broadcast_to(smalls[None], (count,) + smalls.shape))
    smalls = smalls.sum(axis=0)
    ready_xn0 = after(state0["xn"], out_send)
    qkv_keep, qkv_send = across_parts(
        attention_grad(ready_xn0, side_xn0, dqkv0, side_dqkv0), section
    )
    late = after(section, qkv_send)
    far_rows = stack(pick(far_mine0, far_mine1, late), pick(far_peer0, far_peer1, late))
    far_dy = stack(pick(far_dys0[0], far_dys1[0], late), pick(far_dys0[1], far_dys1[1], late))
    far_before = dot(far_rows, w_in[0, 0], 1, 0)
    half0 = jnp.concatenate(
        [
            across_sum(after(qkv_keep, far_before, far_dy), qkv_send),
            across_sum(out_keep, out_send),
        ],
        axis=2,
    )
    reduced0 = all_to_all(half0)
    pair_grad0 = pair_up(after(grad0, qkv_send), tensor)
    far_grad0 = one_way(after(pair_grad0, half0), "section", 1, 0)
    far_dy, reduced1 = after((far_dy, reduced1), half0)
    far_act, far_dpre = gelu_pair(far_before, dot(far_dy, w_exp_out[0, 0], 1, 1))
    in_w_grad = near_in + dot(far_rows, far_dpre, 0, 0)
    expert_w_grad = near_out + dot(far_act, far_dy, 0, 0)

    smalls = after(smalls, qkv_send)
    smalls = smalls + swap(smalls, "tensor")
    own_small = pick(smalls[0], smalls[1]) + swap(pick(smalls[1], smalls[0]), "section")

    reduced1 = reduced1.astype(F32).sum(axis=0)
    reduced0 = after(reduced0, in_w_grad, expert_w_grad, far_grad0, far_out1, own_small)
    reduced0 = reduced0.astype(F32).sum(axis=0)
    own_half = pick(reduced0, reduced1)
    other_half = swap(pick(reduced1, reduced0).astype(BF16), "section").astype(F32)
    joined = ordered(section, own_half, other_half)
    qkv_grad = jnp.stack([joined[:, part * kind:part * (kind + 1)] for kind in range(3)])
    out_grad = joined[:, 3 * part:].T
    section_out = by_section([pair_out0, pair_out1], [far_out0, far_out1], section)
    section_in_grad = by_section([pair_grad0, pair_grad1], [far_grad0, far_grad1], section)
    return (
        section_out[None],
        section_in_grad[None],
        own_small[0][None],
        qkv_grad[None],
        out_grad[None],
        own_small[1][None],
        own_small[2:].T[None],
        in_w_grad[None, None],
        expert_w_grad[None, None],
    )


def solution(mesh):
    in_specs = (
        P(None, ("dp", "tensor"), None),
        P(None, ("dp", "tensor"), None),
        P(None, "dp", None),
        P("section", None, "dp", None),
        P("section", None),
        P("section", None, "dp", "tensor"),
        P("section", "tensor", "dp"),
        P("section", None),
        P("section", None, None),
        P("section", "dp", None, "tensor"),
        P("section", "dp", "tensor", None),
    )
    out_specs = (
        P("section", None, ("dp", "tensor"), None),
        P("section", None, ("dp", "tensor"), None),
        P("section", None),
        P("section", None, "dp", "tensor"),
        P("section", "tensor", "dp"),
        P("section", None),
        P("section", None, None),
        P("section", "dp", None, "tensor"),
        P("section", "dp", "tensor", None),
    )
    return jax.shard_map(shards, mesh=mesh, in_specs=in_specs, out_specs=out_specs, check_vma=False)
```

```python
import functools
import math

import jax
import jax.numpy as jnp
from jax import lax
from jax.experimental import pallas as pl
from jax.experimental.pallas import tpu as pltpu
from jax.sharding import PartitionSpec as P

HD = 64
LANES = 128
EPSILON = 1e-06
NEGATIVE = -1e30
F32 = jnp.float32
BF16 = jnp.bfloat16
CUBIC = 0.044715
VMEM_LIMIT = 56 * 1024 * 1024
SLOPE = math.sqrt(2.0 / math.pi)


def swap(values, axis):
    return lax.ppermute(values, axis, [(0, 1), (1, 0)])


def all_to_all(values):
    return lax.all_to_all(values, "dp", split_axis=0, concat_axis=0, tiled=True)


def after(value, *anchors):
    return lax.optimization_barrier((value, anchors))[0]


def dot(left, right, left_dim, right_dim):
    return lax.dot_general(
        left, right, (((left_dim,), (right_dim,)), ((), ())), preferred_element_type=F32
    )


def ordered(index, own, other):
    return jnp.where(
        index == 0, jnp.concatenate([own, other], axis=0), jnp.concatenate([other, own], axis=0)
    )


def entry(array, index):
    return lax.dynamic_index_in_dim(array, index, 0, keepdims=False)


def norm_forward(inputs, gain):
    scaling = lax.rsqrt(jnp.mean(inputs * inputs, axis=-1, keepdims=True) + EPSILON)
    return inputs * scaling * gain


def norm_back(upstream, inputs, gain):
    scaling = lax.rsqrt(jnp.mean(inputs * inputs, axis=-1, keepdims=True) + EPSILON)
    weighted = upstream * gain
    scaled = inputs * scaling
    inner = jnp.mean(weighted * inputs, axis=-1, keepdims=True)
    return (
        scaling * weighted - scaled * (scaling * scaling * inner),
        jnp.sum(upstream * scaled, axis=0, keepdims=True),
    )


def smooth_gate(values):
    return jax.nn.gelu(values, approximate=True)


def routing(route_row, experts):
    count = route_row.shape[0]
    capacity = 2 * count // experts
    hot = route_row[:, None] == jnp.arange(experts, dtype=jnp.int32)[None, :]
    places = jnp.arange(count, dtype=jnp.int32)
    earlier = (places[:, None] > places[None, :]).astype(BF16)
    ranks = dot(earlier, hot.astype(BF16), 1, 0)
    ranking = jnp.sum(ranks * hot.astype(F32), axis=1).astype(jnp.int32)
    slots = route_row * capacity + ranking
    places = jnp.arange(experts * capacity, dtype=jnp.int32)
    return (
        (slots[None, :] == places[:, None]).astype(BF16),
        (slots[:, None] == places[None, :]).astype(BF16),
    )


def head_lanes(count):
    return lax.broadcasted_iota(jnp.int32, (count, LANES), 1) // HD


def attention_bias(seg_col, seg_row, count):
    rows = lax.broadcasted_iota(jnp.int32, (count, count), 0)
    cols = lax.broadcasted_iota(jnp.int32, (count, count), 1)
    return jnp.where((seg_col == seg_row) & (rows >= cols), 0.0, NEGATIVE)


def expert_chances(rows, router, experts):
    logits = dot(rows, router, 1, 1)
    lane = lax.broadcasted_iota(jnp.int32, logits.shape, 1)
    logits = jnp.where(lane < experts, logits, NEGATIVE)
    raised = jnp.exp(logits - jnp.max(logits, axis=-1, keepdims=True))
    return raised * (1.0 / jnp.sum(raised, axis=-1, keepdims=True))


def forward_kernel(get, outs, send, *, experts, joined):
    (xn_ref, qkv_ref, lse_ref, *o_refs) = outs[:5]
    (h_ref, gate_ref, out_ref) = outs[5:8]
    if joined:
        mixed_in = dot(get("taking")[...], get("back")[...], 1, 0)
        result = (get("h_before")[...] + get("gate_before")[...] * mixed_in).astype(BF16)
        outs[8][...] = result
        send(8)
        a = result.astype(F32)
    else:
        a = get("a")[...].astype(F32)
    count, width = a.shape
    part = width // 2
    pairs = part // LANES
    gains = get("gains")
    xn = norm_forward(a, gains[0:1, :]).astype(BF16)
    xn_ref[...] = xn
    send(0)
    bias = attention_bias(get("seg_col")[...], get("seg_row")[...], count)
    lanes = head_lanes(count)
    scale = 1.0 / math.sqrt(HD)
    w_ref = get("weights")
    for half in range(2):
        base = half * 3 * part
        qkv_ref[:, base:base + 3 * part] = dot(
            xn, w_ref[:, half * 4 * part:half * 4 * part + 3 * part], 1, 0
        ).astype(BF16)
    send(1)
    attended = a
    lse = jnp.zeros((count, LANES), F32)
    for half in range(2):
        base = half * 3 * part
        for pair in range(pairs):
            at = base + pair * LANES
            query = qkv_ref[:, at:at + LANES]
            key = qkv_ref[:, at + part:at + part + LANES]
            value = qkv_ref[:, at + 2 * part:at + 2 * part + LANES]
            mixed = None
            for head in range(2):
                own = jnp.where(lanes == head, query, jnp.zeros_like(query))
                scores = dot(own, key, 1, 1) * scale + bias
                top = jnp.max(scores, axis=-1, keepdims=True)
                weight = jnp.exp(scores - top)
                total = jnp.sum(weight, axis=-1, keepdims=True)
                probs = (weight * (1.0 / total)).astype(BF16)
                number = (half * pairs + pair) * 2 + head
                lse = jnp.where(
                    lax.broadcasted_iota(jnp.int32, lse.shape, 1) == number,
                    top + jnp.log(total), lse,
                )
                part_out = dot(probs, value, 1, 0)
                mixed = part_out if head == 0 else jnp.where(lanes == 0, mixed, part_out)
            o_refs[half][:, pair * LANES:(pair + 1) * LANES] = mixed.astype(BF16)
        send(3 + half)
        attended = attended + dot(
            o_refs[half][...],
            w_ref[:, half * 4 * part + 3 * part:(half + 1) * 4 * part], 1, 1,
        )
    lse_ref[...] = lse
    send(2)
    h_ref[...] = attended
    send(5)
    hn = norm_forward(attended, gains[1:2, :]).astype(BF16)
    out_ref[...] = dot(get("placing")[...], hn, 1, 0).astype(BF16)
    send(7)
    chances = expert_chances(hn, get("router")[...], experts)
    lane = lax.broadcasted_iota(jnp.int32, chances.shape, 1)
    gate_ref[...] = jnp.sum(
        jnp.where(lane == get("route")[...], chances, 0.0), axis=-1, keepdims=True
    )
    send(6)


def hidden_kernel(get, outs, send):
    (dattn_ref, dh_ref, small_ref) = outs
    hn_grad = dot(get("taking")[...], get("back")[...], 1, 0)
    gains = get("gains")
    dz = get("dz")[...].astype(F32)
    hidden_part, small_ref[...] = norm_back(hn_grad, get("h")[...], gains[1:2, :])
    hidden_grad = dz + hidden_part
    dattn_ref[...] = hidden_grad.astype(BF16)
    send(0)
    dh_ref[...] = hidden_grad
    send(1)
    send(2)


def backward_kernel(get, outs, send, *, spread):
    (da_ref, *dqkv_refs, small_ref) = outs[:4]
    gains = get("gains")
    attended_grad = get("dattn")[...]
    count, width = attended_grad.shape
    part = width // 2
    pairs = part // LANES
    bias = attention_bias(get("seg_col")[...], get("seg_row")[...], count)
    lanes = head_lanes(count)
    scale = 1.0 / math.sqrt(HD)
    w_ref, qkv_ref, lse_ref = (get("weights"), get("qkv"), get("lse"))
    normed_grad = jnp.zeros((count, width), F32)
    for half in range(2):
        base = half * 3 * part
        mixed_grad = dot(
            attended_grad, w_ref[:, half * 4 * part + 3 * part:(half + 1) * 4 * part], 1, 0
        ).astype(BF16)
        for pair in range(pairs):
            at = base + pair * LANES
            query = qkv_ref[:, at:at + LANES]
            key = qkv_ref[:, at + part:at + part + LANES]
            value = qkv_ref[:, at + 2 * part:at + 2 * part + LANES]
            grad = mixed_grad[:, pair * LANES:(pair + 1) * LANES]
            dq = dk = dv = None
            for head in range(2):
                number = (half * pairs + pair) * 2 + head
                zero = jnp.zeros_like(query)
                own_q = jnp.where(lanes == head, query, zero)
                own_g = jnp.where(lanes == head, grad, zero)
                scores = dot(own_q, key, 1, 1) * scale + bias
                probs = jnp.exp(scores - lse_ref[:, number:number + 1])
                prob_grad = dot(own_g, value, 1, 1)
                inner = jnp.sum(probs * prob_grad, axis=-1, keepdims=True)
                score_grad = (probs * (prob_grad - inner)).astype(BF16)
                head_dv = dot(probs.astype(BF16), own_g, 0, 0)
                head_dk = dot(score_grad, own_q, 0, 0)
                head_dq = dot(score_grad, key, 1, 0)
                if head == 0:
                    dq, dk, dv = (head_dq, head_dk, head_dv)
                else:
                    dq = jnp.where(lanes == 0, dq, head_dq)
                    dk = dk + head_dk
                    dv = dv + head_dv
            at = pair * LANES
            dqkv_refs[half][:, at:at + LANES] = (dq * scale).astype(BF16)
            dqkv_refs[half][:, at + part:at + part + LANES] = (dk * scale).astype(BF16)
            dqkv_refs[half][:, at + 2 * part:at + 2 * part + LANES] = dv.astype(BF16)
        send(1 + half)
        normed_grad = normed_grad + dot(
            dqkv_refs[half][...],
            w_ref[:, half * 4 * part:half * 4 * part + 3 * part], 1, 1,
        )
    input_part, small_ref[...] = norm_back(
        normed_grad, get("a")[...].astype(F32), gains[0:1, :]
    )
    input_grad = (get("dh")[...] + input_part).astype(BF16)
    if spread:
        outs[4][...] = dot(get("placing")[...], input_grad, 1, 0).astype(BF16)
        send(4)
    da_ref[...] = input_grad
    send(0)
    send(3)


def staged_call(kernel, inputs, outs, flops):
    names = list(inputs)
    args = [inputs[name] for name in names]
    count = len(args)
    total = count + len(outs)

    def body(*refs):
        held, marks = (refs[total:-1], refs[-1])
        copies = [
            pltpu.make_async_copy(*pair, marks.at[number])
            for number, pair in enumerate(
                [(refs[i], held[i]) for i in range(count)]
                + [(held[i], refs[i]) for i in range(count, total)]
            )
        ]
        for copy in copies[:count]:
            copy.start()
        ready = set()

        def get(name):
            number = names.index(name)
            if number not in ready:
                ready.add(number)
                copies[number].wait()
            return held[number]

        kernel(get, held[count:], lambda number: copies[count + number].start())
        for copy in copies[count:]:
            copy.wait()

    moved = sum(math.prod(v.shape) * v.dtype.itemsize for v in (*args, *outs))
    return pl.pallas_call(
        body,
        out_shape=outs,
        in_specs=[pl.BlockSpec(memory_space=pltpu.HBM)] * count,
        out_specs=[pl.BlockSpec(memory_space=pltpu.HBM)] * len(outs),
        scratch_shapes=[pltpu.VMEM(v.shape, v.dtype) for v in (*args, *outs)]
        + [pltpu.SemaphoreType.DMA((total,))],
        compiler_params=pltpu.CompilerParams(vmem_limit_bytes=VMEM_LIMIT),
        cost_estimate=pl.CostEstimate(flops=flops, bytes_accessed=moved, transcendentals=0),
    )(*args)


def layer_start(source, params, segments, route_col, placing):
    gains, weights, router_w, experts = params
    joined = "back" in source
    struct = jax.ShapeDtypeStruct
    count = route_col.shape[0]
    width = weights.shape[0]
    outs = [
        struct((count, width), BF16),
        struct((count, 3 * width), BF16),
        struct((count, LANES), F32),
        struct((count, width // 2), BF16),
        struct((count, width // 2), BF16),
        struct((count, width), F32),
        struct((count, 1), F32),
        struct((placing.shape[0], width), BF16),
    ]
    if joined:
        outs.append(struct((count, width), BF16))
    inputs = dict(
        source, gains=gains, seg_col=segments[0], seg_row=segments[1], weights=weights,
        placing=placing, router=router_w, route=route_col,
    )
    return staged_call(
        functools.partial(forward_kernel, experts=experts, joined=joined), inputs, outs, 3 * 10**9
    )


def hidden_end(back, taking, upstream, state, params):
    count, width = upstream.shape
    struct = jax.ShapeDtypeStruct
    outs = [struct((count, width), BF16), struct((count, width), F32), struct((1, width), F32)]
    given = dict(taking=taking, back=back, gains=params[0], dz=upstream, h=state["h"])
    return staged_call(hidden_kernel, given, outs, 3 * 10**8)


def layer_end(dattn, hidden_grad, inputs, state, params, segments, placing):
    gains, weights = params[:2]
    count, width = inputs.shape
    struct = jax.ShapeDtypeStruct
    outs = [
        struct((count, width), BF16),
        struct((count, 3 * width // 2), BF16),
        struct((count, 3 * width // 2), BF16),
        struct((1, width), F32),
    ]
    given = dict(
        gains=gains, dattn=dattn, seg_col=segments[0], seg_row=segments[1], weights=weights,
        qkv=state["qkv"], lse=state["lse"], a=inputs, dh=hidden_grad,
    )
    if placing is not None:
        given["placing"] = placing
        outs.append(struct((placing.shape[0], width), BF16))
    return staged_call(
        functools.partial(backward_kernel, spread=placing is not None), given, outs, 5 * 10**9
    )


def split_dot(left, right, left_dim, right_dim):
    high = left.astype(BF16)
    low = (left - high.astype(F32)).astype(BF16)
    return dot(high, right, left_dim, right_dim) + dot(low, right, left_dim, right_dim)


def expert_kernel(
    rows_ref, dz_ref, in_ref, out_ref, router_ref, hot_ref,
    dx_ref, act_ref, dpre_ref, dy_ref, g_router_ref, chance_ref, gate_ref, total_ref, *, experts,
):
    step = pl.program_id(0)
    rows = rows_ref[...]

    @pl.when(step == 0)
    def _():
        chances = expert_chances(rows, router_ref[...], experts)
        chance_ref[...] = chances
        gate = jnp.sum(chances * hot_ref[...], axis=-1, keepdims=True)
        dy_ref[...] = (gate * dz_ref[...].astype(F32)).astype(BF16)
        gate_ref[...] = jnp.zeros_like(gate_ref)
        total_ref[...] = jnp.zeros_like(total_ref)

    before = dot(rows, in_ref[...], 1, 0)
    square = before * before
    bent = jnp.tanh(SLOPE * before * (1.0 + CUBIC * square))
    lifted = 0.5 * (1.0 + bent)
    act = (before * lifted).astype(BF16)
    slope = lifted + 0.5 * before * (1.0 - bent * bent) * (
        SLOPE * (1.0 + 3.0 * CUBIC * square)
    )
    act_grad = dot(dy_ref[...], out_ref[...], 1, 1)
    dpre = (act_grad * slope).astype(BF16)
    act_ref[...] = act
    dpre_ref[...] = dpre
    gate_ref[...] += jnp.sum(act_grad * act.astype(F32), axis=-1, keepdims=True)
    total_ref[...] += dot(dpre, in_ref[...], 1, 1)

    @pl.when(step == pl.num_programs(0) - 1)
    def _():
        logit_grad = (hot_ref[...] - chance_ref[...]) * gate_ref[...]
        g_router_ref[...] = split_dot(logit_grad, rows, 0, 0)
        dx_ref[...] = (total_ref[...] + split_dot(logit_grad, router_ref[...], 1, 0)).astype(
            dx_ref.dtype
        )


def expert_back(rows, dz, in_w, expert_w, layer, router_w, hot_row, experts, kind):
    count, width = rows.shape
    hidden = in_w.shape[1]
    block = 512
    struct = jax.ShapeDtypeStruct
    whole = pl.BlockSpec((count, width), lambda j: (0, 0))
    wide = pl.BlockSpec((count, block), lambda j: (0, j))
    router_spec = pl.BlockSpec((LANES, width), lambda j: (0, 0))
    return pl.pallas_call(
        functools.partial(expert_kernel, experts=experts),
        grid=(hidden // block,),
        out_shape=[
            struct((count, width), kind),
            struct((count, hidden), BF16),
            struct((count, hidden), BF16),
            struct((count, width), BF16),
            struct((LANES, width), F32),
        ],
        in_specs=[
            whole,
            whole,
            pl.BlockSpec((width, block), lambda j: (0, j)),
            pl.BlockSpec((None, block, width), lambda j: (layer, j, 0)),
            router_spec,
            pl.BlockSpec((1, LANES), lambda j: (0, 0)),
        ],
        out_specs=[whole, wide, wide, whole, router_spec],
        scratch_shapes=[
            pltpu.VMEM((count, LANES), F32),
            pltpu.VMEM((count, 1), F32),
            pltpu.VMEM((count, width), F32),
        ],
        compiler_params=pltpu.CompilerParams(
            dimension_semantics=("arbitrary",), vmem_limit_bytes=VMEM_LIMIT
        ),
        cost_estimate=pl.CostEstimate(
            flops=6 * count * width * hidden, bytes_accessed=12 * 10**6, transcendentals=0
        ),
    )(rows, dz, in_w, expert_w, router_w, hot_row)


def across_parts(grad, section):
    width = grad.shape[0]
    count = lax.axis_size("dp")
    halves = grad.reshape(count, 2, width // count // 2, -1)
    keep = lax.dynamic_index_in_dim(halves, section, 1, keepdims=False)
    send = lax.dynamic_index_in_dim(halves, 1 - section, 1, keepdims=False)
    return (keep, send.astype(BF16))


def across_sum(keep, send):
    return (keep + swap(send, "section").astype(F32)).astype(BF16)


def exchange_across(grad, section):
    return across_sum(*across_parts(grad, section))


def pair_up(values, tensor):
    half = values.shape[0] // 2
    halves = values.reshape(2, half, -1)
    own = entry(halves, tensor)
    other = swap(entry(halves, 1 - tensor), "tensor")
    return ordered(tensor, own[None], other[None])


def gelu_pair(before, active_grad):
    activated, back = jax.vjp(smooth_gate, before)
    return (activated.astype(BF16), back(active_grad)[0].astype(BF16))


def shards(
    x_in, d_out, lengths, routes, gain_attn, w_qkv, w_attn_out, gain_ffn, w_router, w_in, w_exp_out
):
    section = lax.axis_index("section")
    tensor = lax.axis_index("tensor")
    count = lax.axis_size("dp")
    width = x_in.shape[2]
    part = width // 2
    rows = 2 * x_in.shape[1]
    experts = w_router.shape[2]
    own_batch = 2 * section + tensor
    peer_batch = 2 * section + 1 - tensor

    def of_layer(layer, own, other):
        return jnp.where(section == layer, own, other)

    def pick(first, second):
        return jnp.where(section == 0, first, second)

    def by_layer(own):
        other = swap(own, "section")
        return [of_layer(layer, own, other) for layer in range(2)]

    def whole_group(array):
        return ordered(
            tensor, entry(array, own_batch), swap(entry(array, peer_batch), "tensor")
        )

    packed = jnp.concatenate([w_qkv[0], w_attn_out[0].T[None]], axis=0)
    packed = jnp.moveaxis(packed, 0, 1).reshape(width // count, -1)
    small = by_layer(jnp.concatenate([gain_attn, gain_ffn, w_router[0].T], axis=0))
    own_route = entry(routes[0, :, :, 0], own_batch)
    other_route = swap(entry(routes[0, :, :, 0], 2 * (1 - section) + tensor), "section")
    route = [of_layer(layer, own_route, other_route) for layer in range(2)]
    far_pack = swap(packed, "section")
    first_pack = of_layer(0, packed, far_pack)
    first_beside = swap(first_pack, "tensor")
    first_packs = jnp.concatenate([first_pack, first_beside], axis=1)
    first_w = lax.all_gather(first_packs, "dp", axis=0, tiled=True)
    x_own = whole_group(x_in)
    far_pack, d_last = after((far_pack, d_out), first_beside)
    second_pack = of_layer(1, packed, far_pack)
    second_pack = jnp.concatenate([second_pack, swap(second_pack, "tensor")], axis=1)
    dz_last = whole_group(d_last)
    far_in = swap(w_in[0, 0], "section")
    in_w = [of_layer(layer, w_in[0, 0], far_in) for layer in range(2)]
    both_out = lax.all_gather(after(w_exp_out[0, 0], first_packs), "section", axis=0)
    expert_w = [both_out[0], both_out[1]]

    tables = [routing(row, experts) for row in route]
    placing = [table[0] for table in tables]
    taking = [table[1] for table in tables]
    route_col = [row[:, None] for row in route]
    gains = [small[layer][:2].astype(F32) for layer in range(2)]
    router_w = [jnp.pad(small[layer][2:], ((0, LANES - experts), (0, 0))) for layer in range(2)]
    bounds = jnp.cumsum(entry(lengths[:, 0], own_batch))
    places = jnp.arange(rows, dtype=jnp.int32)
    segment = jnp.sum((places[:, None] >= bounds[None, :]).astype(jnp.int32), axis=1)
    segments = (segment[:, None], segment[None, :])
    hot_row = (
        jnp.arange(LANES, dtype=jnp.int32)[None, :] == lax.axis_index("dp")
    ).astype(F32)
    keys = ("xn", "qkv", "lse", "o", "o_far", "h", "gate")

    def expert_forward(values, layer):
        active = smooth_gate(dot(values, in_w[layer], 1, 0)).astype(BF16)
        return dot(active, expert_w[layer], 1, 0)

    def fold(own, peer):
        own = lax.optimization_barrier(own)
        return (own + swap(peer.astype(BF16), "tensor").astype(F32)).astype(BF16)

    params0 = (gains[0], first_w, router_w[0], experts)
    *state0, outgoing0 = layer_start(
        {"a": after(x_own, far_in)}, params0, segments, route_col[0], placing[0]
    )
    state0 = dict(zip(keys, state0))
    mine0 = all_to_all(outgoing0)
    side_xn0 = swap(state0["xn"], "tensor")
    side_o0 = swap(state0["o_far"], "tensor")
    peer0 = swap(
        after(mine0, side_xn0, side_o0, in_w), "tensor"
    )
    second_w = lax.all_gather(after(second_pack, mine0), "dp", axis=0, tiled=True)
    back0 = all_to_all(fold(expert_forward(mine0, 0), expert_forward(peer0, 0)))

    dz_out1 = dot(placing[1], dz_last, 1, 0).astype(BF16)
    mine_dz1 = all_to_all(after(dz_out1, back0))
    params1 = (gains[1], second_w, router_w[1], experts)
    *state1, outgoing1, out0 = layer_start(
        {"taking": taking[0], "back": back0, "h_before": state0["h"],
         "gate_before": state0["gate"]},
        params1, segments, route_col[1], placing[1],
    )
    state1 = dict(zip(keys, state1))
    peer_dz1 = swap(mine_dz1, "tensor")
    pair_out0 = pair_up(out0, tensor)
    mine1 = all_to_all(after(outgoing1, mine_dz1, pair_out0))
    peer1 = swap(after(mine1, peer_dz1), "tensor")

    def both_back(layer, mine, peer, mine_dz, peer_dz):
        args = (in_w[layer], both_out, layer, router_w[layer], hot_row, experts)
        own = expert_back(mine, mine_dz, *args, F32)
        peer, peer_dz = after((peer, peer_dz), own[0])
        return (own, expert_back(peer, peer_dz, *args, BF16))

    own_b1, peer_b1 = both_back(1, mine1, peer1, mine_dz1, peer_dz1)
    peer_dx1 = swap(peer_b1[0], "tensor")
    far_mine = swap(pick(mine1, mine0), "section")
    far_peer = swap(pick(after(peer1, own_b1[0]), peer0), "section")
    dback1 = all_to_all(
        after((own_b1[0] + peer_dx1.astype(F32)).astype(BF16), far_mine)
    )
    late_mine1, late_peer1 = after((mine1, peer1), peer_b1[0])
    peer_y1 = expert_forward(late_peer1, 1).astype(BF16)
    own_y1 = expert_forward(late_mine1, 1)
    side_y1 = swap(after(peer_y1, peer_dx1), "tensor")
    total_y1 = (own_y1 + side_y1.astype(F32)).astype(BF16)
    side_xn1, side_o1 = [
        swap(half, "tensor")
        for half in after((state1["xn"], state1["o_far"]), peer_dx1)
    ]
    dattn1, dh1, gain_f1 = hidden_end(
        after(dback1, own_y1, peer_y1, side_xn1, side_o1, far_peer), taking[1], dz_last, state1, params1
    )
    side_dattn1 = swap(dattn1, "tensor")
    grad1, dqkv1, dqkv_far1, gain_a1, outgoing_dz0 = layer_end(
        dattn1, dh1, out0, state1, params1, segments, placing[0]
    )

    mine_dz0 = all_to_all(outgoing_dz0)
    side_dqkv1 = swap(dqkv_far1, "tensor")
    def stack(first, second):
        return jnp.concatenate([first, second], axis=0)

    def attention_grad(xn, side_xn, dqkv, side_dqkv):
        return dot(stack(xn, side_xn), stack(dqkv, side_dqkv), 0, 0)

    def output_grad(dattn, side_dattn, mixed, side_mixed):
        return dot(stack(dattn, side_dattn), stack(mixed, side_mixed), 0, 0)

    full1 = jnp.concatenate(
        [
            attention_grad(state1["xn"], side_xn1, dqkv1, side_dqkv1),
            output_grad(dattn1, side_dattn1, state1["o"], side_o1),
        ],
        axis=1,
    )
    keep1, send1 = across_parts(full1, section)
    peer_dz0 = swap(after(mine_dz0, send1, side_y1), "tensor")
    across1 = swap(send1, "section")
    back1 = all_to_all(after(total_y1, mine_dz0))
    peer_dz0 = after(peer_dz0, across1, back1)
    own_b0, peer_b0 = both_back(0, mine0, peer0, mine_dz0, peer_dz0)
    keep1, across1 = after((keep1, across1), own_b0[0])
    reduced1 = all_to_all((keep1 + across1.astype(F32)).astype(BF16))
    peer_dx0 = swap(peer_b0[0], "tensor")
    pair_grad1 = pair_up(after(grad1, peer_dx0), tensor)


    def gather_rows(number, index):
        return stack((own_b0, own_b1)[number][index], (peer_b0, peer_b1)[number][index])

    late_mine0, late_mine1, own_b1, peer_b1 = after((mine0, mine1, own_b1, peer_b1), peer_b0[0])
    near_rows = pick(stack(late_mine0, peer0), stack(late_mine1, peer1))
    near_dpre = pick(gather_rows(0, 2), gather_rows(1, 2))
    near_in = dot(near_rows, near_dpre, 0, 0)
    far_dys = [
        swap(pick(*after((part_b1[3], part_b0[3]), peer_b0[0])), "section")
        for part_b1, part_b0 in ((own_b1, own_b0), (peer_b1, peer_b0))
    ]
    total_dx0 = after(
        (own_b0[0] + peer_dx0.astype(F32)).astype(BF16), near_in, reduced1
    )
    dback0 = all_to_all(total_dx0)
    dy0, dy1 = (gather_rows(0, 3), gather_rows(1, 3))
    near_dy = pick(dy0, dy1)
    late_back1 = after(back1, total_dx0)
    out1 = (state1["h"] + state1["gate"] * dot(taking[1], late_back1, 1, 0)).astype(BF16)
    pair_out1 = pair_up(out1, tensor)
    far_outs = swap(pick(pair_out1, pair_out0), "section")
    near_act = pick(*after((gather_rows(0, 1), gather_rows(1, 1)), total_dx0))
    near_out = dot(near_act, near_dy, 0, 0)
    dattn0, dh0, gain_f0 = hidden_end(
        after(dback0, near_out, pair_out1), taking[0], grad1, state0, params0
    )
    side_dattn0 = swap(dattn0, "tensor")
    grad0, dqkv0, dqkv_far0, gain_a0 = layer_end(
        dattn0, dh0, x_own, state0, params0, segments, None
    )

    side_dqkv0 = swap(dqkv_far0, "tensor")
    late_dattn0, late_side = after((dattn0, side_dattn0), dqkv0)
    out_keep, out_send = across_parts(
        output_grad(late_dattn0, late_side, state0["o"], side_o0), section
    )
    smalls = jnp.stack(
        [
            jnp.concatenate([*gain, (own[4] + peer[4])[:experts]], axis=0)
            for gain, own, peer in (
                ((gain_a0, gain_f0), own_b0, peer_b0), ((gain_a1, gain_f1), own_b1, peer_b1)
            )
        ]
    )
    smalls = after(smalls, out_send)
    smalls = all_to_all(jnp.broadcast_to(smalls[None], (count,) + smalls.shape))
    smalls = smalls.sum(axis=0)
    ready_xn0 = after(state0["xn"], out_send)
    qkv_keep, qkv_send = across_parts(
        attention_grad(ready_xn0, side_xn0, dqkv0, side_dqkv0), section
    )
    far_rows = stack(*after((far_mine, far_peer), qkv_send))
    far_dy = stack(*after(tuple(far_dys), qkv_send))
    far_before = dot(far_rows, w_in[0, 0], 1, 0)
    half0 = jnp.concatenate(
        [
            across_sum(after(qkv_keep, far_before, far_dy), qkv_send),
            across_sum(out_keep, out_send),
        ],
        axis=2,
    )
    reduced0 = all_to_all(half0)
    pair_grad0 = pair_up(after(grad0, qkv_send), tensor)
    far_grads = swap(pick(pair_grad1, after(pair_grad0, half0)), "section")
    far_dy, reduced1 = after((far_dy, reduced1), half0)
    far_act, far_dpre = gelu_pair(far_before, dot(far_dy, w_exp_out[0, 0], 1, 1))
    in_w_grad = near_in + dot(far_rows, far_dpre, 0, 0)
    expert_w_grad = near_out + dot(far_act, far_dy, 0, 0)

    smalls = after(smalls, qkv_send)
    smalls = smalls + swap(smalls, "tensor")
    own_small = pick(smalls[0], smalls[1]) + swap(pick(smalls[1], smalls[0]), "section")

    reduced1 = reduced1.astype(F32).sum(axis=0)
    reduced0 = after(reduced0, in_w_grad, expert_w_grad, far_grads, far_outs, own_small)
    reduced0 = reduced0.astype(F32).sum(axis=0)
    own_half = pick(reduced0, reduced1)
    other_half = swap(pick(reduced1, reduced0).astype(BF16), "section").astype(F32)
    joined = ordered(section, own_half, other_half)
    qkv_grad = jnp.stack([joined[:, part * kind:part * (kind + 1)] for kind in range(3)])
    out_grad = joined[:, 3 * part:].T
    section_out = ordered(section, pick(pair_out0, pair_out1), far_outs)
    section_in_grad = ordered(section, pick(pair_grad0, pair_grad1), far_grads)
    return (
        section_out[None],
        section_in_grad[None],
        own_small[0][None],
        qkv_grad[None],
        out_grad[None],
        own_small[1][None],
        own_small[2:].T[None],
        in_w_grad[None, None],
        expert_w_grad[None, None],
    )


def solution(mesh):
    in_specs = (
        P(None, ("dp", "tensor"), None),
        P(None, ("dp", "tensor"), None),
        P(None, "dp", None),
        P("section", None, "dp", None),
        P("section", None),
        P("section", None, "dp", "tensor"),
        P("section", "tensor", "dp"),
        P("section", None),
        P("section", None, None),
        P("section", "dp", None, "tensor"),
        P("section", "dp", "tensor", None),
    )
    out_specs = (
        P("section", None, ("dp", "tensor"), None),
        P("section", None, ("dp", "tensor"), None),
        P("section", None),
        P("section", None, "dp", "tensor"),
        P("section", "tensor", "dp"),
        P("section", None),
        P("section", None, None),
        P("section", "dp", None, "tensor"),
        P("section", "dp", "tensor", None),
    )
    return jax.shard_map(shards, mesh=mesh, in_specs=in_specs, out_specs=out_specs, check_vma=False)
```

```python
import functools
import math

import jax
import jax.numpy as jnp
from jax import lax
from jax.experimental import pallas as pl
from jax.experimental.pallas import tpu as pltpu
from jax.sharding import PartitionSpec as P

HD = 64
LANES = 128
EPSILON = 1e-06
NEGATIVE = -1e30
F32 = jnp.float32
BF16 = jnp.bfloat16
CUBIC = 0.044715
VMEM_LIMIT = 56 * 1024 * 1024
SLOPE = math.sqrt(2.0 / math.pi)


def swap(values, axis):
    return lax.ppermute(values, axis, [(0, 1), (1, 0)])


def all_to_all(values):
    return lax.all_to_all(values, "dp", split_axis=0, concat_axis=0, tiled=True)


def after(value, *anchors):
    return lax.optimization_barrier((value, anchors))[0]


def dot(left, right, left_dim, right_dim):
    return lax.dot_general(
        left, right, (((left_dim,), (right_dim,)), ((), ())), preferred_element_type=F32
    )


def ordered(index, own, other):
    return jnp.where(
        index == 0, jnp.concatenate([own, other], axis=0), jnp.concatenate([other, own], axis=0)
    )


def entry(array, index):
    return lax.dynamic_index_in_dim(array, index, 0, keepdims=False)


def norm_forward(inputs, gain):
    scaling = lax.rsqrt(jnp.mean(inputs * inputs, axis=-1, keepdims=True) + EPSILON)
    return inputs * scaling * gain


def norm_back(upstream, inputs, gain):
    scaling = lax.rsqrt(jnp.mean(inputs * inputs, axis=-1, keepdims=True) + EPSILON)
    weighted = upstream * gain
    scaled = inputs * scaling
    inner = jnp.mean(weighted * inputs, axis=-1, keepdims=True)
    return (
        scaling * weighted - scaled * (scaling * scaling * inner),
        jnp.sum(upstream * scaled, axis=0, keepdims=True),
    )


def smooth_gate(values):
    return jax.nn.gelu(values, approximate=True)


def routing(route_row, experts):
    count = route_row.shape[0]
    capacity = 2 * count // experts
    hot = route_row[:, None] == jnp.arange(experts, dtype=jnp.int32)[None, :]
    places = jnp.arange(count, dtype=jnp.int32)
    earlier = (places[:, None] > places[None, :]).astype(BF16)
    ranks = dot(earlier, hot.astype(BF16), 1, 0)
    ranking = jnp.sum(ranks * hot.astype(F32), axis=1).astype(jnp.int32)
    slots = route_row * capacity + ranking
    places = jnp.arange(experts * capacity, dtype=jnp.int32)
    return (
        (slots[None, :] == places[:, None]).astype(BF16),
        (slots[:, None] == places[None, :]).astype(BF16),
    )


def head_lanes(count):
    return lax.broadcasted_iota(jnp.int32, (count, LANES), 1) // HD


def attention_bias(seg_col, seg_row, count):
    rows = lax.broadcasted_iota(jnp.int32, (count, count), 0)
    cols = lax.broadcasted_iota(jnp.int32, (count, count), 1)
    return jnp.where((seg_col == seg_row) & (rows >= cols), 0.0, NEGATIVE)


def expert_chances(rows, router, experts):
    logits = dot(rows, router, 1, 1)
    lane = lax.broadcasted_iota(jnp.int32, logits.shape, 1)
    logits = jnp.where(lane < experts, logits, NEGATIVE)
    raised = jnp.exp(logits - jnp.max(logits, axis=-1, keepdims=True))
    return raised * (1.0 / jnp.sum(raised, axis=-1, keepdims=True))


def forward_kernel(get, outs, send, *, experts, joined):
    (xn_ref, qkv_ref, lse_ref, *o_refs) = outs[:5]
    (h_ref, gate_ref, out_ref) = outs[5:8]
    if joined:
        mixed_in = dot(get("taking")[...], get("back")[...], 1, 0)
        result = (get("h_before")[...] + get("gate_before")[...] * mixed_in).astype(BF16)
        outs[8][...] = result
        send(8)
        a = result.astype(F32)
    else:
        a = get("a")[...].astype(F32)
    count, width = a.shape
    part = width // 2
    pairs = part // LANES
    gains = get("gains")
    xn = norm_forward(a, gains[0:1, :]).astype(BF16)
    xn_ref[...] = xn
    send(0)
    bias = attention_bias(get("seg_col")[...], get("seg_row")[...], count)
    lanes = head_lanes(count)
    scale = 1.0 / math.sqrt(HD)
    w_ref = get("weights")
    for half in range(2):
        base = half * 3 * part
        qkv_ref[:, base:base + 3 * part] = dot(
            xn, w_ref[:, half * 4 * part:half * 4 * part + 3 * part], 1, 0
        ).astype(BF16)
    send(1)
    attended = a
    lse = jnp.zeros((count, LANES), F32)
    for half in range(2):
        base = half * 3 * part
        for pair in range(pairs):
            at = base + pair * LANES
            query = qkv_ref[:, at:at + LANES]
            key = qkv_ref[:, at + part:at + part + LANES]
            value = qkv_ref[:, at + 2 * part:at + 2 * part + LANES]
            mixed = None
            for head in range(2):
                own = jnp.where(lanes == head, query, jnp.zeros_like(query))
                scores = dot(own, key, 1, 1) * scale + bias
                top = jnp.max(scores, axis=-1, keepdims=True)
                weight = jnp.exp(scores - top)
                total = jnp.sum(weight, axis=-1, keepdims=True)
                probs = (weight * (1.0 / total)).astype(BF16)
                number = (half * pairs + pair) * 2 + head
                lse = jnp.where(
                    lax.broadcasted_iota(jnp.int32, lse.shape, 1) == number,
                    top + jnp.log(total), lse,
                )
                part_out = dot(probs, value, 1, 0)
                mixed = part_out if head == 0 else jnp.where(lanes == 0, mixed, part_out)
            o_refs[half][:, pair * LANES:(pair + 1) * LANES] = mixed.astype(BF16)
        send(3 + half)
        attended = attended + dot(
            o_refs[half][...],
            w_ref[:, half * 4 * part + 3 * part:(half + 1) * 4 * part], 1, 1,
        )
    lse_ref[...] = lse
    send(2)
    h_ref[...] = attended
    send(5)
    hn = norm_forward(attended, gains[1:2, :]).astype(BF16)
    out_ref[...] = dot(get("placing")[...], hn, 1, 0).astype(BF16)
    send(7)
    chances = expert_chances(hn, get("router")[...], experts)
    lane = lax.broadcasted_iota(jnp.int32, chances.shape, 1)
    gate_ref[...] = jnp.sum(
        jnp.where(lane == get("route")[...], chances, 0.0), axis=-1, keepdims=True
    )
    send(6)


def hidden_kernel(get, outs, send):
    (dattn_ref, dh_ref, small_ref) = outs
    hn_grad = dot(get("taking")[...], get("back")[...], 1, 0)
    gains = get("gains")
    dz = get("dz")[...].astype(F32)
    hidden_part, small_ref[...] = norm_back(hn_grad, get("h")[...], gains[1:2, :])
    hidden_grad = dz + hidden_part
    dattn_ref[...] = hidden_grad.astype(BF16)
    send(0)
    dh_ref[...] = hidden_grad
    send(1)
    send(2)


def backward_kernel(get, outs, send, *, spread):
    (da_ref, *dqkv_refs, small_ref) = outs[:4]
    gains = get("gains")
    attended_grad = get("dattn")[...]
    count, width = attended_grad.shape
    part = width // 2
    pairs = part // LANES
    bias = attention_bias(get("seg_col")[...], get("seg_row")[...], count)
    lanes = head_lanes(count)
    scale = 1.0 / math.sqrt(HD)
    w_ref, qkv_ref, lse_ref = (get("weights"), get("qkv"), get("lse"))
    normed_grad = jnp.zeros((count, width), F32)
    for half in range(2):
        base = half * 3 * part
        mixed_grad = dot(
            attended_grad, w_ref[:, half * 4 * part + 3 * part:(half + 1) * 4 * part], 1, 0
        ).astype(BF16)
        for pair in range(pairs):
            at = base + pair * LANES
            query = qkv_ref[:, at:at + LANES]
            key = qkv_ref[:, at + part:at + part + LANES]
            value = qkv_ref[:, at + 2 * part:at + 2 * part + LANES]
            grad = mixed_grad[:, pair * LANES:(pair + 1) * LANES]
            dq = dk = dv = None
            for head in range(2):
                number = (half * pairs + pair) * 2 + head
                zero = jnp.zeros_like(query)
                own_q = jnp.where(lanes == head, query, zero)
                own_g = jnp.where(lanes == head, grad, zero)
                scores = dot(own_q, key, 1, 1) * scale + bias
                probs = jnp.exp(scores - lse_ref[:, number:number + 1])
                prob_grad = dot(own_g, value, 1, 1)
                inner = jnp.sum(probs * prob_grad, axis=-1, keepdims=True)
                score_grad = (probs * (prob_grad - inner)).astype(BF16)
                head_dv = dot(probs.astype(BF16), own_g, 0, 0)
                head_dk = dot(score_grad, own_q, 0, 0)
                head_dq = dot(score_grad, key, 1, 0)
                if head == 0:
                    dq, dk, dv = (head_dq, head_dk, head_dv)
                else:
                    dq = jnp.where(lanes == 0, dq, head_dq)
                    dk = dk + head_dk
                    dv = dv + head_dv
            at = pair * LANES
            dqkv_refs[half][:, at:at + LANES] = (dq * scale).astype(BF16)
            dqkv_refs[half][:, at + part:at + part + LANES] = (dk * scale).astype(BF16)
            dqkv_refs[half][:, at + 2 * part:at + 2 * part + LANES] = dv.astype(BF16)
        send(1 + half)
        normed_grad = normed_grad + dot(
            dqkv_refs[half][...],
            w_ref[:, half * 4 * part:half * 4 * part + 3 * part], 1, 1,
        )
    input_part, small_ref[...] = norm_back(
        normed_grad, get("a")[...].astype(F32), gains[0:1, :]
    )
    input_grad = (get("dh")[...] + input_part).astype(BF16)
    if spread:
        outs[4][...] = dot(get("placing")[...], input_grad, 1, 0).astype(BF16)
        send(4)
    da_ref[...] = input_grad
    send(0)
    send(3)


def staged_call(kernel, inputs, outs, flops):
    names = list(inputs)
    args = [inputs[name] for name in names]
    count = len(args)
    total = count + len(outs)

    def body(*refs):
        held, marks = (refs[total:-1], refs[-1])
        copies = [
            pltpu.make_async_copy(*pair, marks.at[number])
            for number, pair in enumerate(
                [(refs[i], held[i]) for i in range(count)]
                + [(held[i], refs[i]) for i in range(count, total)]
            )
        ]
        for copy in copies[:count]:
            copy.start()
        ready = set()

        def get(name):
            number = names.index(name)
            if number not in ready:
                ready.add(number)
                copies[number].wait()
            return held[number]

        kernel(get, held[count:], lambda number: copies[count + number].start())
        for copy in copies[count:]:
            copy.wait()

    moved = sum(math.prod(v.shape) * v.dtype.itemsize for v in (*args, *outs))
    return pl.pallas_call(
        body,
        out_shape=outs,
        in_specs=[pl.BlockSpec(memory_space=pltpu.HBM)] * count,
        out_specs=[pl.BlockSpec(memory_space=pltpu.HBM)] * len(outs),
        scratch_shapes=[pltpu.VMEM(v.shape, v.dtype) for v in (*args, *outs)]
        + [pltpu.SemaphoreType.DMA((total,))],
        compiler_params=pltpu.CompilerParams(vmem_limit_bytes=VMEM_LIMIT),
        cost_estimate=pl.CostEstimate(flops=flops, bytes_accessed=moved, transcendentals=0),
    )(*args)


def layer_start(source, params, segments, route_col, placing):
    gains, weights, router_w, experts = params
    joined = "back" in source
    struct = jax.ShapeDtypeStruct
    count = route_col.shape[0]
    width = weights.shape[0]
    outs = [
        struct((count, width), BF16),
        struct((count, 3 * width), BF16),
        struct((count, LANES), F32),
        struct((count, width // 2), BF16),
        struct((count, width // 2), BF16),
        struct((count, width), F32),
        struct((count, 1), F32),
        struct((placing.shape[0], width), BF16),
    ]
    if joined:
        outs.append(struct((count, width), BF16))
    inputs = dict(
        source, gains=gains, seg_col=segments[0], seg_row=segments[1], weights=weights,
        placing=placing, router=router_w, route=route_col,
    )
    return staged_call(
        functools.partial(forward_kernel, experts=experts, joined=joined), inputs, outs, 3 * 10**9
    )


def hidden_end(back, taking, upstream, state, params):
    count, width = upstream.shape
    struct = jax.ShapeDtypeStruct
    outs = [struct((count, width), BF16), struct((count, width), F32), struct((1, width), F32)]
    given = dict(taking=taking, back=back, gains=params[0], dz=upstream, h=state["h"])
    return staged_call(hidden_kernel, given, outs, 3 * 10**8)


def layer_end(dattn, hidden_grad, inputs, state, params, segments, placing):
    gains, weights = params[:2]
    count, width = inputs.shape
    struct = jax.ShapeDtypeStruct
    outs = [
        struct((count, width), BF16),
        struct((count, 3 * width // 2), BF16),
        struct((count, 3 * width // 2), BF16),
        struct((1, width), F32),
    ]
    given = dict(
        gains=gains, dattn=dattn, seg_col=segments[0], seg_row=segments[1], weights=weights,
        qkv=state["qkv"], lse=state["lse"], a=inputs, dh=hidden_grad,
    )
    if placing is not None:
        given["placing"] = placing
        outs.append(struct((placing.shape[0], width), BF16))
    return staged_call(
        functools.partial(backward_kernel, spread=placing is not None), given, outs, 5 * 10**9
    )


def split_dot(left, right, left_dim, right_dim):
    high = left.astype(BF16)
    low = (left - high.astype(F32)).astype(BF16)
    return dot(high, right, left_dim, right_dim) + dot(low, right, left_dim, right_dim)


def expert_kernel(
    rows_ref, dz_ref, in_ref, out_ref, router_ref, hot_ref,
    dx_ref, act_ref, dpre_ref, dy_ref, g_router_ref, chance_ref, gate_ref, total_ref, *, experts,
):
    step = pl.program_id(0)
    rows = rows_ref[...]

    @pl.when(step == 0)
    def _():
        chances = expert_chances(rows, router_ref[...], experts)
        chance_ref[...] = chances
        gate = jnp.sum(chances * hot_ref[...], axis=-1, keepdims=True)
        dy_ref[...] = (gate * dz_ref[...].astype(F32)).astype(BF16)
        gate_ref[...] = jnp.zeros_like(gate_ref)
        total_ref[...] = jnp.zeros_like(total_ref)

    before = dot(rows, in_ref[...], 1, 0)
    square = before * before
    bent = jnp.tanh(SLOPE * before * (1.0 + CUBIC * square))
    lifted = 0.5 * (1.0 + bent)
    act = (before * lifted).astype(BF16)
    slope = lifted + 0.5 * before * (1.0 - bent * bent) * (
        SLOPE * (1.0 + 3.0 * CUBIC * square)
    )
    act_grad = dot(dy_ref[...], out_ref[...], 1, 1)
    dpre = (act_grad * slope).astype(BF16)
    act_ref[...] = act
    dpre_ref[...] = dpre
    gate_ref[...] += jnp.sum(act_grad * act.astype(F32), axis=-1, keepdims=True)
    total_ref[...] += dot(dpre, in_ref[...], 1, 1)

    @pl.when(step == pl.num_programs(0) - 1)
    def _():
        logit_grad = (hot_ref[...] - chance_ref[...]) * gate_ref[...]
        g_router_ref[...] = split_dot(logit_grad, rows, 0, 0)
        dx_ref[...] = (total_ref[...] + split_dot(logit_grad, router_ref[...], 1, 0)).astype(
            dx_ref.dtype
        )


def expert_back(rows, dz, in_w, expert_w, layer, router_w, hot_row, experts, kind):
    count, width = rows.shape
    hidden = in_w.shape[1]
    block = 512
    struct = jax.ShapeDtypeStruct
    whole = pl.BlockSpec((count, width), lambda j: (0, 0))
    wide = pl.BlockSpec((count, block), lambda j: (0, j))
    router_spec = pl.BlockSpec((LANES, width), lambda j: (0, 0))
    return pl.pallas_call(
        functools.partial(expert_kernel, experts=experts),
        grid=(hidden // block,),
        out_shape=[
            struct((count, width), kind),
            struct((count, hidden), BF16),
            struct((count, hidden), BF16),
            struct((count, width), BF16),
            struct((LANES, width), F32),
        ],
        in_specs=[
            whole,
            whole,
            pl.BlockSpec((width, block), lambda j: (0, j)),
            pl.BlockSpec((None, block, width), lambda j: (layer, j, 0)),
            router_spec,
            pl.BlockSpec((1, LANES), lambda j: (0, 0)),
        ],
        out_specs=[whole, wide, wide, whole, router_spec],
        scratch_shapes=[
            pltpu.VMEM((count, LANES), F32),
            pltpu.VMEM((count, 1), F32),
            pltpu.VMEM((count, width), F32),
        ],
        compiler_params=pltpu.CompilerParams(
            dimension_semantics=("arbitrary",), vmem_limit_bytes=VMEM_LIMIT
        ),
        cost_estimate=pl.CostEstimate(
            flops=6 * count * width * hidden, bytes_accessed=12 * 10**6, transcendentals=0
        ),
    )(rows, dz, in_w, expert_w, router_w, hot_row)


def across_parts(grad, section):
    width = grad.shape[0]
    count = lax.axis_size("dp")
    halves = grad.reshape(count, 2, width // count // 2, -1)
    keep = lax.dynamic_index_in_dim(halves, section, 1, keepdims=False)
    send = lax.dynamic_index_in_dim(halves, 1 - section, 1, keepdims=False)
    return (keep, send.astype(BF16))


def across_sum(keep, send):
    return (keep + swap(send, "section").astype(F32)).astype(BF16)


def exchange_across(grad, section):
    return across_sum(*across_parts(grad, section))


def pair_up(values, tensor):
    half = values.shape[0] // 2
    halves = values.reshape(2, half, -1)
    own = entry(halves, tensor)
    other = swap(entry(halves, 1 - tensor), "tensor")
    return ordered(tensor, own[None], other[None])


def gelu_pair(before, active_grad):
    activated, back = jax.vjp(smooth_gate, before)
    return (activated.astype(BF16), back(active_grad)[0].astype(BF16))


def shards(
    x_in, d_out, lengths, routes, gain_attn, w_qkv, w_attn_out, gain_ffn, w_router, w_in, w_exp_out
):
    section = lax.axis_index("section")
    tensor = lax.axis_index("tensor")
    count = lax.axis_size("dp")
    width = x_in.shape[2]
    part = width // 2
    rows = 2 * x_in.shape[1]
    experts = w_router.shape[2]
    own_batch = 2 * section + tensor
    peer_batch = 2 * section + 1 - tensor

    def of_layer(layer, own, other):
        return jnp.where(section == layer, own, other)

    def pick(first, second):
        return jnp.where(section == 0, first, second)

    def by_layer(own):
        other = swap(own, "section")
        return [of_layer(layer, own, other) for layer in range(2)]

    def whole_group(array):
        return ordered(
            tensor, entry(array, own_batch), swap(entry(array, peer_batch), "tensor")
        )

    packed = jnp.concatenate([w_qkv[0], w_attn_out[0].T[None]], axis=0)
    packed = jnp.moveaxis(packed, 0, 1).reshape(width // count, -1)
    small = by_layer(jnp.concatenate([gain_attn, gain_ffn, w_router[0].T], axis=0))
    own_route = entry(routes[0, :, :, 0], own_batch)
    other_route = swap(entry(routes[0, :, :, 0], 2 * (1 - section) + tensor), "section")
    route = [of_layer(layer, own_route, other_route) for layer in range(2)]
    far_pack = swap(packed, "section")
    first_pack = of_layer(0, packed, far_pack)
    first_beside = swap(first_pack, "tensor")
    first_packs = jnp.concatenate([first_pack, first_beside], axis=1)
    first_w = lax.all_gather(first_packs, "dp", axis=0, tiled=True)
    x_own = whole_group(x_in)
    far_pack, d_last = after((far_pack, d_out), first_beside)
    second_pack = of_layer(1, packed, far_pack)
    second_pack = jnp.concatenate([second_pack, swap(second_pack, "tensor")], axis=1)
    dz_last = whole_group(d_last)
    far_in = swap(w_in[0, 0], "section")
    in_w = [of_layer(layer, w_in[0, 0], far_in) for layer in range(2)]
    both_out = lax.all_gather(after(w_exp_out[0, 0], first_packs), "section", axis=0)
    expert_w = [both_out[0], both_out[1]]

    tables = [routing(row, experts) for row in route]
    placing = [table[0] for table in tables]
    taking = [table[1] for table in tables]
    route_col = [row[:, None] for row in route]
    gains = [small[layer][:2].astype(F32) for layer in range(2)]
    router_w = [jnp.pad(small[layer][2:], ((0, LANES - experts), (0, 0))) for layer in range(2)]
    bounds = jnp.cumsum(entry(lengths[:, 0], own_batch))
    places = jnp.arange(rows, dtype=jnp.int32)
    segment = jnp.sum((places[:, None] >= bounds[None, :]).astype(jnp.int32), axis=1)
    segments = (segment[:, None], segment[None, :])
    hot_row = (
        jnp.arange(LANES, dtype=jnp.int32)[None, :] == lax.axis_index("dp")
    ).astype(F32)
    keys = ("xn", "qkv", "lse", "o", "o_far", "h", "gate")

    def expert_forward(values, layer):
        active = smooth_gate(dot(values, in_w[layer], 1, 0)).astype(BF16)
        return dot(active, expert_w[layer], 1, 0)

    def fold(own, peer):
        own = lax.optimization_barrier(own)
        return (own + swap(peer.astype(BF16), "tensor").astype(F32)).astype(BF16)

    params0 = (gains[0], first_w, router_w[0], experts)
    *state0, outgoing0 = layer_start(
        {"a": after(x_own, far_in)}, params0, segments, route_col[0], placing[0]
    )
    state0 = dict(zip(keys, state0))
    mine0 = all_to_all(outgoing0)
    side_xn0 = swap(state0["xn"], "tensor")
    side_o0 = swap(state0["o_far"], "tensor")
    peer0 = swap(
        after(mine0, side_xn0, side_o0, in_w), "tensor"
    )
    second_w = lax.all_gather(after(second_pack, mine0), "dp", axis=0, tiled=True)
    dz_out1 = dot(placing[1], dz_last, 1, 0).astype(BF16)
    mine_dz1 = all_to_all(after(dz_out1, mine0))
    total_y0 = fold(expert_forward(mine0, 0), expert_forward(peer0, 0))
    back0 = all_to_all(after(total_y0, mine_dz1))

    params1 = (gains[1], second_w, router_w[1], experts)
    *state1, outgoing1, out0 = layer_start(
        {"taking": taking[0], "back": back0, "h_before": state0["h"],
         "gate_before": state0["gate"]},
        params1, segments, route_col[1], placing[1],
    )
    state1 = dict(zip(keys, state1))
    peer_dz1 = swap(mine_dz1, "tensor")
    pair_out0 = pair_up(out0, tensor)
    mine1 = all_to_all(outgoing1)
    peer1 = swap(after(mine1, peer_dz1, pair_out0), "tensor")

    def both_back(layer, mine, peer, mine_dz, peer_dz):
        args = (in_w[layer], both_out, layer, router_w[layer], hot_row, experts)
        own = expert_back(mine, mine_dz, *args, F32)
        peer, peer_dz = after((peer, peer_dz), own[0])
        return (own, expert_back(peer, peer_dz, *args, BF16))

    own_b1, peer_b1 = both_back(1, mine1, peer1, mine_dz1, peer_dz1)
    peer_dx1 = swap(peer_b1[0], "tensor")
    far_mine = swap(pick(mine1, mine0), "section")
    far_peer = swap(pick(after(peer1, own_b1[0]), peer0), "section")
    dback1 = all_to_all(
        after((own_b1[0] + peer_dx1.astype(F32)).astype(BF16), far_mine)
    )
    late_mine1, late_peer1 = after((mine1, peer1), peer_b1[0])
    peer_y1 = expert_forward(late_peer1, 1).astype(BF16)
    own_y1 = expert_forward(late_mine1, 1)
    side_y1 = swap(after(peer_y1, peer_dx1), "tensor")
    total_y1 = (own_y1 + side_y1.astype(F32)).astype(BF16)
    side_xn1, side_o1 = [
        swap(half, "tensor")
        for half in after((state1["xn"], state1["o_far"]), peer_dx1)
    ]
    dattn1, dh1, gain_f1 = hidden_end(
        after(dback1, own_y1, peer_y1, side_xn1, side_o1, far_peer), taking[1], dz_last, state1, params1
    )
    side_dattn1 = swap(dattn1, "tensor")
    grad1, dqkv1, dqkv_far1, gain_a1, outgoing_dz0 = layer_end(
        dattn1, dh1, out0, state1, params1, segments, placing[0]
    )

    mine_dz0 = all_to_all(outgoing_dz0)
    side_dqkv1 = swap(dqkv_far1, "tensor")
    def stack(first, second):
        return jnp.concatenate([first, second], axis=0)

    def attention_grad(xn, side_xn, dqkv, side_dqkv):
        return dot(stack(xn, side_xn), stack(dqkv, side_dqkv), 0, 0)

    def output_grad(dattn, side_dattn, mixed, side_mixed):
        return dot(stack(dattn, side_dattn), stack(mixed, side_mixed), 0, 0)

    full1 = jnp.concatenate(
        [
            attention_grad(state1["xn"], side_xn1, dqkv1, side_dqkv1),
            output_grad(dattn1, side_dattn1, state1["o"], side_o1),
        ],
        axis=1,
    )
    keep1, send1 = across_parts(full1, section)
    peer_dz0 = swap(after(mine_dz0, send1, side_y1), "tensor")
    across1 = swap(send1, "section")
    back1 = all_to_all(after(total_y1, mine_dz0))
    peer_dz0 = after(peer_dz0, across1, back1)
    own_b0, peer_b0 = both_back(0, mine0, peer0, mine_dz0, peer_dz0)
    keep1, across1 = after((keep1, across1), own_b0[0])
    reduced1 = all_to_all((keep1 + across1.astype(F32)).astype(BF16))
    peer_dx0 = swap(peer_b0[0], "tensor")
    pair_grad1 = pair_up(after(grad1, peer_dx0), tensor)


    def gather_rows(number, index):
        return stack((own_b0, own_b1)[number][index], (peer_b0, peer_b1)[number][index])

    late_mine0, late_mine1, own_b1, peer_b1 = after((mine0, mine1, own_b1, peer_b1), peer_b0[0])
    near_rows = pick(stack(late_mine0, peer0), stack(late_mine1, peer1))
    near_dpre = pick(gather_rows(0, 2), gather_rows(1, 2))
    near_in = dot(near_rows, near_dpre, 0, 0)
    far_dys = [
        swap(pick(*after((part_b1[3], part_b0[3]), peer_b0[0])), "section")
        for part_b1, part_b0 in ((own_b1, own_b0), (peer_b1, peer_b0))
    ]
    total_dx0 = after(
        (own_b0[0] + peer_dx0.astype(F32)).astype(BF16), near_in, reduced1
    )
    dback0 = all_to_all(total_dx0)
    dy0, dy1 = (gather_rows(0, 3), gather_rows(1, 3))
    near_dy = pick(dy0, dy1)
    late_back1 = after(back1, total_dx0)
    out1 = (state1["h"] + state1["gate"] * dot(taking[1], late_back1, 1, 0)).astype(BF16)
    pair_out1 = pair_up(out1, tensor)
    far_outs = swap(pick(pair_out1, pair_out0), "section")
    near_act = pick(*after((gather_rows(0, 1), gather_rows(1, 1)), total_dx0))
    near_out = dot(near_act, near_dy, 0, 0)
    dattn0, dh0, gain_f0 = hidden_end(
        after(dback0, near_out, pair_out1), taking[0], grad1, state0, params0
    )
    side_dattn0 = swap(dattn0, "tensor")
    grad0, dqkv0, dqkv_far0, gain_a0 = layer_end(
        dattn0, dh0, x_own, state0, params0, segments, None
    )

    side_dqkv0 = swap(dqkv_far0, "tensor")
    late_dattn0, late_side = after((dattn0, side_dattn0), dqkv0)
    out_keep, out_send = across_parts(
        output_grad(late_dattn0, late_side, state0["o"], side_o0), section
    )
    smalls = jnp.stack(
        [
            jnp.concatenate([*gain, (own[4] + peer[4])[:experts]], axis=0)
            for gain, own, peer in (
                ((gain_a0, gain_f0), own_b0, peer_b0), ((gain_a1, gain_f1), own_b1, peer_b1)
            )
        ]
    )
    smalls = after(smalls, out_send)
    smalls = all_to_all(jnp.broadcast_to(smalls[None], (count,) + smalls.shape))
    smalls = smalls.sum(axis=0)
    ready_xn0 = after(state0["xn"], out_send)
    qkv_keep, qkv_send = across_parts(
        attention_grad(ready_xn0, side_xn0, dqkv0, side_dqkv0), section
    )
    far_rows = stack(*after((far_mine, far_peer), qkv_send))
    far_dy = stack(*after(tuple(far_dys), qkv_send))
    far_before = dot(far_rows, w_in[0, 0], 1, 0)
    half0 = jnp.concatenate(
        [
            across_sum(after(qkv_keep, far_before, far_dy), qkv_send),
            across_sum(out_keep, out_send),
        ],
        axis=2,
    )
    reduced0 = all_to_all(half0)
    pair_grad0 = pair_up(after(grad0, qkv_send), tensor)
    far_grads = swap(pick(pair_grad1, after(pair_grad0, half0)), "section")
    far_dy, reduced1 = after((far_dy, reduced1), half0)
    far_act, far_dpre = gelu_pair(far_before, dot(far_dy, w_exp_out[0, 0], 1, 1))
    in_w_grad = near_in + dot(far_rows, far_dpre, 0, 0)
    expert_w_grad = near_out + dot(far_act, far_dy, 0, 0)

    smalls = after(smalls, qkv_send)
    smalls = smalls + swap(smalls, "tensor")
    own_small = pick(smalls[0], smalls[1]) + swap(pick(smalls[1], smalls[0]), "section")

    reduced1 = reduced1.astype(F32).sum(axis=0)
    reduced0 = after(reduced0, in_w_grad, expert_w_grad, far_grads, far_outs, own_small)
    reduced0 = reduced0.astype(F32).sum(axis=0)
    own_half = pick(reduced0, reduced1)
    other_half = swap(pick(reduced1, reduced0).astype(BF16), "section").astype(F32)
    joined = ordered(section, own_half, other_half)
    qkv_grad = jnp.stack([joined[:, part * kind:part * (kind + 1)] for kind in range(3)])
    out_grad = joined[:, 3 * part:].T
    section_out = ordered(section, pick(pair_out0, pair_out1), far_outs)
    section_in_grad = ordered(section, pick(pair_grad0, pair_grad1), far_grads)
    return (
        section_out[None],
        section_in_grad[None],
        own_small[0][None],
        qkv_grad[None],
        out_grad[None],
        own_small[1][None],
        own_small[2:].T[None],
        in_w_grad[None, None],
        expert_w_grad[None, None],
    )


def solution(mesh):
    in_specs = (
        P(None, ("dp", "tensor"), None),
        P(None, ("dp", "tensor"), None),
        P(None, "dp", None),
        P("section", None, "dp", None),
        P("section", None),
        P("section", None, "dp", "tensor"),
        P("section", "tensor", "dp"),
        P("section", None),
        P("section", None, None),
        P("section", "dp", None, "tensor"),
        P("section", "dp", "tensor", None),
    )
    out_specs = (
        P("section", None, ("dp", "tensor"), None),
        P("section", None, ("dp", "tensor"), None),
        P("section", None),
        P("section", None, "dp", "tensor"),
        P("section", "tensor", "dp"),
        P("section", None),
        P("section", None, None),
        P("section", "dp", None, "tensor"),
        P("section", "dp", "tensor", None),
    )
    return jax.shard_map(shards, mesh=mesh, in_specs=in_specs, out_specs=out_specs, check_vma=False)
```
